32 devices in a mesh: panel: 8 (over z, x), cam: 2 (over y), frame: 2 (over core).
Axes of the slice: x: 2, y: 2, z: 4, core: 2. Of those that a mesh axis runs over, the one named last changes fastest.
Arguments:
- front_jc: bfloat16 [1024, 4, 2, 6, 128], P(('panel', 'cam', 'frame')), as said below
- front_jp: bfloat16 [1024, 4, 2, 6, 128], P(('panel', 'cam', 'frame')), as said below
- front_res: bfloat16 [1024, 4, 2, 128], P(('panel', 'cam', 'frame')), may hold values from -96 to 96
- front_corners: int32 [1024, 4, 128], P(('panel', 'cam', 'frame')), may hold values from 0 to 4095
- front_cams: int32 [1024, 4], P(('panel', 'cam', 'frame')), may hold values from 0 to 31
- back_jc: bfloat16 [1024, 4, 2, 6, 128], P(('panel', 'cam', 'frame')), as said below
- back_jp: bfloat16 [1024, 4, 2, 6, 128], P(('panel', 'cam', 'frame')), as said below
- back_res: bfloat16 [1024, 4, 2, 128], P(('panel', 'cam', 'frame')), may hold values from -96 to 96
- back_corners: int32 [1024, 4, 128], P(('panel', 'cam', 'frame')), may hold values from 0 to 4095
- back_cams: int32 [1024, 4], P(('panel', 'cam', 'frame')), may hold values from 0 to 31
- back_match: int32 [1024], P(('panel', 'cam', 'frame')), may hold values from 0 to 31, as said below
- face: int32 [1024], P(('panel', 'cam', 'frame')), may hold values from 0 to 1
- corner_gain: float32 [8192], replicated, may hold values from 0.3 to 3
Outputs:
- cam_step: float32 [6, 128], P(None, 'panel')
- pose_step: float32 [6, 1024], P(None, ('panel', 'cam', 'frame'))
The draws below stay inside these ranges and needn't reach their ends.
Inputs may be any that keep to these rules, and one draw needn't show every extreme that they name: `back_match`: in each aligned block of 32 entries every number appears exactly once. `front_cams`: codes below 8 * 2 name a camera of the storing panel, the others one of the next panel. `front_jc`: camera derivatives of one view. `front_jp`: pose derivatives of one view. `back_jc`: camera derivatives of one view. `back_jp`: pose derivatives of one view.
All inputs are finite; a program needn't handle non-finite values.
Results may differ from the reference program's by a relative error of at most 0.0035.
Values may be sent and summed in bfloat16 or wider, within the bound.
A program may use at most 64 MiB of HBM per device.

```python
import math
import jax
import jax.numpy as jnp
from jax import lax

FRAME_DEV = 32
VIEWS = 4
CORNERS = 128
GRID = 4096
CAM_DEV = 8
ITERS = 4
FRAMES = 1024
CAMERAS = 128
N_PANEL = 8
N_CAM = 2
N_FRAME = 2


def panel_gain(key):
    panel_levels = jnp.exp(jax.random.uniform(jax.random.fold_in(key, 41), (N_PANEL, 1), jnp.float32, -1.0, 1.0))
    return jnp.broadcast_to(panel_levels, (N_PANEL, FRAMES // N_PANEL)).reshape(FRAMES, 1, 1, 1, 1)


def jacobian_pair(key, salt):
    shape = (FRAMES, VIEWS, 2, 6, CORNERS)
    scale = (2.0 * CORNERS) ** (-0.5)
    shared = jax.random.normal(jax.random.fold_in(key, salt), shape, jnp.float32)
    fresh = jax.random.normal(jax.random.fold_in(key, salt + 1), shape, jnp.float32)
    view_scale = jnp.exp(jax.random.uniform(jax.random.fold_in(key, salt + 2), (FRAMES, VIEWS, 1, 1, 1), jnp.float32, -0.35, 0.35))
    total_scale = scale * view_scale * panel_gain(key)
    return (shared * total_scale, (0.8 * shared + 0.6 * fresh) * total_scale)


def draw_front_jc(key, part):
    return jacobian_pair(key, 11)[0].astype(jnp.bfloat16)


def draw_front_jp(key, part):
    return jacobian_pair(key, 11)[1].astype(jnp.bfloat16)


def draw_back_jc(key, part):
    return jacobian_pair(key, 21)[0].astype(jnp.bfloat16)


def draw_back_jp(key, part):
    return jacobian_pair(key, 21)[1].astype(jnp.bfloat16)


def draw_back_match(key, part):
    keys = jax.random.split(jax.random.fold_in(key, 31), FRAMES // FRAME_DEV)
    orders = jax.vmap(lambda single: jax.random.permutation(single, FRAME_DEV))(keys)
    return orders.reshape(FRAMES).astype(jnp.int32)


def with_ends(result, key, least, high):
    extent = result.shape
    index_at = [jax.random.randint(jax.random.fold_in(key, axis), (), 0, extent[axis]) for axis in range(len(extent))]
    result = result.at[tuple(index_at)].set(least)
    longest = extent.index(max(extent))
    index_at[longest] = (index_at[longest] + 1) % extent[longest]
    return result.at[tuple(index_at)].set(high)


def block_levels(own_key, dims, cuts, smallest, largest):
    gain, own = 1.0, jax.random.fold_in(own_key, 6)
    for dim, blocks in cuts:
        draws = jnp.exp(jax.random.uniform(jax.random.fold_in(own, dim), (blocks,), jnp.float32, smallest / len(cuts), largest / len(cuts)))
        gain = gain * jnp.repeat(draws, dims[dim] // blocks).reshape([-1 if axis == dim else 1 for axis in range(len(dims))])
    return gain


def gaussian(stream_key, dims, width, most, cuts=(), held_as=jnp.bfloat16):
    level = block_levels(stream_key, dims, cuts, -0.22, 0.18) if cuts else 1.0
    entries = jax.random.normal(stream_key, dims, jnp.float32) * width * level
    return jnp.minimum(jnp.maximum(entries, -most), most).astype(held_as)


def setup_inputs(seed: int = 0) -> dict:
    streams_of = jax.random.split(jax.random.key(seed), 14)
    return {
        "front_jc": draw_front_jc(jax.random.fold_in(streams_of[13], 71), 0),
        "front_jp": draw_front_jp(jax.random.fold_in(streams_of[13], 71), 0),
        "front_res": gaussian(streams_of[2], (FRAMES, VIEWS, 2, CORNERS), 16.0, 96.0, ((0, 32),)),
        "front_corners": with_ends(jax.random.randint(streams_of[3], (FRAMES, VIEWS, CORNERS), 0, GRID), jax.random.fold_in(streams_of[3], 1), 0, GRID - 1).astype(jnp.int32),
        "front_cams": with_ends(jax.random.randint(streams_of[4], (FRAMES, VIEWS), 0, 2 * CAM_DEV * N_CAM), jax.random.fold_in(streams_of[4], 1), 0, (2 * CAM_DEV * N_CAM) - 1).astype(jnp.int32),
        "back_jc": draw_back_jc(jax.random.fold_in(streams_of[13], 71), 0),
        "back_jp": draw_back_jp(jax.random.fold_in(streams_of[13], 71), 0),
        "back_res": gaussian(streams_of[7], (FRAMES, VIEWS, 2, CORNERS), 16.0, 96.0, ((0, 32),)),
        "back_corners": with_ends(jax.random.randint(streams_of[8], (FRAMES, VIEWS, CORNERS), 0, GRID), jax.random.fold_in(streams_of[8], 1), 0, GRID - 1).astype(jnp.int32),
        "back_cams": with_ends(jax.random.randint(streams_of[9], (FRAMES, VIEWS), 0, 2 * CAM_DEV * N_CAM), jax.random.fold_in(streams_of[9], 1), 0, (2 * CAM_DEV * N_CAM) - 1).astype(jnp.int32),
        "back_match": draw_back_match(jax.random.fold_in(streams_of[13], 71), 0),
        "face": with_ends(jax.random.randint(streams_of[11], (FRAMES,), 0, 2), jax.random.fold_in(streams_of[11], 1), 0, 1).astype(jnp.int32),
        "corner_gain": jnp.clip(jnp.exp(jax.random.uniform(streams_of[12], (2 * GRID,), jnp.float32, math.log(0.3), math.log(3.0))), 0.3, 3.0),
    }


precise = lax.Precision.HIGHEST
damp_pose = 0.1
damp_camera = 0.5


def invert_six(matrix):
    dimension = matrix.shape[-1]
    working = matrix
    inverse = jnp.broadcast_to(jnp.eye(dimension, dtype=matrix.dtype), matrix.shape)
    row_ids = jnp.arange(dimension)[:, None]
    for column in range(dimension):
        pivot = working[..., column:column + 1, column:column + 1]
        row_work = working[..., column:column + 1, :] / pivot
        row_inverse = inverse[..., column:column + 1, :] / pivot
        factor = working[..., :, column:column + 1]
        chosen = row_ids == column
        working = jnp.where(chosen, row_work, working - factor * row_work)
        inverse = jnp.where(chosen, row_inverse, inverse - factor * row_inverse)
    return inverse


def view_grams(jac_cam, jac_pose, residual, corner_ids, face_ids, corner_gain, grid_size):
    weight = jnp.take(corner_gain, face_ids[:, None] * grid_size + corner_ids, axis=0)
    stacked = jnp.concatenate([jac_cam, jac_pose], axis=2)
    weighted = (stacked.astype(jnp.float32) * weight[:, None, None, :]).astype(jnp.bfloat16)
    normal_blocks = jnp.einsum("ncak,ncbk->nab", weighted.astype(jnp.float32), stacked.astype(jnp.float32), precision=precise)
    gradients = jnp.einsum("ncak,nck->na", weighted.astype(jnp.float32), residual.astype(jnp.float32), precision=precise)
    return normal_blocks, gradients


def conjugate(operate, dot_product, right_side, iterations):
    cam_update = jnp.zeros_like(right_side)
    residual = -right_side
    direction = residual
    norm_now = dot_product(residual, residual)
    for iteration in range(iterations):
        image_vec = operate(direction)
        step_size = norm_now / dot_product(direction, image_vec)
        cam_update = cam_update + step_size * direction
        residual = residual - step_size * image_vec
        norm_next = dot_product(residual, residual)
        direction = residual + (norm_next / norm_now) * direction
        norm_now = norm_next
    return cam_update


def reference(front_jc, front_jp, front_res, front_corners, front_cams, back_jc, back_jp, back_res, back_corners, back_cams, back_match, face, corner_gain):
    block_count = FRAMES // FRAME_DEV
    per_panel = CAM_DEV * N_CAM
    group_size = N_CAM * N_FRAME
    per_dev = FRAME_DEV * VIEWS
    frame_ids = jnp.arange(FRAMES, dtype=jnp.int32)
    store_panel = frame_ids // FRAME_DEV // group_size
    home_block = ((store_panel + N_PANEL // 2) % N_PANEL) * group_size + (frame_ids // FRAME_DEV) % group_size
    home_frame = (home_block * FRAME_DEV + back_match).astype(jnp.int32)

    def grams_of(jac_cam, jac_pose, residual, corner_ids, face_ids):
        def per_block(pieces):
            return view_grams(pieces[0], pieces[1], pieces[2], pieces[3], pieces[4], corner_gain, GRID)
        blocks_in = (jac_cam.reshape(block_count, per_dev, 2, 6, CORNERS),
                     jac_pose.reshape(block_count, per_dev, 2, 6, CORNERS),
                     residual.reshape(block_count, per_dev, 2, CORNERS),
                     corner_ids.reshape(block_count, per_dev, CORNERS),
                     jnp.repeat(face_ids, VIEWS).reshape(block_count, per_dev))
        normal_blocks, gradients = lax.map(per_block, blocks_in)
        return normal_blocks.reshape(-1, 12, 12), gradients.reshape(-1, 12)

    gram_front, grad_front = grams_of(front_jc, front_jp, front_res, front_corners, face)
    gram_back, grad_back = grams_of(back_jc, back_jp, back_res, back_corners, 1 - face[home_frame])
    normal_blocks = jnp.concatenate([gram_front, gram_back])
    gradients = jnp.concatenate([grad_front, grad_back])
    cam_block = normal_blocks[:, :6, :6]
    cam_pose = normal_blocks[:, :6, 6:]
    pose_block = normal_blocks[:, 6:, 6:]
    view_frame = jnp.concatenate([jnp.repeat(frame_ids, VIEWS), jnp.repeat(home_frame, VIEWS)])
    view_panel = jnp.concatenate([jnp.repeat(store_panel, VIEWS), jnp.repeat(store_panel, VIEWS)])
    codes = jnp.concatenate([front_cams.reshape(-1), back_cams.reshape(-1)])
    view_cam = (((view_panel + codes // per_panel) % N_PANEL) * per_panel + codes % per_panel).astype(jnp.int32)

    pose_mat = jax.ops.segment_sum(pose_block, view_frame, num_segments=FRAMES) + damp_pose * jnp.eye(6, dtype=jnp.float32)
    pose_inv = invert_six(pose_mat)
    pose_grad = jax.ops.segment_sum(gradients[:, 6:], view_frame, num_segments=FRAMES)

    def couple(x_views):
        return jax.ops.segment_sum(jnp.einsum("nab,na->nb", cam_pose, x_views, precision=precise), view_frame, num_segments=FRAMES)

    def solve_pose(pose_vec):
        return jnp.einsum("fab,fb->fa", pose_inv, pose_vec, precision=precise)

    def spread(pose_vec):
        return jnp.einsum("nab,nb->na", cam_pose, pose_vec[view_frame], precision=precise)

    def operate(vector):
        x_views = vector[view_cam]
        view_terms = jnp.einsum("nab,nb->na", cam_block, x_views, precision=precise) - spread(solve_pose(couple(x_views)))
        return damp_camera * vector + jax.ops.segment_sum(view_terms, view_cam, num_segments=CAMERAS)

    def dot_product(vector_a, vector_b):
        return jnp.sum(vector_a * vector_b)

    right_side = jax.ops.segment_sum(gradients[:, :6] - spread(solve_pose(pose_grad)), view_cam, num_segments=CAMERAS)
    cam_update = conjugate(operate, dot_product, right_side, ITERS)
    pose_update = -solve_pose(pose_grad + couple(cam_update[view_cam]))
    return cam_update.T, pose_update.T
```

```python
import functools

import jax
import jax.numpy as jnp
import numpy as np
from jax import lax
from jax.experimental import pallas as pl
from jax.experimental.pallas import tpu as pltpu
from jax.sharding import PartitionSpec as P

CAM_DEV = 8
ITERS = 4
LANES = 128
SLOT = 16
SUB = 8
DIM = 6
COORDS = 2

damp_pose = 0.1
damp_camera = 0.5
MESH = pl.DeviceIdType.MESH
NT = (((1,), (1,)), ((), ()))

BACK0, BACK1, FRONT, MISC, FIRST = 0, 9, 18, 27, 28
U_BACK0, U_BACK1, U_FRONT, SECOND = 0, 6, 12, 18


def selection(view_count):
    block = view_count * DIM * COORDS
    res_rows = view_count * COORDS
    table = np.zeros((2, COORDS, 2, view_count, SLOT, 4 * block + 4 * res_rows), np.float32)
    for parity in range(2):
        for coord in range(COORDS):
            for side in range(2):
                for view in range(view_count):
                    for a in range(DIM):
                        column = side * 2 * block + (view * DIM + a) * COORDS + coord
                        table[parity, coord, side, view, a, column] = 1
                        table[parity, coord, side, view, SUB + a, column + block] = 1
                    column = 4 * block + side * 2 * res_rows + parity * res_rows + view * COORDS + coord
                    table[parity, coord, side, view, SUB + DIM, column] = 1
    return jnp.asarray(table.reshape(2, COORDS * 2 * view_count * SLOT, -1), jnp.bfloat16)


def row_of(value, index):
    return jnp.broadcast_to(value[index : index + 1, :], (SUB, value.shape[1]))


def halves(value):
    high = value.astype(jnp.bfloat16)
    low = (value - high.astype(jnp.float32)).astype(jnp.bfloat16)
    return jnp.concatenate([high, low], axis=0)


def invert(working):
    sub = lax.broadcasted_iota(jnp.int32, working[0].shape, 0)
    inverse = [jnp.where(sub == row, 1.0, 0.0) for row in range(DIM)]
    working = list(working)
    for column in range(DIM):
        pivot = 1.0 / row_of(working[column], column)
        row_work = working[column] * pivot
        row_inverse = inverse[column] * pivot
        for row in range(DIM):
            if row == column:
                continue
            factor = row_of(working[row], column)
            working[row] = working[row] - factor * row_work
            inverse[row] = inverse[row] - factor * row_inverse
        working[column] = row_work
        inverse[column] = row_inverse
    return inverse


def step_kernel(
    sizes,
    per_panel,
    frames,
    view_count,
    face_s,
    match_s,
    fjc,
    fjp,
    fres,
    fcor,
    fcam,
    bjc,
    bjp,
    bres,
    bcor,
    bcam,
    gain,
    pick,
    cam_out,
    pose_out,
    weights,
    grams0,
    grams1,
    own1,
    own2,
    got1,
    got2,
    turned,
    hot,
    send,
    recv,
    swap_send,
    swap_recv,
    send_sem,
    recv_sem,
):
    panels, cams, cores = sizes
    group = cams * cores
    half = panels // 2
    peers = half * group
    width = panels * per_panel
    views = frames * view_count
    table_rows = gain.shape[0] // 2
    panel = lax.axis_index("panel")
    cam = lax.axis_index("cam")
    core = lax.axis_index("frame")
    other_panel = lax.rem(panel + half, panels)
    partner = (other_panel, cam, core)
    side = panel // half
    me = (lax.rem(panel, half) * cams + cam) * cores + core

    def coords(device):
        return (side * half + device // group, (device // cores) % cams, device % cores)

    def each_peer(action):
        if peers <= 16:
            for offset in range(1, peers):
                action(coords(lax.rem(me + offset, peers)))
        else:

            @pl.loop(1, peers)
            def _(offset):
                action(coords(lax.rem(me + offset, peers)))

    barrier = pltpu.get_barrier_semaphore()
    pl.semaphore_signal(barrier, inc=1, device_id=partner, device_id_type=MESH)
    each_peer(lambda device: pl.semaphore_signal(barrier, inc=1, device_id=device, device_id_type=MESH))

    sub = lax.broadcasted_iota(jnp.int32, (SUB, LANES), 0)
    lane = lax.broadcasted_iota(jnp.int32, (SUB, LANES), 1)

    def look_up(step, _):
        rows = pl.ds(pl.multiple_of(step * SUB, SUB), SUB)
        own_face = jnp.where(sub < view_count, face_s[2 * step], face_s[2 * step + 1]) == 0
        front, back = fcor[rows, :], bcor[rows, :]
        front_low, front_high = front & (LANES - 1), front // LANES
        back_low, back_high = back & (LANES - 1), back // LANES
        found = [jnp.zeros((SUB, LANES), jnp.float32)] * 3
        for entry in range(table_rows):
            table = [
                jnp.broadcast_to(gain[face * table_rows + entry : face * table_rows + entry + 1, :], (SUB, LANES))
                for face in range(2)
            ]
            mixed = jnp.where(own_face, table[0], table[1])
            here = back_high == entry
            for place, (source, low, mask) in enumerate(
                ((mixed, front_low, front_high == entry), (table[0], back_low, here), (table[1], back_low, here))
            ):
                picked = jnp.take_along_axis(source, low, axis=1, mode="promise_in_bounds")
                found[place] = jnp.where(mask, picked, found[place])
        for place in range(3):
            weights[place, rows, :] = found[place]
        return 0

    lax.fori_loop(0, views // SUB, look_up, 0)

    block_rows = view_count * DIM * COORDS
    span = 2 * view_count * SLOT
    slot_view = lax.broadcasted_iota(jnp.int32, (SLOT, LANES), 1) // SLOT

    def gram(step, _):
        for parity in range(2):
            frame = 2 * step + parity
            rows = pl.ds(pl.multiple_of(frame * block_rows, SLOT), block_rows)
            res_rows = pl.ds(pl.multiple_of(step * SLOT, SLOT), SLOT)
            stored = jnp.concatenate(
                [fjc[rows, :], fjp[rows, :], bjc[rows, :], bjp[rows, :], fres[res_rows, :], bres[res_rows, :]], axis=0
            )
            plain = jnp.dot(pick[parity], stored, preferred_element_type=jnp.float32)
            left, right = [], []
            for coord in range(COORDS):
                part = plain[coord * span : (coord + 1) * span]
                left.append(part.astype(jnp.bfloat16))
                scaled = []
                for place in range(3):
                    for view in range(view_count):
                        weight = weights[place, pl.ds(frame * view_count + view, 1), :]
                        start = ((view_count if place else 0) + view) * SLOT
                        scaled.append(part[start : start + SLOT] * jnp.broadcast_to(weight, (SLOT, LANES)))
                right.append(jnp.concatenate(scaled, axis=0).astype(jnp.bfloat16))
            product = lax.dot_general(
                jnp.concatenate(left, axis=1),
                jnp.concatenate(right, axis=1),
                NT,
                preferred_element_type=jnp.float32,
            )
            both = product[:SLOT, :LANES]
            for view in range(1, 2 * view_count):
                both = jnp.where(slot_view == view, product[view * SLOT : (view + 1) * SLOT, :LANES], both)
            start = view_count * SLOT
            last = product[start : start + SLOT, LANES:]
            for view in range(1, view_count):
                rows_of = product[start + view * SLOT : start + (view + 1) * SLOT, LANES:]
                last = jnp.where(slot_view[:, : last.shape[1]] == view, rows_of, last)
            out_rows = pl.ds(pl.multiple_of(frame * SLOT, SLOT), SLOT)
            grams0[out_rows, :] = both
            grams1[out_rows, : last.shape[1]] = last
        return 0

    lax.fori_loop(0, frames // 2, gram, 0)

    quarter = lane // frames
    count = LANES // frames

    def turn(scratch, rows):
        result = []
        for quad in range(SLOT // count):
            block = jnp.concatenate(
                [scratch[pl.ds(quad * count + i, frames, stride=SLOT), :] for i in range(count)], axis=0
            )
            result.append(block.T[:rows])
        return result

    def swap_quarters(r):
        low = quarter < 2
        even = quarter % 2 == 0
        u0 = jnp.where(low, r[0], pltpu.roll(r[2], 2 * frames, 1))
        u1 = jnp.where(low, r[1], pltpu.roll(r[3], 2 * frames, 1))
        u2 = jnp.where(low, pltpu.roll(r[0], 2 * frames, 1), r[2])
        u3 = jnp.where(low, pltpu.roll(r[1], 2 * frames, 1), r[3])
        back = LANES - frames
        return [
            jnp.where(even, u0, pltpu.roll(u1, frames, 1)),
            jnp.where(even, pltpu.roll(u0, back, 1), u1),
            jnp.where(even, u2, pltpu.roll(u3, frames, 1)),
            jnp.where(even, pltpu.roll(u2, back, 1), u3),
        ]

    inverse_match = jnp.zeros((SUB, LANES), jnp.int32)
    in_frames = lane % frames
    face_row = jnp.zeros((SUB, LANES), jnp.float32)
    for frame in range(frames):
        inverse_match = jnp.where(in_frames == match_s[frame], frame, inverse_match)
        face_row = jnp.where(in_frames == frame, face_s[frame].astype(jnp.float32), face_row)
    home = quarter * frames + inverse_match

    def to_home(value):
        return jnp.take_along_axis(value, home, axis=1, mode="promise_in_bounds")

    def lay_out(turned_grams, first_view, message, place, u_place, order):
        columns = []
        sums = []
        for quad, tall in enumerate(turned_grams):
            pieces = [
                tall[(first_view + view) * SLOT : (first_view + view) * SLOT + SUB] for view in range(view_count)
            ]
            columns += swap_quarters(pieces)
            if quad >= 2:
                total = None
                for view in range(view_count):
                    start = (first_view + view) * SLOT + SUB
                    piece = tall[start : start + SUB]
                    total = piece if total is None else total + piece
                sums.append(jnp.where(sub < DIM, total, 0.0))
        for b in range(DIM):
            own2[u_place + b] = order(columns[b])
        for b in range(DIM + 1):
            own1[place + b] = order(columns[SUB + b])
        for i in range(2):
            own1[place + DIM + 1 + i] = order(sums[i])

    tall0 = turn(grams0, LANES)
    tall1 = turn(grams1, view_count * SLOT)
    lay_out(tall0, view_count, own1, BACK0, U_BACK0, to_home)
    lay_out(tall1, 0, own1, BACK1, U_BACK1, to_home)
    lay_out(tall0, 0, own1, FRONT, U_FRONT, lambda value: value)

    def code_row(ref):
        row = jnp.concatenate([ref[view : view + 1, :] for view in range(view_count)], axis=1)
        return jnp.broadcast_to(row, (SUB, LANES)).astype(jnp.float32)

    misc = jnp.where(sub == 0, code_row(fcam), to_home(code_row(bcam)))
    own1[MISC] = jnp.where(sub == 2, face_row, misc)

    pl.semaphore_wait(barrier, peers)
    swaps = [
        pltpu.make_async_remote_copy(
            src_ref=source,
            dst_ref=target,
            send_sem=swap_send.at[index],
            recv_sem=swap_recv.at[index],
            device_id=partner,
            device_id_type=MESH,
        )
        for index, (source, target) in enumerate(((own1, got1), (own2, got2)))
    ]
    for swap in swaps:
        swap.start()
    swaps[0].wait_recv()

    own_first = own1[MISC][2:3, :] < 0.5
    far_first = got1[MISC][2:3, :] < 0.5
    own_first = jnp.broadcast_to(own_first, (SUB, LANES))
    far_first = jnp.broadcast_to(far_first, (SUB, LANES))

    def choose(mask, ref, one, zero, index):
        return jnp.where(mask, ref[one + index], ref[zero + index])

    def coupling(index):
        return [
            own1[FRONT + index],
            choose(own_first, got1, BACK1, BACK0, index),
            got1[FRONT + index],
            choose(far_first, own1, BACK1, BACK0, index),
        ]

    for b in range(DIM):
        for place, value in enumerate(coupling(b)):
            turned[place, b * SUB : (b + 1) * SUB, :] = value
    for place in range(4):
        turned[place, DIM * SUB :, :] = jnp.zeros((2 * SUB, LANES), jnp.float32)
    cam_grads = coupling(DIM)
    pose_sums = [coupling(DIM + 1 + i) for i in range(2)]

    cam_row = lax.broadcasted_iota(jnp.int32, (width, LANES), 0)
    own_codes, far_codes = own1[MISC], got1[MISC]
    for place, (codes, row, base) in enumerate(
        ((own_codes, 0, panel), (far_codes, 1, other_panel), (far_codes, 0, other_panel), (own_codes, 1, panel))
    ):
        camera = codes[row : row + 1, :].astype(jnp.int32) + base * per_panel
        camera = jnp.where(camera >= width, camera - width, camera)
        chosen = jnp.broadcast_to(camera, (width, LANES)) == cam_row
        hot[:, place * LANES : (place + 1) * LANES] = jnp.where(chosen, 1.0, 0.0).astype(jnp.bfloat16)

    def spread(value, place):
        only = jnp.where(quarter == place, value, 0.0)
        only = only + pltpu.roll(only, 2 * frames, 1)
        return only + pltpu.roll(only, frames, 1)

    inverses, pose_grads = [], []
    for which in range(2):
        total = [pose_sums[i][2 * which] + pose_sums[i][2 * which + 1] for i in range(2)]
        columns = [spread(total[b // count], b % count) for b in range(DIM + 1)]
        pose_grads.append(columns[DIM])
        inverses.append(invert([columns[b] + jnp.where(sub == b, damp_pose, 0.0) for b in range(DIM)]))

    def solve_pose(which, value):
        result = inverses[which][0] * row_of(value, 0)
        for b in range(1, DIM):
            result = result + inverses[which][b] * row_of(value, b)
        return result

    def lanes_of(place):
        return slice(place * LANES, (place + 1) * LANES)

    def couple(which, seen):
        total = None
        for place in (2 * which, 2 * which + 1):
            for a in range(DIM):
                term = turned[place, pl.ds(a, SUB, stride=SUB), :] * row_of(seen[:, lanes_of(place)], a)
                total = term if total is None else total + term
        total = total + pltpu.roll(total, 2 * frames, 1)
        return total + pltpu.roll(total, frames, 1)

    def minus_spread(place, value, solved):
        for b in range(DIM):
            value = value - turned[place, b * SUB : (b + 1) * SUB, :] * row_of(solved, b)
        return value

    def look(vector):
        both = jnp.dot(halves(vector), hot[...], preferred_element_type=jnp.float32)
        return both[:SUB] + both[SUB:]

    def scatter(pieces):
        both = lax.dot_general(
            halves(jnp.concatenate(pieces, axis=1)), hot[...], NT, preferred_element_type=jnp.float32
        )
        return both[:SUB] + both[SUB:]

    def exchange(round_id, value):
        send[round_id] = value
        each_peer(
            lambda device: pltpu.make_async_remote_copy(
                src_ref=send.at[round_id],
                dst_ref=recv.at[round_id, me],
                send_sem=send_sem.at[round_id],
                recv_sem=recv_sem.at[round_id],
                device_id=device,
                device_id_type=MESH,
            ).start()
        )
        recv[round_id, pl.ds(me, 1)] = value[None]
        others = recv.at[round_id, pl.ds(0, peers - 1)]

        def finish():
            pltpu.make_async_copy(others, others, recv_sem.at[round_id]).wait()
            parts = [recv[round_id, source] for source in range(peers)]
            while len(parts) > 1:
                tail = [parts[-1]] if len(parts) % 2 else []
                parts = [a + b for a, b in zip(parts[::2], parts[1::2])] + tail
            return parts[0]

        return finish

    def drain(round_id):
        others = recv.at[round_id, pl.ds(0, peers - 1)]
        pltpu.make_async_copy(others, others, send_sem.at[round_id]).wait()

    solved = [solve_pose(which, pose_grads[which]) for which in range(2)]
    right_side = exchange(0, scatter([minus_spread(place, cam_grads[place], solved[place // 2]) for place in range(4)]))

    swaps[1].wait_recv()

    def curvature(b):
        return [
            own2[U_FRONT + b],
            choose(own_first, got2, U_BACK1, U_BACK0, b),
            got2[U_FRONT + b],
            choose(far_first, own2, U_BACK1, U_BACK0, b),
        ]

    blocks = [curvature(b) for b in range(DIM)]

    def apply(vector):
        seen = look(vector)
        pieces = []
        for which in range(2):
            result = solve_pose(which, couple(which, seen))
            for place in (2 * which, 2 * which + 1):
                value = blocks[0][place] * row_of(seen[:, lanes_of(place)], 0)
                for b in range(1, DIM):
                    value = value + blocks[b][place] * row_of(seen[:, lanes_of(place)], b)
                pieces.append(minus_spread(place, value, result))
        return scatter(pieces)

    def dot(left, right):
        return jnp.sum(jnp.sum(left * right, axis=1, keepdims=True), axis=0, keepdims=True)

    residual = -right_side()
    update = jnp.zeros_like(residual)
    direction = residual
    norm_now = dot(residual, residual)
    for iteration in range(ITERS):
        image = damp_camera * direction + exchange(iteration + 1, apply(direction))()
        size = norm_now / dot(direction, image)
        update = update + size * direction
        if iteration + 1 < ITERS:
            residual = residual - size * image
            norm_next = dot(residual, residual)
            direction = residual + norm_next / norm_now * direction
            norm_now = norm_next

    cam_out[...] = pltpu.roll(update, lax.rem(panels - panel, panels) * per_panel, 1)[:, :LANES]
    pose_out[...] = -solve_pose(0, pose_grads[0] + couple(0, look(update)))
    for swap in swaps:
        swap.wait_send()
    for round_id in range(ITERS + 1):
        drain(round_id)


def local(
    sizes,
    front_jc,
    front_jp,
    front_res,
    front_corners,
    front_cams,
    back_jc,
    back_jp,
    back_res,
    back_corners,
    back_cams,
    back_match,
    face,
    corner_gain,
):
    frames = face.shape[0]
    view_count = front_cams.shape[1]
    views = frames * view_count
    per_panel = CAM_DEV * sizes[1]
    width = sizes[0] * per_panel
    peers = sizes[0] // 2 * sizes[1] * sizes[2]

    def as_stored(jacobian):
        return jacobian.transpose(0, 1, 3, 2, 4).reshape(-1, LANES)

    pick = selection(view_count)
    smem = pl.BlockSpec(memory_space=pltpu.SMEM)
    vmem = pl.BlockSpec(memory_space=pltpu.VMEM)
    out = jax.ShapeDtypeStruct((SUB, LANES), jnp.float32)
    cam_rows, pose_rows = pl.pallas_call(
        functools.partial(step_kernel, sizes, per_panel, frames, view_count),
        in_specs=[smem] * 2 + [vmem] * 12,
        out_specs=(vmem, vmem),
        out_shape=(out, out),
        scratch_shapes=[
            pltpu.VMEM((3, views, LANES), jnp.float32),
            pltpu.VMEM((frames * SLOT, LANES), jnp.float32),
            pltpu.VMEM((frames * SLOT, LANES), jnp.float32),
            pltpu.VMEM((FIRST, SUB, LANES), jnp.float32),
            pltpu.VMEM((SECOND, SUB, LANES), jnp.float32),
            pltpu.VMEM((FIRST, SUB, LANES), jnp.float32),
            pltpu.VMEM((SECOND, SUB, LANES), jnp.float32),
            pltpu.VMEM((4, SUB * SUB, LANES), jnp.float32),
            pltpu.VMEM((width, 4 * LANES), jnp.bfloat16),
            pltpu.VMEM((ITERS + 1, SUB, width), jnp.float32),
            pltpu.VMEM((ITERS + 1, peers, SUB, width), jnp.float32),
            pltpu.SemaphoreType.DMA((2,)),
            pltpu.SemaphoreType.DMA((2,)),
            pltpu.SemaphoreType.DMA((ITERS + 1,)),
            pltpu.SemaphoreType.DMA((ITERS + 1,)),
        ],
        compiler_params=pltpu.CompilerParams(
            collective_id=0, has_side_effects=True, vmem_limit_bytes=48 * 1024 * 1024
        ),
        name="step",
    )(
        face,
        back_match,
        as_stored(front_jc),
        as_stored(front_jp),
        front_res.reshape(-1, LANES),
        front_corners.reshape(-1, LANES),
        front_cams.T,
        as_stored(back_jc),
        as_stored(back_jp),
        back_res.reshape(-1, LANES),
        back_corners.reshape(-1, LANES),
        back_cams.T,
        corner_gain.reshape(-1, LANES),
        pick,
    )
    return cam_rows[:DIM, :per_panel], pose_rows[:DIM, :frames]


def solution(mesh):
    wide = ("panel", "cam", "frame")
    sizes = tuple(mesh.shape[name] for name in wide)
    in_specs = (
        P(wide, None, None, None, None),
        P(wide, None, None, None, None),
        P(wide, None, None, None),
        P(wide, None, None),
        P(wide, None),
        P(wide, None, None, None, None),
        P(wide, None, None, None, None),
        P(wide, None, None, None),
        P(wide, None, None),
        P(wide, None),
        P(wide),
        P(wide),
        P(),
    )
    out_specs = (P(None, "panel"), P(None, wide))
    return jax.shard_map(
        functools.partial(local, sizes), mesh=mesh, in_specs=in_specs, out_specs=out_specs, check_vma=False
    )
```

```python
import functools

import jax
import jax.numpy as jnp
import numpy as np
from jax import lax
from jax.experimental import pallas as pl
from jax.experimental.pallas import tpu as pltpu
from jax.sharding import PartitionSpec as P

CAM_DEV = 8
ITERS = 4
LANES = 128
SLOT = 16
SUB = 8
DIM = 6
COORDS = 2

damp_pose = 0.1
damp_camera = 0.5
MESH = pl.DeviceIdType.MESH
NT = (((1,), (1,)), ((), ()))

BACK0, BACK1, FRONT, MISC, FIRST = 0, 9, 18, 27, 28
U_BACK0, U_BACK1, U_FRONT, SECOND = 0, 6, 12, 18


def selection(view_count):
    block = view_count * DIM * COORDS
    res_rows = view_count * COORDS
    table = np.zeros((2, COORDS, 2, view_count, SLOT, 4 * block + 4 * res_rows), np.float32)
    for parity in range(2):
        for coord in range(COORDS):
            for side in range(2):
                for view in range(view_count):
                    for a in range(DIM):
                        column = side * 2 * block + (view * DIM + a) * COORDS + coord
                        table[parity, coord, side, view, a, column] = 1
                        table[parity, coord, side, view, SUB + a, column + block] = 1
                    column = 4 * block + side * 2 * res_rows + parity * res_rows + view * COORDS + coord
                    table[parity, coord, side, view, SUB + DIM, column] = 1
    return jnp.asarray(table.reshape(2, COORDS * 2 * view_count * SLOT, -1), jnp.bfloat16)


def row_of(value, index):
    return jnp.broadcast_to(value[index : index + 1, :], (SUB, value.shape[1]))


def halves(value):
    high = value.astype(jnp.bfloat16)
    low = (value - high.astype(jnp.float32)).astype(jnp.bfloat16)
    return jnp.concatenate([high, low], axis=0)


def invert(working):
    sub = lax.broadcasted_iota(jnp.int32, working[0].shape, 0)
    inverse = [jnp.where(sub == row, 1.0, 0.0) for row in range(DIM)]
    working = list(working)
    for column in range(DIM):
        pivot = 1.0 / row_of(working[column], column)
        row_work = working[column] * pivot
        row_inverse = inverse[column] * pivot
        for row in range(DIM):
            if row == column:
                continue
            factor = row_of(working[row], column)
            working[row] = working[row] - factor * row_work
            inverse[row] = inverse[row] - factor * row_inverse
        working[column] = row_work
        inverse[column] = row_inverse
    return inverse


def step_kernel(
    sizes,
    per_panel,
    frames,
    view_count,
    *refs,
):
    stored, (cam_out, pose_out), held = refs[:14], refs[14:16], refs[16:30]
    step_body(sizes, per_panel, frames, view_count, stored, held, cam_out, pose_out, *held, *refs[30:])


def step_body(
    sizes,
    per_panel,
    frames,
    view_count,
    stored_refs,
    held_refs,
    cam_out,
    pose_out,
    face_s,
    match_s,
    gain,
    fcor,
    bcor,
    fjc,
    fjp,
    bjc,
    bjp,
    fres,
    bres,
    fcam,
    bcam,
    pick,
    weights,
    left,
    right,
    grams0,
    grams1,
    own1,
    own2,
    got1,
    got2,
    turned,
    hot,
    send,
    recv,
    swap_send,
    swap_recv,
    send_sem,
    recv_sem,
    load_sem,
):
    panels, cams, cores = sizes
    group = cams * cores
    half = panels // 2
    peers = half * group
    width = panels * per_panel
    views = frames * view_count
    table_rows = gain.shape[0] // 2
    panel = lax.axis_index("panel")
    cam = lax.axis_index("cam")
    core = lax.axis_index("frame")
    other_panel = lax.rem(panel + half, panels)
    partner = (other_panel, cam, core)
    side = panel // half
    me = (lax.rem(panel, half) * cams + cam) * cores + core

    def coords(device):
        return (side * half + device // group, (device // cores) % cams, device % cores)

    def each_peer(action):
        if peers <= 16:
            for offset in range(1, peers):
                action(coords(lax.rem(me + offset, peers)))
        else:

            @pl.loop(1, peers)
            def _(offset):
                action(coords(lax.rem(me + offset, peers)))

    loads = [
        pltpu.make_async_copy(source, target, load_sem.at[index])
        for index, (source, target) in enumerate(zip(stored_refs, held_refs))
    ]
    for load in loads:
        load.start()

    barrier = pltpu.get_barrier_semaphore()
    pl.semaphore_signal(barrier, inc=1, device_id=partner, device_id_type=MESH)
    each_peer(lambda device: pl.semaphore_signal(barrier, inc=1, device_id=device, device_id_type=MESH))

    def early():
        pl.semaphore_wait(barrier, peers)
        cam_out[...] = weights[0, :SUB, :]
        pose_out[...] = weights[0, :SUB, :]

    for load in loads[:5]:
        load.wait()

    sub = lax.broadcasted_iota(jnp.int32, (SUB, LANES), 0)
    lane = lax.broadcasted_iota(jnp.int32, (SUB, LANES), 1)

    def look_up(step, _):
        rows = pl.ds(pl.multiple_of(step * SUB, SUB), SUB)
        own_face = jnp.where(sub < view_count, face_s[2 * step], face_s[2 * step + 1]) == 0
        front, back = fcor[rows, :], bcor[rows, :]
        front_low, front_high = front & (LANES - 1), front // LANES
        back_low, back_high = back & (LANES - 1), back // LANES
        found = [jnp.zeros((SUB, LANES), jnp.float32)] * 3
        for entry in range(table_rows):
            table = [
                jnp.broadcast_to(gain[face * table_rows + entry : face * table_rows + entry + 1, :], (SUB, LANES))
                for face in range(2)
            ]
            mixed = jnp.where(own_face, table[0], table[1])
            here = back_high == entry
            for place, (source, low, mask) in enumerate(
                ((mixed, front_low, front_high == entry), (table[0], back_low, here), (table[1], back_low, here))
            ):
                picked = jnp.take_along_axis(source, low, axis=1, mode="promise_in_bounds")
                found[place] = jnp.where(mask, picked, found[place])
        for place in range(3):
            weights[place, rows, :] = found[place]
        return 0

    lax.fori_loop(0, views // SUB, look_up, 0)
    for load in loads[5:]:
        load.wait()

    block_rows = view_count * DIM * COORDS
    span = 2 * view_count * SLOT
    slot_view = lax.broadcasted_iota(jnp.int32, (SLOT, LANES), 1) // SLOT

    def prepare(step, _):
        for parity in range(2):
            frame = 2 * step + parity
            rows = pl.ds(pl.multiple_of(frame * block_rows, SLOT), block_rows)
            res_rows = pl.ds(pl.multiple_of(step * SLOT, SLOT), SLOT)
            stored = jnp.concatenate(
                [fjc[rows, :], fjp[rows, :], bjc[rows, :], bjp[rows, :], fres[res_rows, :], bres[res_rows, :]], axis=0
            )
            plain = jnp.dot(pick[parity], stored, preferred_element_type=jnp.float32)
            for coord in range(COORDS):
                part = plain[coord * span : (coord + 1) * span]
                lanes = slice(coord * LANES, (coord + 1) * LANES)
                left[frame, :, lanes] = part.astype(jnp.bfloat16)
                scaled = []
                for place in range(3):
                    for view in range(view_count):
                        weight = weights[place, pl.ds(frame * view_count + view, 1), :]
                        start = ((view_count if place else 0) + view) * SLOT
                        scaled.append(part[start : start + SLOT] * jnp.broadcast_to(weight, (SLOT, LANES)))
                right[frame, :, lanes] = jnp.concatenate(scaled, axis=0).astype(jnp.bfloat16)
        return 0

    def gram(frame, _):
        product = lax.dot_general(left[frame], right[frame], NT, preferred_element_type=jnp.float32)
        both = product[:SLOT, :LANES]
        for view in range(1, 2 * view_count):
            both = jnp.where(slot_view == view, product[view * SLOT : (view + 1) * SLOT, :LANES], both)
        start = view_count * SLOT
        last = product[start : start + SLOT, LANES:]
        for view in range(1, view_count):
            rows_of = product[start + view * SLOT : start + (view + 1) * SLOT, LANES:]
            last = jnp.where(slot_view[:, : last.shape[1]] == view, rows_of, last)
        out_rows = pl.ds(pl.multiple_of(frame * SLOT, SLOT), SLOT)
        grams0[out_rows, :] = both
        grams1[out_rows, : last.shape[1]] = last
        return 0

    lax.fori_loop(0, frames // 2, prepare, 0, unroll=True)
    lax.fori_loop(0, frames, gram, 0, unroll=True)
    quarter = lane // frames
    count = LANES // frames

    def turn(scratch, rows):
        result = []
        for quad in range(SLOT // count):
            block = jnp.concatenate(
                [scratch[pl.ds(quad * count + i, frames, stride=SLOT), :] for i in range(count)], axis=0
            )
            result.append(block.T[:rows])
        return result

    def swap_quarters(r):
        low = quarter < 2
        even = quarter % 2 == 0
        u0 = jnp.where(low, r[0], pltpu.roll(r[2], 2 * frames, 1))
        u1 = jnp.where(low, r[1], pltpu.roll(r[3], 2 * frames, 1))
        u2 = jnp.where(low, pltpu.roll(r[0], 2 * frames, 1), r[2])
        u3 = jnp.where(low, pltpu.roll(r[1], 2 * frames, 1), r[3])
        back = LANES - frames
        return [
            jnp.where(even, u0, pltpu.roll(u1, frames, 1)),
            jnp.where(even, pltpu.roll(u0, back, 1), u1),
            jnp.where(even, u2, pltpu.roll(u3, frames, 1)),
            jnp.where(even, pltpu.roll(u2, back, 1), u3),
        ]

    inverse_match = jnp.zeros((SUB, LANES), jnp.int32)
    in_frames = lane % frames
    face_row = jnp.zeros((SUB, LANES), jnp.float32)
    for frame in range(frames):
        inverse_match = jnp.where(in_frames == match_s[frame], frame, inverse_match)
        face_row = jnp.where(in_frames == frame, face_s[frame].astype(jnp.float32), face_row)
    home = quarter * frames + inverse_match

    def to_home(value):
        return jnp.take_along_axis(value, home, axis=1, mode="promise_in_bounds")

    def lay_out(turned_grams, first_view, message, place, u_place, order):
        columns = []
        sums = []
        for quad, tall in enumerate(turned_grams):
            pieces = [
                tall[(first_view + view) * SLOT : (first_view + view) * SLOT + SUB] for view in range(view_count)
            ]
            columns += swap_quarters(pieces)
            if quad >= 2:
                total = None
                for view in range(view_count):
                    start = (first_view + view) * SLOT + SUB
                    piece = tall[start : start + SUB]
                    total = piece if total is None else total + piece
                sums.append(jnp.where(sub < DIM, total, 0.0))
        for b in range(DIM):
            own2[u_place + b] = order(columns[b])
        for b in range(DIM + 1):
            own1[place + b] = order(columns[SUB + b])
        for i in range(2):
            own1[place + DIM + 1 + i] = order(sums[i])

    tall0 = turn(grams0, LANES)
    tall1 = turn(grams1, view_count * SLOT)
    lay_out(tall0, view_count, own1, BACK0, U_BACK0, to_home)
    lay_out(tall1, 0, own1, BACK1, U_BACK1, to_home)
    lay_out(tall0, 0, own1, FRONT, U_FRONT, lambda value: value)

    def code_row(ref):
        row = jnp.concatenate([ref[view : view + 1, :] for view in range(view_count)], axis=1)
        return jnp.broadcast_to(row, (SUB, LANES)).astype(jnp.float32)

    misc = jnp.where(sub == 0, code_row(fcam), to_home(code_row(bcam)))
    own1[MISC] = jnp.where(sub == 2, face_row, misc)

    pl.semaphore_wait(barrier, peers)
    swaps = [
        pltpu.make_async_remote_copy(
            src_ref=source,
            dst_ref=target,
            send_sem=swap_send.at[index],
            recv_sem=swap_recv.at[index],
            device_id=partner,
            device_id_type=MESH,
        )
        for index, (source, target) in enumerate(((own1, got1), (own2, got2)))
    ]
    for swap in swaps:
        swap.start()
    swaps[0].wait_recv()

    own_first = own1[MISC][2:3, :] < 0.5
    far_first = got1[MISC][2:3, :] < 0.5
    own_first = jnp.broadcast_to(own_first, (SUB, LANES))
    far_first = jnp.broadcast_to(far_first, (SUB, LANES))

    def choose(mask, ref, one, zero, index):
        return jnp.where(mask, ref[one + index], ref[zero + index])

    def coupling(index):
        return [
            own1[FRONT + index],
            choose(own_first, got1, BACK1, BACK0, index),
            got1[FRONT + index],
            choose(far_first, own1, BACK1, BACK0, index),
        ]

    for b in range(DIM):
        for place, value in enumerate(coupling(b)):
            turned[place, b * SUB : (b + 1) * SUB, :] = value
    for place in range(4):
        turned[place, DIM * SUB :, :] = jnp.zeros((2 * SUB, LANES), jnp.float32)
    cam_grads = coupling(DIM)
    pose_sums = [coupling(DIM + 1 + i) for i in range(2)]

    cam_row = lax.broadcasted_iota(jnp.int32, (width, LANES), 0)
    own_codes, far_codes = own1[MISC], got1[MISC]
    for place, (codes, row, base) in enumerate(
        ((own_codes, 0, panel), (far_codes, 1, other_panel), (far_codes, 0, other_panel), (own_codes, 1, panel))
    ):
        camera = codes[row : row + 1, :].astype(jnp.int32) + base * per_panel
        camera = jnp.where(camera >= width, camera - width, camera)
        chosen = jnp.broadcast_to(camera, (width, LANES)) == cam_row
        hot[:, place * LANES : (place + 1) * LANES] = jnp.where(chosen, 1.0, 0.0).astype(jnp.bfloat16)

    def spread(value, place):
        only = jnp.where(quarter == place, value, 0.0)
        only = only + pltpu.roll(only, 2 * frames, 1)
        return only + pltpu.roll(only, frames, 1)

    inverses, pose_grads = [], []
    for which in range(2):
        total = [pose_sums[i][2 * which] + pose_sums[i][2 * which + 1] for i in range(2)]
        columns = [spread(total[b // count], b % count) for b in range(DIM + 1)]
        pose_grads.append(columns[DIM])
        inverses.append(invert([columns[b] + jnp.where(sub == b, damp_pose, 0.0) for b in range(DIM)]))

    def solve_pose(which, value):
        result = inverses[which][0] * row_of(value, 0)
        for b in range(1, DIM):
            result = result + inverses[which][b] * row_of(value, b)
        return result

    def lanes_of(place):
        return slice(place * LANES, (place + 1) * LANES)

    def couple(which, seen):
        total = None
        for place in (2 * which, 2 * which + 1):
            for a in range(DIM):
                term = turned[place, pl.ds(a, SUB, stride=SUB), :] * row_of(seen[:, lanes_of(place)], a)
                total = term if total is None else total + term
        total = total + pltpu.roll(total, 2 * frames, 1)
        return total + pltpu.roll(total, frames, 1)

    def minus_spread(place, value, solved):
        for b in range(DIM):
            value = value - turned[place, b * SUB : (b + 1) * SUB, :] * row_of(solved, b)
        return value

    def look(vector):
        both = jnp.dot(halves(vector), hot[...], preferred_element_type=jnp.float32)
        return both[:SUB] + both[SUB:]

    def scatter(pieces):
        both = lax.dot_general(
            halves(jnp.concatenate(pieces, axis=1)), hot[...], NT, preferred_element_type=jnp.float32
        )
        return both[:SUB] + both[SUB:]

    def exchange(round_id, value):
        send[round_id] = value
        each_peer(
            lambda device: pltpu.make_async_remote_copy(
                src_ref=send.at[round_id],
                dst_ref=recv.at[round_id, me],
                send_sem=send_sem.at[round_id],
                recv_sem=recv_sem.at[round_id],
                device_id=device,
                device_id_type=MESH,
            ).start()
        )
        recv[round_id, pl.ds(me, 1)] = value[None]
        others = recv.at[round_id, pl.ds(0, peers - 1)]

        def finish():
            pltpu.make_async_copy(others, others, recv_sem.at[round_id]).wait()
            parts = [recv[round_id, source] for source in range(peers)]
            while len(parts) > 1:
                tail = [parts[-1]] if len(parts) % 2 else []
                parts = [a + b for a, b in zip(parts[::2], parts[1::2])] + tail
            return parts[0]

        return finish

    def drain(round_id):
        others = recv.at[round_id, pl.ds(0, peers - 1)]
        pltpu.make_async_copy(others, others, send_sem.at[round_id]).wait()

    solved = [solve_pose(which, pose_grads[which]) for which in range(2)]
    right_side = exchange(0, scatter([minus_spread(place, cam_grads[place], solved[place // 2]) for place in range(4)]))

    swaps[1].wait_recv()

    def curvature(b):
        return [
            own2[U_FRONT + b],
            choose(own_first, got2, U_BACK1, U_BACK0, b),
            got2[U_FRONT + b],
            choose(far_first, own2, U_BACK1, U_BACK0, b),
        ]

    blocks = [curvature(b) for b in range(DIM)]

    def apply(vector):
        seen = look(vector)
        pieces = []
        for which in range(2):
            result = solve_pose(which, couple(which, seen))
            for place in (2 * which, 2 * which + 1):
                value = blocks[0][place] * row_of(seen[:, lanes_of(place)], 0)
                for b in range(1, DIM):
                    value = value + blocks[b][place] * row_of(seen[:, lanes_of(place)], b)
                pieces.append(minus_spread(place, value, result))
        return scatter(pieces)

    def dot(left, right):
        return jnp.sum(jnp.sum(left * right, axis=1, keepdims=True), axis=0, keepdims=True)

    residual = -right_side()
    update = jnp.zeros_like(residual)
    direction = residual
    norm_now = dot(residual, residual)
    for iteration in range(ITERS):
        image = damp_camera * direction + exchange(iteration + 1, apply(direction))()
        size = norm_now / dot(direction, image)
        update = update + size * direction
        if iteration + 1 < ITERS:
            residual = residual - size * image
            norm_next = dot(residual, residual)
            direction = residual + norm_next / norm_now * direction
            norm_now = norm_next

    cam_out[...] = pltpu.roll(update, lax.rem(panels - panel, panels) * per_panel, 1)[:, :LANES]
    pose_out[...] = -solve_pose(0, pose_grads[0] + couple(0, look(update)))
    for swap in swaps:
        swap.wait_send()
    for round_id in range(ITERS + 1):
        drain(round_id)


def local(
    sizes,
    front_jc,
    front_jp,
    front_res,
    front_corners,
    front_cams,
    back_jc,
    back_jp,
    back_res,
    back_corners,
    back_cams,
    back_match,
    face,
    corner_gain,
):
    frames = face.shape[0]
    view_count = front_cams.shape[1]
    views = frames * view_count
    per_panel = CAM_DEV * sizes[1]
    width = sizes[0] * per_panel
    peers = sizes[0] // 2 * sizes[1] * sizes[2]

    def as_stored(jacobian):
        return jacobian.transpose(0, 1, 3, 2, 4).reshape(-1, LANES)

    arguments = (
        face,
        back_match,
        corner_gain.reshape(-1, LANES),
        front_corners.reshape(-1, LANES),
        back_corners.reshape(-1, LANES),
        as_stored(front_jc),
        as_stored(front_jp),
        as_stored(back_jc),
        as_stored(back_jp),
        front_res.reshape(-1, LANES),
        back_res.reshape(-1, LANES),
        front_cams.T,
        back_cams.T,
        selection(view_count),
    )
    spaces = [pltpu.SMEM] * 2 + [pltpu.VMEM] * 12
    vmem = pl.BlockSpec(memory_space=pltpu.VMEM)
    out = jax.ShapeDtypeStruct((SUB, LANES), jnp.float32)
    cam_rows, pose_rows = pl.pallas_call(
        functools.partial(step_kernel, sizes, per_panel, frames, view_count),
        in_specs=[pl.BlockSpec(memory_space=pltpu.HBM)] * len(arguments),
        out_specs=(vmem, vmem),
        out_shape=(out, out),
        scratch_shapes=[space(value.shape, value.dtype) for space, value in zip(spaces, arguments)]
        + [
            pltpu.VMEM((3, views, LANES), jnp.float32),
            pltpu.VMEM((frames, 2 * view_count * SLOT, COORDS * LANES), jnp.bfloat16),
            pltpu.VMEM((frames, 3 * view_count * SLOT, COORDS * LANES), jnp.bfloat16),
            pltpu.VMEM((frames * SLOT, LANES), jnp.float32),
            pltpu.VMEM((frames * SLOT, LANES), jnp.float32),
            pltpu.VMEM((FIRST, SUB, LANES), jnp.float32),
            pltpu.VMEM((SECOND, SUB, LANES), jnp.float32),
            pltpu.VMEM((FIRST, SUB, LANES), jnp.float32),
            pltpu.VMEM((SECOND, SUB, LANES), jnp.float32),
            pltpu.VMEM((4, SUB * SUB, LANES), jnp.float32),
            pltpu.VMEM((width, 4 * LANES), jnp.bfloat16),
            pltpu.VMEM((ITERS + 1, SUB, width), jnp.float32),
            pltpu.VMEM((ITERS + 1, peers, SUB, width), jnp.float32),
            pltpu.SemaphoreType.DMA((2,)),
            pltpu.SemaphoreType.DMA((2,)),
            pltpu.SemaphoreType.DMA((ITERS + 1,)),
            pltpu.SemaphoreType.DMA((ITERS + 1,)),
            pltpu.SemaphoreType.DMA((len(arguments),)),
        ],
        compiler_params=pltpu.CompilerParams(
            collective_id=0, has_side_effects=True, vmem_limit_bytes=60 * 1024 * 1024
        ),
        name="step",
    )(*arguments)
    return cam_rows[:DIM, :per_panel], pose_rows[:DIM, :frames]


def solution(mesh):
    wide = ("panel", "cam", "frame")
    sizes = tuple(mesh.shape[name] for name in wide)
    in_specs = (
        P(wide, None, None, None, None),
        P(wide, None, None, None, None),
        P(wide, None, None, None),
        P(wide, None, None),
        P(wide, None),
        P(wide, None, None, None, None),
        P(wide, None, None, None, None),
        P(wide, None, None, None),
        P(wide, None, None),
        P(wide, None),
        P(wide),
        P(wide),
        P(),
    )
    out_specs = (P(None, "panel"), P(None, wide))
    return jax.shard_map(
        functools.partial(local, sizes), mesh=mesh, in_specs=in_specs, out_specs=out_specs, check_vma=False
    )
```

```python
import functools

import jax
import jax.numpy as jnp
import numpy as np
from jax import lax
from jax.experimental import pallas as pl
from jax.experimental.pallas import tpu as pltpu
from jax.sharding import PartitionSpec as P

CAM_DEV = 8
ITERS = 4
LANES = 128
SLOT = 16
SUB = 8
DIM = 6
COORDS = 2

damp_pose = 0.1
damp_camera = 0.5
MESH = pl.DeviceIdType.MESH
NT = (((1,), (1,)), ((), ()))

GRAD, SUMS, PER_SET = 6, 7, 9
FRONT, BACK = 0, PER_SET


def selection(view_count):
    block = view_count * DIM * COORDS
    res_rows = view_count * COORDS
    table = np.zeros((2, COORDS, 2, view_count, SLOT, 4 * block + 4 * res_rows), np.float32)
    for parity in range(2):
        for coord in range(COORDS):
            for side in range(2):
                for view in range(view_count):
                    for a in range(DIM):
                        column = side * 2 * block + (view * DIM + a) * COORDS + coord
                        table[parity, coord, side, view, a, column] = 1
                        table[parity, coord, side, view, SUB + a, column + block] = 1
                    column = 4 * block + side * 2 * res_rows + parity * res_rows + view * COORDS + coord
                    table[parity, coord, side, view, SUB + DIM, column] = 1
    return jnp.asarray(table.reshape(2, COORDS * 2 * view_count * SLOT, -1), jnp.bfloat16)


def row_of(value, index):
    return jnp.broadcast_to(value[index : index + 1, :], (SUB, value.shape[1]))


def halves(value):
    high = value.astype(jnp.bfloat16)
    low = (value - high.astype(jnp.float32)).astype(jnp.bfloat16)
    return jnp.concatenate([high, low], axis=0)


def invert(working):
    sub = lax.broadcasted_iota(jnp.int32, working[0].shape, 0)
    inverse = [jnp.where(sub == row, 1.0, 0.0) for row in range(DIM)]
    working = list(working)
    for column in range(DIM):
        pivot = 1.0 / row_of(working[column], column)
        row_work = working[column] * pivot
        row_inverse = inverse[column] * pivot
        for row in range(DIM):
            if row == column:
                continue
            factor = row_of(working[row], column)
            working[row] = working[row] - factor * row_work
            inverse[row] = inverse[row] - factor * row_inverse
        working[column] = row_work
        inverse[column] = row_inverse
    return inverse


def step_kernel(
    sizes,
    per_panel,
    frames,
    view_count,
    *refs,
):
    stored, (cam_out, pose_out), held = refs[:14], refs[14:16], refs[16:30]
    step_body(sizes, per_panel, frames, view_count, stored, held, cam_out, pose_out, *held, *refs[30:])


def step_body(
    sizes,
    per_panel,
    frames,
    view_count,
    stored_refs,
    held_refs,
    cam_out,
    pose_out,
    face_s,
    match_s,
    gain,
    fcor,
    bcor,
    fjc,
    fjp,
    bjc,
    bjp,
    fres,
    bres,
    fcam,
    bcam,
    pick,
    weights,
    left,
    right,
    grams0,
    grams1,
    own0,
    own1,
    own2,
    got0,
    got1,
    got2,
    turned,
    hot,
    send,
    recv,
    swap_send,
    swap_recv,
    send_sem,
    recv_sem,
    load_sem,
):
    panels, cams, cores = sizes
    group = cams * cores
    half = panels // 2
    peers = half * group
    width = panels * per_panel
    views = frames * view_count
    table_rows = gain.shape[0] // 2
    panel = lax.axis_index("panel")
    cam = lax.axis_index("cam")
    core = lax.axis_index("frame")
    other_panel = lax.rem(panel + half, panels)
    partner = (other_panel, cam, core)
    side = panel // half
    me = (lax.rem(panel, half) * cams + cam) * cores + core

    def coords(device):
        return (side * half + device // group, (device // cores) % cams, device % cores)

    def each_peer(action):
        if peers <= 16:
            for offset in range(1, peers):
                action(coords(lax.rem(me + offset, peers)))
        else:

            @pl.loop(1, peers)
            def _(offset):
                action(coords(lax.rem(me + offset, peers)))

    loads = [
        pltpu.make_async_copy(source, target, load_sem.at[index])
        for index, (source, target) in enumerate(zip(stored_refs, held_refs))
    ]
    for load in loads:
        load.start()

    barrier = pltpu.get_barrier_semaphore()
    pl.semaphore_signal(barrier, inc=1, device_id=partner, device_id_type=MESH)
    each_peer(lambda device: pl.semaphore_signal(barrier, inc=1, device_id=device, device_id_type=MESH))

    for load in loads[:5]:
        load.wait()

    sub = lax.broadcasted_iota(jnp.int32, (SUB, LANES), 0)
    lane = lax.broadcasted_iota(jnp.int32, (SUB, LANES), 1)

    def look_up(step, _):
        rows = pl.ds(pl.multiple_of(step * SUB, SUB), SUB)
        own_face = jnp.where(sub < view_count, face_s[2 * step], face_s[2 * step + 1]) == 0
        front, back = fcor[rows, :], bcor[rows, :]
        front_low, front_high = front & (LANES - 1), front // LANES
        back_low, back_high = back & (LANES - 1), back // LANES
        found = [jnp.zeros((SUB, LANES), jnp.float32)] * 3
        for entry in range(table_rows):
            table = [
                jnp.broadcast_to(gain[face * table_rows + entry : face * table_rows + entry + 1, :], (SUB, LANES))
                for face in range(2)
            ]
            mixed = jnp.where(own_face, table[0], table[1])
            here = back_high == entry
            for place, (source, low, mask) in enumerate(
                ((mixed, front_low, front_high == entry), (table[0], back_low, here), (table[1], back_low, here))
            ):
                picked = jnp.take_along_axis(source, low, axis=1, mode="promise_in_bounds")
                found[place] = jnp.where(mask, picked, found[place])
        for place in range(3):
            weights[place, rows, :] = found[place]
        return 0

    lax.fori_loop(0, views // SUB, look_up, 0)
    for load in loads[5:]:
        load.wait()

    quarter = lane // frames
    count = LANES // frames
    inverse_match = jnp.zeros((SUB, LANES), jnp.int32)
    in_frames = lane % frames
    face_row = jnp.zeros((SUB, LANES), jnp.float32)
    for frame in range(frames):
        inverse_match = jnp.where(in_frames == match_s[frame], frame, inverse_match)
        face_row = jnp.where(in_frames == frame, face_s[frame].astype(jnp.float32), face_row)
    home = quarter * frames + inverse_match

    def to_home(value):
        return jnp.take_along_axis(value, home, axis=1, mode="promise_in_bounds")

    def code_row(ref):
        row = jnp.concatenate([ref[view : view + 1, :] for view in range(view_count)], axis=1)
        return jnp.broadcast_to(row, (SUB, LANES)).astype(jnp.float32)

    own0[...] = jnp.where(sub == 2, face_row, jnp.where(sub == 0, code_row(fcam), to_home(code_row(bcam))))

    def to_partner(source, target, index):
        return pltpu.make_async_remote_copy(
            src_ref=source,
            dst_ref=target,
            send_sem=swap_send.at[index],
            recv_sem=swap_recv.at[index],
            device_id=partner,
            device_id_type=MESH,
        )

    pl.semaphore_wait(barrier, peers)
    greeting = to_partner(own0, got0, 0)
    greeting.start()

    block_rows = view_count * DIM * COORDS
    span = 2 * view_count * SLOT
    slot_view = lax.broadcasted_iota(jnp.int32, (SLOT, LANES), 1) // SLOT

    def prepare(step, _):
        for parity in range(2):
            frame = 2 * step + parity
            rows = pl.ds(pl.multiple_of(frame * block_rows, SLOT), block_rows)
            res_rows = pl.ds(pl.multiple_of(step * SLOT, SLOT), SLOT)
            stored = jnp.concatenate(
                [fjc[rows, :], fjp[rows, :], bjc[rows, :], bjp[rows, :], fres[res_rows, :], bres[res_rows, :]], axis=0
            )
            plain = jnp.dot(pick[parity], stored, preferred_element_type=jnp.float32)
            for coord in range(COORDS):
                part = plain[coord * span : (coord + 1) * span]
                lanes = slice(coord * LANES, (coord + 1) * LANES)
                left[frame, :, lanes] = part.astype(jnp.bfloat16)
                scaled = []
                for place in range(3):
                    for view in range(view_count):
                        weight = weights[place, pl.ds(frame * view_count + view, 1), :]
                        start = ((view_count if place else 0) + view) * SLOT
                        scaled.append(part[start : start + SLOT] * jnp.broadcast_to(weight, (SLOT, LANES)))
                right[frame, :, lanes] = jnp.concatenate(scaled, axis=0).astype(jnp.bfloat16)
        return 0

    def gram(frame, _):
        product = lax.dot_general(left[frame], right[frame], NT, preferred_element_type=jnp.float32)
        both = product[:SLOT, :LANES]
        for view in range(1, 2 * view_count):
            both = jnp.where(slot_view == view, product[view * SLOT : (view + 1) * SLOT, :LANES], both)
        start = view_count * SLOT
        last = product[start : start + SLOT, LANES:]
        for view in range(1, view_count):
            rows_of = product[start + view * SLOT : start + (view + 1) * SLOT, LANES:]
            last = jnp.where(slot_view[:, : last.shape[1]] == view, rows_of, last)
        out_rows = pl.ds(pl.multiple_of(frame * SLOT, SLOT), SLOT)
        grams0[out_rows, :] = both
        grams1[out_rows, : last.shape[1]] = last
        return 0

    lax.fori_loop(0, frames // 2, prepare, 0, unroll=True)
    lax.fori_loop(0, frames, gram, 0, unroll=True)
    def turn(scratch, rows):
        result = []
        for quad in range(SLOT // count):
            block = jnp.concatenate(
                [scratch[pl.ds(quad * count + i, frames, stride=SLOT), :] for i in range(count)], axis=0
            )
            result.append(block.T[:rows])
        return result

    def swap_quarters(r):
        low = quarter < 2
        even = quarter % 2 == 0
        u0 = jnp.where(low, r[0], pltpu.roll(r[2], 2 * frames, 1))
        u1 = jnp.where(low, r[1], pltpu.roll(r[3], 2 * frames, 1))
        u2 = jnp.where(low, pltpu.roll(r[0], 2 * frames, 1), r[2])
        u3 = jnp.where(low, pltpu.roll(r[1], 2 * frames, 1), r[3])
        back = LANES - frames
        return [
            jnp.where(even, u0, pltpu.roll(u1, frames, 1)),
            jnp.where(even, pltpu.roll(u0, back, 1), u1),
            jnp.where(even, u2, pltpu.roll(u3, frames, 1)),
            jnp.where(even, pltpu.roll(u2, back, 1), u3),
        ]

    def lay_out(turned_grams, first_view, order):
        columns, sums = [], []
        for quad, tall in enumerate(turned_grams):
            starts = [(first_view + view) * SLOT for view in range(view_count)]
            columns += swap_quarters([tall[start : start + SUB] for start in starts])
            if quad >= 2:
                total = tall[starts[0] + SUB : starts[0] + SLOT]
                for start in starts[1:]:
                    total = total + tall[start + SUB : start + SLOT]
                sums.append(total)
        return [order(value) for value in columns[:DIM]], [order(value) for value in columns[SUB : SUB + GRAD + 1] + sums]

    def hot_columns(place, codes, row, base):
        camera = codes[row : row + 1, :].astype(jnp.int32) + base * per_panel
        camera = jnp.where(camera >= width, camera - width, camera)
        chosen = jnp.broadcast_to(camera, (width, LANES)) == lax.broadcasted_iota(jnp.int32, (width, LANES), 0)
        hot[:, place * LANES : (place + 1) * LANES] = jnp.where(chosen, 1.0, 0.0).astype(jnp.bfloat16)

    def lanes_of(place, places=1):
        return slice(place * LANES, (place + places) * LANES)

    def keep(place, ref, first):
        for b in range(DIM):
            turned[place, b * SUB : (b + 1) * SUB, :] = ref[first + b]

    tall0 = turn(grams0, LANES)
    tall1 = turn(grams1, view_count * SLOT)
    front_cam, front_rest = lay_out(tall0, 0, lambda value: value)
    for index, value in enumerate(front_rest):
        own1[FRONT + index] = value
    back0_cam, back0_rest = lay_out(tall0, view_count, to_home)
    back1_cam, back1_rest = lay_out(tall1, 0, to_home)
    for place in range(4):
        turned[place, DIM * SUB :, :] = jnp.zeros((2 * SUB, LANES), jnp.float32)
    keep(1, own1, FRONT)
    own_codes = own0[...]
    hot_columns(1, own_codes, 0, panel)
    hot_columns(2, own_codes, 1, panel)

    greeting.wait_recv()
    far_codes = got0[...]
    first_face = row_of(far_codes, 2) < 0.5
    for index, (zero, one) in enumerate(zip(back0_rest, back1_rest)):
        own1[BACK + index] = jnp.where(first_face, one, zero)
    swap = to_partner(own1.at[:, pl.ds(0, DIM)], got1.at[:, pl.ds(0, DIM)], 1)
    swap.start()

    stacked = jnp.concatenate(
        [
            jnp.concatenate([front, jnp.where(first_face, one, zero)], axis=1)
            for front, zero, one in zip(front_cam, back0_cam, back1_cam)
        ],
        axis=0,
    )
    summed = lax.dot_general(halves(stacked), hot[:, lanes_of(1, 2)], NT, preferred_element_type=jnp.float32)
    for b in range(DIM):
        rows = slice(b * SUB, (b + 1) * SUB)
        own2[b] = summed[rows] + summed[DIM * SUB + b * SUB : DIM * SUB + (b + 1) * SUB]
    swap_cam = to_partner(own2.at[:, pl.ds(0, DIM)], got2.at[:, pl.ds(0, DIM)], 2)
    swap_cam.start()
    keep(2, own1, BACK)
    hot_columns(0, far_codes, 1, other_panel)
    hot_columns(3, far_codes, 0, other_panel)
    swap.wait_recv()
    keep(0, got1, BACK)
    keep(3, got1, FRONT)
    cam_grads = [got1[BACK + GRAD], own1[FRONT + GRAD], own1[BACK + GRAD], got1[FRONT + GRAD]]

    def spread(value, place):
        only = jnp.where(quarter == place, value, 0.0)
        only = only + pltpu.roll(only, 2 * frames, 1)
        return only + pltpu.roll(only, frames, 1)

    inverses, pose_grads = [], []
    for back, front in ((got1, own1), (own1, got1)):
        total = [jnp.where(sub < DIM, back[BACK + SUMS + i] + front[FRONT + SUMS + i], 0.0) for i in range(2)]
        columns = [spread(total[b // count], b % count) for b in range(DIM + 1)]
        pose_grads.append(columns[DIM])
        inverses.append(invert([columns[b] + jnp.where(sub == b, damp_pose, 0.0) for b in range(DIM)]))

    def solve_pose(which, value):
        result = inverses[which][0] * row_of(value, 0)
        for b in range(1, DIM):
            result = result + inverses[which][b] * row_of(value, b)
        return result

    def couple(which, seen):
        total = None
        for place in (2 * which, 2 * which + 1):
            for a in range(DIM):
                term = turned[place, pl.ds(a, SUB, stride=SUB), :] * row_of(seen[:, lanes_of(place)], a)
                total = term if total is None else total + term
        total = total + pltpu.roll(total, 2 * frames, 1)
        return total + pltpu.roll(total, frames, 1)

    def minus_spread(place, value, solved):
        for b in range(DIM):
            value = value - turned[place, b * SUB : (b + 1) * SUB, :] * row_of(solved, b)
        return value

    def look(vector, places):
        both = jnp.dot(halves(vector), hot[:, lanes_of(0, places)], preferred_element_type=jnp.float32)
        return both[:SUB] + both[SUB:]

    def scatter(pieces):
        both = lax.dot_general(
            halves(jnp.concatenate(pieces, axis=1)), hot[...], NT, preferred_element_type=jnp.float32
        )
        return both[:SUB] + both[SUB:]

    def exchange(round_id, value):
        send[round_id] = value
        each_peer(
            lambda device: pltpu.make_async_remote_copy(
                src_ref=send.at[round_id, pl.ds(0, DIM)],
                dst_ref=recv.at[round_id, me, pl.ds(0, DIM)],
                send_sem=send_sem.at[round_id],
                recv_sem=recv_sem.at[round_id],
                device_id=device,
                device_id_type=MESH,
            ).start()
        )
        recv[round_id, pl.ds(me, 1)] = value[None]
        others = recv.at[round_id, pl.ds(0, peers - 1), pl.ds(0, DIM)]

        def finish():
            pltpu.make_async_copy(others, others, recv_sem.at[round_id]).wait()
            parts = [recv[round_id, source] for source in range(peers)]
            while len(parts) > 1:
                tail = [parts[-1]] if len(parts) % 2 else []
                parts = [a + b for a, b in zip(parts[::2], parts[1::2])] + tail
            return jnp.where(lax.broadcasted_iota(jnp.int32, (SUB, width), 0) < DIM, parts[0], 0.0)

        return finish

    def drain(round_id):
        others = recv.at[round_id, pl.ds(0, peers - 1), pl.ds(0, DIM)]
        pltpu.make_async_copy(others, others, send_sem.at[round_id]).wait()

    solved = [solve_pose(which, pose_grads[which]) for which in range(2)]
    right_side = exchange(0, scatter([minus_spread(place, cam_grads[place], solved[place // 2]) for place in range(4)]))

    swap_cam.wait_recv()
    blocks = [own2[b] + got2[b] for b in range(DIM)]

    def apply(vector):
        seen = look(vector, 4)
        pieces = []
        for which in range(2):
            result = solve_pose(which, couple(which, seen))
            for place in (2 * which, 2 * which + 1):
                pieces.append(minus_spread(place, jnp.zeros((SUB, LANES), jnp.float32), result))
        local_part = blocks[0] * row_of(vector, 0)
        for b in range(1, DIM):
            local_part = local_part + blocks[b] * row_of(vector, b)
        return local_part + scatter(pieces)

    def dot(left, right):
        return jnp.sum(jnp.sum(left * right, axis=1, keepdims=True), axis=0, keepdims=True)

    residual = -right_side()
    update = jnp.zeros_like(residual)
    direction = residual
    norm_now = dot(residual, residual)
    for iteration in range(ITERS):
        image = damp_camera * direction + exchange(iteration + 1, apply(direction))()
        size = norm_now / dot(direction, image)
        update = update + size * direction
        if iteration + 1 < ITERS:
            residual = residual - size * image
            norm_next = dot(residual, residual)
            direction = residual + norm_next / norm_now * direction
            norm_now = norm_next

    cam_out[...] = pltpu.roll(update, lax.rem(panels - panel, panels) * per_panel, 1)[:DIM, :per_panel]
    pose_out[...] = -solve_pose(0, pose_grads[0] + couple(0, look(update, 2)))[:DIM, :frames]
    for copy in (greeting, swap, swap_cam):
        copy.wait_send()
    for round_id in range(ITERS + 1):
        drain(round_id)


def local(
    sizes,
    front_jc,
    front_jp,
    front_res,
    front_corners,
    front_cams,
    back_jc,
    back_jp,
    back_res,
    back_corners,
    back_cams,
    back_match,
    face,
    corner_gain,
):
    frames = face.shape[0]
    view_count = front_cams.shape[1]
    views = frames * view_count
    per_panel = CAM_DEV * sizes[1]
    width = sizes[0] * per_panel
    peers = sizes[0] // 2 * sizes[1] * sizes[2]

    def as_stored(jacobian):
        return jacobian.transpose(0, 1, 3, 2, 4).reshape(-1, LANES)

    arguments = (
        face,
        back_match,
        corner_gain.reshape(-1, LANES),
        front_corners.reshape(-1, LANES),
        back_corners.reshape(-1, LANES),
        as_stored(front_jc),
        as_stored(front_jp),
        as_stored(back_jc),
        as_stored(back_jp),
        front_res.reshape(-1, LANES),
        back_res.reshape(-1, LANES),
        front_cams.T,
        back_cams.T,
        selection(view_count),
    )
    spaces = [pltpu.SMEM] * 2 + [pltpu.VMEM] * 12
    vmem = pl.BlockSpec(memory_space=pltpu.VMEM)
    return pl.pallas_call(
        functools.partial(step_kernel, sizes, per_panel, frames, view_count),
        in_specs=[pl.BlockSpec(memory_space=pltpu.HBM)] * len(arguments),
        out_specs=(vmem, vmem),
        out_shape=(
            jax.ShapeDtypeStruct((DIM, per_panel), jnp.float32),
            jax.ShapeDtypeStruct((DIM, frames), jnp.float32),
        ),
        scratch_shapes=[space(value.shape, value.dtype) for space, value in zip(spaces, arguments)]
        + [
            pltpu.VMEM((3, views, LANES), jnp.float32),
            pltpu.VMEM((frames, 2 * view_count * SLOT, COORDS * LANES), jnp.bfloat16),
            pltpu.VMEM((frames, 3 * view_count * SLOT, COORDS * LANES), jnp.bfloat16),
            pltpu.VMEM((frames * SLOT, LANES), jnp.float32),
            pltpu.VMEM((frames * SLOT, LANES), jnp.float32),
            pltpu.VMEM((SUB, LANES), jnp.float32),
            pltpu.VMEM((2 * PER_SET, SUB, LANES), jnp.float32),
            pltpu.VMEM((DIM, SUB, width), jnp.float32),
            pltpu.VMEM((SUB, LANES), jnp.float32),
            pltpu.VMEM((2 * PER_SET, SUB, LANES), jnp.float32),
            pltpu.VMEM((DIM, SUB, width), jnp.float32),
            pltpu.VMEM((4, SUB * SUB, LANES), jnp.float32),
            pltpu.VMEM((width, 4 * LANES), jnp.bfloat16),
            pltpu.VMEM((ITERS + 1, SUB, width), jnp.float32),
            pltpu.VMEM((ITERS + 1, peers, SUB, width), jnp.float32),
            pltpu.SemaphoreType.DMA((3,)),
            pltpu.SemaphoreType.DMA((3,)),
            pltpu.SemaphoreType.DMA((ITERS + 1,)),
            pltpu.SemaphoreType.DMA((ITERS + 1,)),
            pltpu.SemaphoreType.DMA((len(arguments),)),
        ],
        compiler_params=pltpu.CompilerParams(
            collective_id=0, has_side_effects=True, vmem_limit_bytes=60 * 1024 * 1024
        ),
        name="step",
    )(*arguments)


def solution(mesh):
    wide = ("panel", "cam", "frame")
    sizes = tuple(mesh.shape[name] for name in wide)
    in_specs = (
        P(wide, None, None, None, None),
        P(wide, None, None, None, None),
        P(wide, None, None, None),
        P(wide, None, None),
        P(wide, None),
        P(wide, None, None, None, None),
        P(wide, None, None, None, None),
        P(wide, None, None, None),
        P(wide, None, None),
        P(wide, None),
        P(wide),
        P(wide),
        P(),
    )
    out_specs = (P(None, "panel"), P(None, wide))
    return jax.shard_map(
        functools.partial(local, sizes), mesh=mesh, in_specs=in_specs, out_specs=out_specs, check_vma=False
    )
```

```python
import functools

import jax
import jax.numpy as jnp
import numpy as np
from jax import lax
from jax.experimental import pallas as pl
from jax.experimental.pallas import tpu as pltpu
from jax.sharding import PartitionSpec as P

CAM_DEV = 8
ITERS = 4
LANES = 128
SLOT = 16
SUB = 8
DIM = 6
COORDS = 2

damp_pose = 0.1
damp_camera = 0.5
MESH = pl.DeviceIdType.MESH
NT = (((1,), (1,)), ((), ()))

GRAD, SUMS, PER_SET = 6, 7, 9
FRONT, BACK = 0, PER_SET


def selection(view_count):
    block = view_count * DIM * COORDS
    res_rows = view_count * COORDS
    table = np.zeros((2, COORDS, 2, view_count, SLOT, 4 * block + 4 * res_rows), np.float32)
    for parity in range(2):
        for coord in range(COORDS):
            for side in range(2):
                for view in range(view_count):
                    for a in range(DIM):
                        column = side * 2 * block + (view * DIM + a) * COORDS + coord
                        table[parity, coord, side, view, a, column] = 1
                        table[parity, coord, side, view, SUB + a, column + block] = 1
                    column = 4 * block + side * 2 * res_rows + parity * res_rows + view * COORDS + coord
                    table[parity, coord, side, view, SUB + DIM, column] = 1
    return jnp.asarray(table.reshape(2, COORDS * 2 * view_count * SLOT, -1), jnp.bfloat16)


def row_of(value, index):
    return jnp.broadcast_to(value[index : index + 1, :], (SUB, value.shape[1]))


def halves(value):
    high = value.astype(jnp.bfloat16)
    low = (value - high.astype(jnp.float32)).astype(jnp.bfloat16)
    return jnp.concatenate([high, low], axis=0)


def invert(working):
    sub = lax.broadcasted_iota(jnp.int32, working[0].shape, 0)
    inverse = [jnp.where(sub == row, 1.0, 0.0) for row in range(DIM)]
    working = list(working)
    for column in range(DIM):
        pivot = 1.0 / row_of(working[column], column)
        row_work = working[column] * pivot
        row_inverse = inverse[column] * pivot
        for row in range(DIM):
            if row == column:
                continue
            factor = row_of(working[row], column)
            working[row] = working[row] - factor * row_work
            inverse[row] = inverse[row] - factor * row_inverse
        working[column] = row_work
        inverse[column] = row_inverse
    return inverse


def step_kernel(
    sizes,
    per_panel,
    frames,
    view_count,
    *refs,
):
    stored, (cam_out, pose_out), held = refs[:14], refs[14:16], refs[16:30]
    step_body(sizes, per_panel, frames, view_count, stored, held, cam_out, pose_out, *held, *refs[30:])


def step_body(
    sizes,
    per_panel,
    frames,
    view_count,
    stored_refs,
    held_refs,
    cam_out,
    pose_out,
    face_s,
    match_s,
    gain,
    fcor,
    bcor,
    fjc,
    fjp,
    bjc,
    bjp,
    fres,
    bres,
    fcam,
    bcam,
    pick,
    weights,
    left,
    right,
    grams0,
    grams1,
    own0,
    own1,
    own2,
    got0,
    got1,
    got2,
    turned,
    folded,
    upright,
    hot,
    send,
    recv,
    swap_send,
    swap_recv,
    send_sem,
    recv_sem,
    load_sem,
):
    panels, cams, cores = sizes
    group = cams * cores
    half = panels // 2
    peers = half * group
    width = panels * per_panel
    views = frames * view_count
    table_rows = gain.shape[0] // 2
    panel = lax.axis_index("panel")
    cam = lax.axis_index("cam")
    core = lax.axis_index("frame")
    other_panel = lax.rem(panel + half, panels)
    partner = (other_panel, cam, core)
    side = panel // half
    me = (lax.rem(panel, half) * cams + cam) * cores + core

    def coords(device):
        return (side * half + device // group, (device // cores) % cams, device % cores)

    def each_peer(action):
        if peers <= 16:
            for offset in range(1, peers):
                action(coords(lax.rem(me + offset, peers)))
        else:

            @pl.loop(1, peers)
            def _(offset):
                action(coords(lax.rem(me + offset, peers)))

    loads = [
        pltpu.make_async_copy(source, target, load_sem.at[index])
        for index, (source, target) in enumerate(zip(stored_refs, held_refs))
    ]
    for load in loads:
        load.start()

    barrier = pltpu.get_barrier_semaphore()
    pl.semaphore_signal(barrier, inc=1, device_id=partner, device_id_type=MESH)
    each_peer(lambda device: pl.semaphore_signal(barrier, inc=1, device_id=device, device_id_type=MESH))

    for load in loads[:5]:
        load.wait()

    sub = lax.broadcasted_iota(jnp.int32, (SUB, LANES), 0)
    lane = lax.broadcasted_iota(jnp.int32, (SUB, LANES), 1)

    def look_up(step, _):
        rows = pl.ds(pl.multiple_of(step * SUB, SUB), SUB)
        own_face = jnp.where(sub < view_count, face_s[2 * step], face_s[2 * step + 1]) == 0
        front, back = fcor[rows, :], bcor[rows, :]
        front_low, front_high = front & (LANES - 1), front // LANES
        back_low, back_high = back & (LANES - 1), back // LANES
        found = [jnp.zeros((SUB, LANES), jnp.float32)] * 3

        def table(entry, face):
            line = face * table_rows + entry
            return jnp.broadcast_to(gain[line : line + 1, :], (SUB, LANES))

        def pick_from(source, low):
            return jnp.take_along_axis(source, low, axis=1, mode="promise_in_bounds")

        for entry in range(table_rows):
            mixed = jnp.where(own_face, table(entry, 0), table(entry, 1))
            found[0] = jnp.where(front_high == entry, pick_from(mixed, front_low), found[0])
        for entry in range(table_rows):
            here = back_high == entry
            for face in range(2):
                found[1 + face] = jnp.where(here, pick_from(table(entry, face), back_low), found[1 + face])
        for place in range(3):
            weights[place, rows, :] = found[place]
        return 0

    for load in loads[5:]:
        load.wait()

    quarter = lane // frames
    count = LANES // frames
    inverse_match = jnp.zeros((SUB, LANES), jnp.int32)
    in_frames = lane % frames
    face_row = jnp.zeros((SUB, LANES), jnp.float32)
    for frame in range(frames):
        inverse_match = jnp.where(in_frames == match_s[frame], frame, inverse_match)
        face_row = jnp.where(in_frames == frame, face_s[frame].astype(jnp.float32), face_row)
    home = quarter * frames + inverse_match

    def to_home(value):
        return jnp.take_along_axis(value, home, axis=1, mode="promise_in_bounds")

    def code_row(ref):
        row = jnp.concatenate([ref[view : view + 1, :] for view in range(view_count)], axis=1)
        return jnp.broadcast_to(row, (SUB, LANES)).astype(jnp.float32)

    own0[...] = jnp.where(sub == 2, face_row, jnp.where(sub == 0, code_row(fcam), to_home(code_row(bcam))))

    def to_partner(source, target, index):
        return pltpu.make_async_remote_copy(
            src_ref=source,
            dst_ref=target,
            send_sem=swap_send.at[index],
            recv_sem=swap_recv.at[index],
            device_id=partner,
            device_id_type=MESH,
        )

    greeting = to_partner(own0, got0, 0)

    block_rows = view_count * DIM * COORDS
    span = 2 * view_count * SLOT
    slot_view = lax.broadcasted_iota(jnp.int32, (SLOT, LANES), 1) // SLOT

    def prepare(step, _):
        for parity in range(2):
            frame = 2 * step + parity
            rows = pl.ds(pl.multiple_of(frame * block_rows, SLOT), block_rows)
            res_rows = pl.ds(pl.multiple_of(step * SLOT, SLOT), SLOT)
            stored = jnp.concatenate(
                [fjc[rows, :], fjp[rows, :], bjc[rows, :], bjp[rows, :], fres[res_rows, :], bres[res_rows, :]], axis=0
            )
            plain = jnp.dot(pick[parity], stored, preferred_element_type=jnp.float32)
            for coord in range(COORDS):
                part = plain[coord * span : (coord + 1) * span]
                lanes = slice(coord * LANES, (coord + 1) * LANES)
                left[frame, :, lanes] = part.astype(jnp.bfloat16)
                scaled = []
                for place in range(3):
                    for view in range(view_count):
                        weight = weights[place, pl.ds(frame * view_count + view, 1), :]
                        start = ((view_count if place else 0) + view) * SLOT
                        scaled.append(part[start : start + SLOT] * jnp.broadcast_to(weight, (SLOT, LANES)))
                right[frame, :, lanes] = jnp.concatenate(scaled, axis=0).astype(jnp.bfloat16)
        return 0

    def gram(frame, _):
        product = lax.dot_general(left[frame], right[frame], NT, preferred_element_type=jnp.float32)
        both = product[:SLOT, :LANES]
        for view in range(1, 2 * view_count):
            both = jnp.where(slot_view == view, product[view * SLOT : (view + 1) * SLOT, :LANES], both)
        start = view_count * SLOT
        last = product[start : start + SLOT, LANES:]
        for view in range(1, view_count):
            rows_of = product[start + view * SLOT : start + (view + 1) * SLOT, LANES:]
            last = jnp.where(slot_view[:, : last.shape[1]] == view, rows_of, last)
        out_rows = pl.ds(pl.multiple_of(frame * SLOT, SLOT), SLOT)
        grams0[out_rows, :] = both
        grams1[out_rows, : last.shape[1]] = last
        return 0

    def weigh(step, _):
        look_up(step, _)
        return prepare(step, _)

    steps = frames // 2
    lax.fori_loop(0, steps // 4, weigh, 0, unroll=True)
    pl.semaphore_wait(barrier, peers)
    greeting.start()
    lax.fori_loop(steps // 4, steps, weigh, 0, unroll=True)
    lax.fori_loop(0, frames, gram, 0, unroll=True)
    def turn(scratch, rows):
        result = []
        for quad in range(SLOT // count):
            block = jnp.concatenate(
                [scratch[pl.ds(quad * count + i, frames, stride=SLOT), :] for i in range(count)], axis=0
            )
            result.append(block.T[:rows])
        return result

    def swap_quarters(r):
        low = quarter < 2
        even = quarter % 2 == 0
        u0 = jnp.where(low, r[0], pltpu.roll(r[2], 2 * frames, 1))
        u1 = jnp.where(low, r[1], pltpu.roll(r[3], 2 * frames, 1))
        u2 = jnp.where(low, pltpu.roll(r[0], 2 * frames, 1), r[2])
        u3 = jnp.where(low, pltpu.roll(r[1], 2 * frames, 1), r[3])
        back = LANES - frames
        return [
            jnp.where(even, u0, pltpu.roll(u1, frames, 1)),
            jnp.where(even, pltpu.roll(u0, back, 1), u1),
            jnp.where(even, u2, pltpu.roll(u3, frames, 1)),
            jnp.where(even, pltpu.roll(u2, back, 1), u3),
        ]

    def lay_out(turned_grams, first_view, order):
        columns, sums = [], []
        for quad, tall in enumerate(turned_grams):
            starts = [(first_view + view) * SLOT for view in range(view_count)]
            columns += swap_quarters([tall[start : start + SUB] for start in starts])
            if quad >= 2:
                total = tall[starts[0] + SUB : starts[0] + SLOT]
                for start in starts[1:]:
                    total = total + tall[start + SUB : start + SLOT]
                sums.append(total)
        return [order(value) for value in columns[:DIM]], [order(value) for value in columns[SUB : SUB + GRAD + 1] + sums]

    def hot_columns(place, codes, row, base):
        camera = codes[row : row + 1, :].astype(jnp.int32) + base * per_panel
        camera = jnp.where(camera >= width, camera - width, camera)
        chosen = jnp.broadcast_to(camera, (width, LANES)) == lax.broadcasted_iota(jnp.int32, (width, LANES), 0)
        hot[:, place * LANES : (place + 1) * LANES] = jnp.where(chosen, 1.0, 0.0).astype(jnp.bfloat16)

    def lanes_of(place, places=1):
        return slice(place * LANES, (place + places) * LANES)

    def keep(place, ref, first):
        for b in range(DIM):
            turned[place, b * SUB : (b + 1) * SUB, :] = ref[first + b]

    tall0 = turn(grams0, LANES)
    tall1 = turn(grams1, view_count * SLOT)
    front_cam, front_rest = lay_out(tall0, 0, lambda value: value)
    for index, value in enumerate(front_rest):
        own1[FRONT + index] = value
    back0_cam, back0_rest = lay_out(tall0, view_count, to_home)
    back1_cam, back1_rest = lay_out(tall1, 0, to_home)
    for place in range(4):
        turned[place, DIM * SUB :, :] = jnp.zeros((2 * SUB, LANES), jnp.float32)
    keep(1, own1, FRONT)
    own_codes = own0[...]
    hot_columns(1, own_codes, 0, panel)
    hot_columns(2, own_codes, 1, panel)

    greeting.wait_recv()
    far_codes = got0[...]
    first_face = row_of(far_codes, 2) < 0.5
    for index, (zero, one) in enumerate(zip(back0_rest, back1_rest)):
        own1[BACK + index] = jnp.where(first_face, one, zero)
    swap = to_partner(own1.at[:, pl.ds(0, DIM)], got1.at[:, pl.ds(0, DIM)], 1)
    swap.start()

    stacked = jnp.concatenate(
        [
            jnp.concatenate([front, jnp.where(first_face, one, zero)], axis=1)
            for front, zero, one in zip(front_cam, back0_cam, back1_cam)
        ],
        axis=0,
    )
    summed = lax.dot_general(halves(stacked), hot[:, lanes_of(1, 2)], NT, preferred_element_type=jnp.float32)
    for b in range(DIM):
        rows = slice(b * SUB, (b + 1) * SUB)
        own2[b] = summed[rows] + summed[DIM * SUB + b * SUB : DIM * SUB + (b + 1) * SUB]
    swap_cam = to_partner(own2.at[:, pl.ds(0, DIM)], got2.at[:, pl.ds(0, DIM)], 2)
    swap_cam.start()
    keep(2, own1, BACK)
    hot_columns(0, far_codes, 1, other_panel)
    hot_columns(3, far_codes, 0, other_panel)
    swap.wait_recv()
    keep(0, got1, BACK)
    keep(3, got1, FRONT)
    cam_grads = [got1[BACK + GRAD], own1[FRONT + GRAD], own1[BACK + GRAD], got1[FRONT + GRAD]]

    def spread(value, place):
        only = jnp.where(quarter == place, value, 0.0)
        only = only + pltpu.roll(only, 2 * frames, 1)
        return only + pltpu.roll(only, frames, 1)

    inverses, pose_grads = [], []
    for back, front in ((got1, own1), (own1, got1)):
        total = [jnp.where(sub < DIM, back[BACK + SUMS + i] + front[FRONT + SUMS + i], 0.0) for i in range(2)]
        columns = [spread(total[b // count], b % count) for b in range(DIM + 1)]
        pose_grads.append(columns[DIM])
        inverses.append(invert([columns[b] + jnp.where(sub == b, damp_pose, 0.0) for b in range(DIM)]))

    def solve_pose(which, value):
        result = inverses[which][0] * row_of(value, 0)
        for b in range(1, DIM):
            result = result + inverses[which][b] * row_of(value, b)
        return result

    def couple(which, seen):
        total = None
        for place in (2 * which, 2 * which + 1):
            for a in range(DIM):
                term = upright[place, a] * row_of(seen[:, lanes_of(place)], a)
                total = term if total is None else total + term
        total = total + pltpu.roll(total, 2 * frames, 1)
        return total + pltpu.roll(total, frames, 1)

    def minus_spread(place, value, solved):
        for b in range(DIM):
            value = value - turned[place, b * SUB : (b + 1) * SUB, :] * row_of(solved, b)
        return value

    def fold(place):
        for b in range(DIM):
            column = inverses[place // 2][b]
            total = turned[place, :SUB, :] * row_of(column, 0)
            for row in range(1, DIM):
                total = total + turned[place, row * SUB : (row + 1) * SUB, :] * row_of(column, row)
            folded[place, b] = total
            upright[place, b] = turned[place, pl.ds(b, SUB, stride=SUB), :]

    def look(vector, places):
        both = jnp.dot(halves(vector), hot[:, lanes_of(0, places)], preferred_element_type=jnp.float32)
        return both[:SUB] + both[SUB:]

    def scatter(pieces):
        both = lax.dot_general(
            halves(jnp.concatenate(pieces, axis=1)), hot[...], NT, preferred_element_type=jnp.float32
        )
        return both[:SUB] + both[SUB:]

    def exchange(round_id, value):
        send[round_id] = value
        each_peer(
            lambda device: pltpu.make_async_remote_copy(
                src_ref=send.at[round_id, pl.ds(0, DIM)],
                dst_ref=recv.at[round_id, me, pl.ds(0, DIM)],
                send_sem=send_sem.at[round_id],
                recv_sem=recv_sem.at[round_id],
                device_id=device,
                device_id_type=MESH,
            ).start()
        )
        recv[round_id, pl.ds(me, 1)] = value[None]
        others = recv.at[round_id, pl.ds(0, peers - 1), pl.ds(0, DIM)]

        def finish():
            pltpu.make_async_copy(others, others, recv_sem.at[round_id]).wait()
            parts = [recv[round_id, source] for source in range(peers)]
            while len(parts) > 1:
                tail = [parts[-1]] if len(parts) % 2 else []
                parts = [a + b for a, b in zip(parts[::2], parts[1::2])] + tail
            return jnp.where(lax.broadcasted_iota(jnp.int32, (SUB, width), 0) < DIM, parts[0], 0.0)

        return finish

    def drain(round_id):
        others = recv.at[round_id, pl.ds(0, peers - 1), pl.ds(0, DIM)]
        pltpu.make_async_copy(others, others, send_sem.at[round_id]).wait()

    solved = [solve_pose(which, pose_grads[which]) for which in range(2)]
    right_side = exchange(0, scatter([minus_spread(place, cam_grads[place], solved[place // 2]) for place in range(4)]))

    for place in range(4):
        fold(place)
    swap_cam.wait_recv()
    blocks = [own2[b] + got2[b] for b in range(DIM)]

    def apply(vector):
        seen = look(vector, 4)
        pieces = []
        for which in range(2):
            coupled = couple(which, seen)
            for place in (2 * which, 2 * which + 1):
                value = folded[place, 0] * row_of(coupled, 0)
                for b in range(1, DIM):
                    value = value + folded[place, b] * row_of(coupled, b)
                pieces.append(value)
        local_part = blocks[0] * row_of(vector, 0)
        for b in range(1, DIM):
            local_part = local_part + blocks[b] * row_of(vector, b)
        return local_part - scatter(pieces)

    def dot(left, right):
        return jnp.sum(jnp.sum(left * right, axis=1, keepdims=True), axis=0, keepdims=True)

    def pose_of(vector):
        return solve_pose(0, couple(0, look(vector, 2)))

    residual = -right_side()
    direction = residual
    update = jnp.zeros_like(residual)
    share = applied = apply(residual)
    norm_now = dot(residual, residual)
    for iteration in range(ITERS):
        finish = exchange(iteration + 1, share)
        if iteration + 1 == ITERS:
            pose_before = -solve_pose(0, pose_grads[0]) - pose_of(update)
            pose_along = pose_of(direction)
        image = damp_camera * direction + finish()
        if iteration + 1 < ITERS:
            applied_image = apply(image)
        size = norm_now / dot(direction, image)
        update = update + size * direction
        if iteration + 1 < ITERS:
            residual = residual - size * image
            applied = applied - size * applied_image
            norm_next = dot(residual, residual)
            ratio = norm_next / norm_now
            direction = residual + ratio * direction
            share = applied + ratio * share
            norm_now = norm_next

    cam_out[...] = pltpu.roll(update, lax.rem(panels - panel, panels) * per_panel, 1)[:DIM, :per_panel]
    pose_out[...] = (pose_before - size * pose_along)[:DIM, :frames]
    for copy in (greeting, swap, swap_cam):
        copy.wait_send()
    for round_id in range(ITERS + 1):
        drain(round_id)


def local(
    sizes,
    front_jc,
    front_jp,
    front_res,
    front_corners,
    front_cams,
    back_jc,
    back_jp,
    back_res,
    back_corners,
    back_cams,
    back_match,
    face,
    corner_gain,
):
    frames = face.shape[0]
    view_count = front_cams.shape[1]
    views = frames * view_count
    per_panel = CAM_DEV * sizes[1]
    width = sizes[0] * per_panel
    peers = sizes[0] // 2 * sizes[1] * sizes[2]

    def as_stored(jacobian):
        return jacobian.transpose(0, 1, 3, 2, 4).reshape(-1, LANES)

    arguments = (
        face,
        back_match,
        corner_gain.reshape(-1, LANES),
        front_corners.reshape(-1, LANES),
        back_corners.reshape(-1, LANES),
        as_stored(front_jc),
        as_stored(front_jp),
        as_stored(back_jc),
        as_stored(back_jp),
        front_res.reshape(-1, LANES),
        back_res.reshape(-1, LANES),
        front_cams.T,
        back_cams.T,
        selection(view_count),
    )
    spaces = [pltpu.SMEM] * 2 + [pltpu.VMEM] * 12
    vmem = pl.BlockSpec(memory_space=pltpu.VMEM)
    return pl.pallas_call(
        functools.partial(step_kernel, sizes, per_panel, frames, view_count),
        in_specs=[pl.BlockSpec(memory_space=pltpu.HBM)] * len(arguments),
        out_specs=(vmem, vmem),
        out_shape=(
            pltpu.VMEM((DIM, per_panel), jnp.float32),
            pltpu.VMEM((DIM, frames), jnp.float32),
        ),
        scratch_shapes=[space(value.shape, value.dtype) for space, value in zip(spaces, arguments)]
        + [
            pltpu.VMEM((3, views, LANES), jnp.float32),
            pltpu.VMEM((frames, 2 * view_count * SLOT, COORDS * LANES), jnp.bfloat16),
            pltpu.VMEM((frames, 3 * view_count * SLOT, COORDS * LANES), jnp.bfloat16),
            pltpu.VMEM((frames * SLOT, LANES), jnp.float32),
            pltpu.VMEM((frames * SLOT, LANES), jnp.float32),
            pltpu.VMEM((SUB, LANES), jnp.float32),
            pltpu.VMEM((2 * PER_SET, SUB, LANES), jnp.float32),
            pltpu.VMEM((DIM, SUB, width), jnp.float32),
            pltpu.VMEM((SUB, LANES), jnp.float32),
            pltpu.VMEM((2 * PER_SET, SUB, LANES), jnp.float32),
            pltpu.VMEM((DIM, SUB, width), jnp.float32),
            pltpu.VMEM((4, SUB * SUB, LANES), jnp.float32),
            pltpu.VMEM((4, DIM, SUB, LANES), jnp.float32),
            pltpu.VMEM((4, DIM, SUB, LANES), jnp.float32),
            pltpu.VMEM((width, 4 * LANES), jnp.bfloat16),
            pltpu.VMEM((ITERS + 1, SUB, width), jnp.float32),
            pltpu.VMEM((ITERS + 1, peers, SUB, width), jnp.float32),
            pltpu.SemaphoreType.DMA((3,)),
            pltpu.SemaphoreType.DMA((3,)),
            pltpu.SemaphoreType.DMA((ITERS + 1,)),
            pltpu.SemaphoreType.DMA((ITERS + 1,)),
            pltpu.SemaphoreType.DMA((len(arguments),)),
        ],
        compiler_params=pltpu.CompilerParams(
            collective_id=0, has_side_effects=True, vmem_limit_bytes=60 * 1024 * 1024
        ),
        name="step",
    )(*arguments)


def solution(mesh):
    wide = ("panel", "cam", "frame")
    sizes = tuple(mesh.shape[name] for name in wide)
    in_specs = (
        P(wide, None, None, None, None),
        P(wide, None, None, None, None),
        P(wide, None, None, None),
        P(wide, None, None),
        P(wide, None),
        P(wide, None, None, None, None),
        P(wide, None, None, None, None),
        P(wide, None, None, None),
        P(wide, None, None),
        P(wide, None),
        P(wide),
        P(wide),
        P(),
    )
    out_specs = (P(None, "panel"), P(None, wide))
    return jax.shard_map(
        functools.partial(local, sizes), mesh=mesh, in_specs=in_specs, out_specs=out_specs, check_vma=False
    )
```

```python
import functools

import jax
import jax.numpy as jnp
import numpy as np
from jax import lax
from jax.experimental import pallas as pl
from jax.experimental.pallas import tpu as pltpu
from jax.sharding import PartitionSpec as P

CAM_DEV = 8
ITERS = 4
LANES = 128
SLOT = 16
SUB = 8
DIM = 6
COORDS = 2

damp_pose = 0.1
damp_camera = 0.5
MESH = pl.DeviceIdType.MESH
NT = (((1,), (1,)), ((), ()))

GRAD, SUMS, PER_SET = 6, 7, 9
FRONT, BACK = 0, PER_SET


def selection(view_count):
    block = view_count * DIM * COORDS
    res_rows = view_count * COORDS
    table = np.zeros((2, COORDS, 2, view_count, SLOT, 4 * block + 4 * res_rows), np.float32)
    for parity in range(2):
        for coord in range(COORDS):
            for side in range(2):
                for view in range(view_count):
                    for a in range(DIM):
                        column = side * 2 * block + (view * DIM + a) * COORDS + coord
                        table[parity, coord, side, view, a, column] = 1
                        table[parity, coord, side, view, SUB + a, column + block] = 1
                    column = 4 * block + side * 2 * res_rows + parity * res_rows + view * COORDS + coord
                    table[parity, coord, side, view, SUB + DIM, column] = 1
    return jnp.asarray(table.reshape(2, COORDS * 2 * view_count * SLOT, -1), jnp.bfloat16)


def row_of(value, index):
    return jnp.broadcast_to(value[index : index + 1, :], (SUB, value.shape[1]))


def halves(value):
    high = value.astype(jnp.bfloat16)
    low = (value - high.astype(jnp.float32)).astype(jnp.bfloat16)
    return jnp.concatenate([high, low], axis=0)


def invert(working):
    sub = lax.broadcasted_iota(jnp.int32, working[0].shape, 0)
    inverse = [jnp.where(sub == row, 1.0, 0.0) for row in range(DIM)]
    working = list(working)
    for column in range(DIM):
        pivot = 1.0 / row_of(working[column], column)
        row_work = working[column] * pivot
        row_inverse = inverse[column] * pivot
        for row in range(DIM):
            if row == column:
                continue
            factor = row_of(working[row], column)
            working[row] = working[row] - factor * row_work
            inverse[row] = inverse[row] - factor * row_inverse
        working[column] = row_work
        inverse[column] = row_inverse
    return inverse


def step_kernel(
    sizes,
    per_panel,
    frames,
    view_count,
    *refs,
):
    stored, (cam_out, pose_out), held = refs[:14], refs[14:16], refs[16:30]
    step_body(sizes, per_panel, frames, view_count, stored, held, cam_out, pose_out, *held, *refs[30:])


def step_body(
    sizes,
    per_panel,
    frames,
    view_count,
    stored_refs,
    held_refs,
    cam_out,
    pose_out,
    face_s,
    match_s,
    gain,
    fcor,
    bcor,
    fjc,
    fjp,
    bjc,
    bjp,
    fres,
    bres,
    fcam,
    bcam,
    pick,
    weights,
    left,
    right,
    grams0,
    grams1,
    own0,
    own1,
    own2,
    got0,
    got1,
    got2,
    turned,
    folded,
    upright,
    hot,
    tall_hot,
    send,
    recv,
    swap_send,
    swap_recv,
    send_sem,
    recv_sem,
    load_sem,
):
    panels, cams, cores = sizes
    group = cams * cores
    half = panels // 2
    peers = half * group
    width = panels * per_panel
    views = frames * view_count
    table_rows = gain.shape[0] // 2
    panel = lax.axis_index("panel")
    cam = lax.axis_index("cam")
    core = lax.axis_index("frame")
    other_panel = lax.rem(panel + half, panels)
    partner = (other_panel, cam, core)
    side = panel // half
    me = (lax.rem(panel, half) * cams + cam) * cores + core

    near = lax.rem(panel, half)

    def device_at(panel_step, cam_step, core_step):
        place = side * half + lax.rem(near + panel_step, half)
        return (place, lax.rem(cam + cam_step, cams), lax.rem(core + core_step, cores))

    def flipped(bits, cam_step, core_step):
        place = panel
        for bit in range(bits.bit_length()):
            if bits >> bit & 1:
                place = place + 2**bit - 2 * 2**bit * lax.rem(near // 2**bit, 2)
        return (place, lax.rem(cam + cam_step, cams), lax.rem(core + core_step, cores))

    def each_peer(action):
        if peers <= 16:
            places = [(p, c, k) for p in range(half) for c in range(cams) for k in range(cores)][1:]
            for place in sorted(places, key=lambda place: -(place[0].bit_count() + place[1])):
                action((device_at if half & (half - 1) else flipped)(*place))
        else:

            @pl.loop(1, peers)
            def _(offset):
                action(device_at(offset // group, (offset // cores) % cams, offset % cores))

    loads = [
        pltpu.make_async_copy(source, target, load_sem.at[index])
        for index, (source, target) in enumerate(zip(stored_refs, held_refs))
    ]
    for load in loads:
        load.start()

    barrier = pltpu.get_barrier_semaphore()
    pl.semaphore_signal(barrier, inc=1, device_id=partner, device_id_type=MESH)
    each_peer(lambda device: pl.semaphore_signal(barrier, inc=1, device_id=device, device_id_type=MESH))

    for load in loads[:5]:
        load.wait()

    sub = lax.broadcasted_iota(jnp.int32, (SUB, LANES), 0)
    lane = lax.broadcasted_iota(jnp.int32, (SUB, LANES), 1)

    def look_up(step, _):
        rows = pl.ds(pl.multiple_of(step * SUB, SUB), SUB)
        own_face = jnp.where(sub < view_count, face_s[2 * step], face_s[2 * step + 1]) == 0
        front, back = fcor[rows, :], bcor[rows, :]
        front_low, front_high = front & (LANES - 1), front // LANES
        back_low, back_high = back & (LANES - 1), back // LANES
        found = [jnp.zeros((SUB, LANES), jnp.float32)] * 3

        def table(entry, face):
            line = face * table_rows + entry
            return jnp.broadcast_to(gain[line : line + 1, :], (SUB, LANES))

        def pick_from(source, low):
            return jnp.take_along_axis(source, low, axis=1, mode="promise_in_bounds")

        for entry in range(table_rows):
            mixed = jnp.where(own_face, table(entry, 0), table(entry, 1))
            found[0] = jnp.where(front_high == entry, pick_from(mixed, front_low), found[0])
        for entry in range(table_rows):
            here = back_high == entry
            for face in range(2):
                found[1 + face] = jnp.where(here, pick_from(table(entry, face), back_low), found[1 + face])
        for place in range(3):
            weights[place, rows, :] = found[place]
        return 0

    for load in loads[5:]:
        load.wait()

    quarter = lane // frames
    count = LANES // frames
    inverse_match = jnp.zeros((SUB, LANES), jnp.int32)
    in_frames = lane % frames
    face_row = jnp.zeros((SUB, LANES), jnp.float32)
    for frame in range(frames):
        inverse_match = jnp.where(in_frames == match_s[frame], frame, inverse_match)
        face_row = jnp.where(in_frames == frame, face_s[frame].astype(jnp.float32), face_row)
    home = quarter * frames + inverse_match

    def to_home(value):
        return jnp.take_along_axis(value, home, axis=1, mode="promise_in_bounds")

    def code_row(ref):
        row = jnp.concatenate([ref[view : view + 1, :] for view in range(view_count)], axis=1)
        return jnp.broadcast_to(row, (SUB, LANES)).astype(jnp.float32)

    own0[...] = jnp.where(sub == 2, face_row, jnp.where(sub == 0, code_row(fcam), to_home(code_row(bcam))))

    def to_partner(source, target, index):
        return pltpu.make_async_remote_copy(
            src_ref=source,
            dst_ref=target,
            send_sem=swap_send.at[index],
            recv_sem=swap_recv.at[index],
            device_id=partner,
            device_id_type=MESH,
        )

    greeting = to_partner(own0, got0, 0)

    block_rows = view_count * DIM * COORDS
    span = 2 * view_count * SLOT
    slot_view = lax.broadcasted_iota(jnp.int32, (SLOT, LANES), 1) // SLOT

    def prepare(step, _):
        for parity in range(2):
            frame = 2 * step + parity
            rows = pl.ds(pl.multiple_of(frame * block_rows, SLOT), block_rows)
            res_rows = pl.ds(pl.multiple_of(step * SLOT, SLOT), SLOT)
            stored = jnp.concatenate(
                [fjc[rows, :], fjp[rows, :], bjc[rows, :], bjp[rows, :], fres[res_rows, :], bres[res_rows, :]], axis=0
            )
            plain = jnp.dot(pick[parity], stored, preferred_element_type=jnp.float32)
            for coord in range(COORDS):
                part = plain[coord * span : (coord + 1) * span]
                lanes = slice(coord * LANES, (coord + 1) * LANES)
                left[frame, :, lanes] = part.astype(jnp.bfloat16)
                scaled = []
                for place in range(3):
                    for view in range(view_count):
                        weight = weights[place, pl.ds(frame * view_count + view, 1), :]
                        start = ((view_count if place else 0) + view) * SLOT
                        scaled.append(part[start : start + SLOT] * jnp.broadcast_to(weight, (SLOT, LANES)))
                right[frame, :, lanes] = jnp.concatenate(scaled, axis=0).astype(jnp.bfloat16)
        return 0

    def gram(frame, _):
        product = lax.dot_general(left[frame], right[frame], NT, preferred_element_type=jnp.float32)
        both = product[:SLOT, :LANES]
        for view in range(1, 2 * view_count):
            both = jnp.where(slot_view == view, product[view * SLOT : (view + 1) * SLOT, :LANES], both)
        start = view_count * SLOT
        last = product[start : start + SLOT, LANES:]
        for view in range(1, view_count):
            rows_of = product[start + view * SLOT : start + (view + 1) * SLOT, LANES:]
            last = jnp.where(slot_view[:, : last.shape[1]] == view, rows_of, last)
        out_rows = pl.ds(pl.multiple_of(frame * SLOT, SLOT), SLOT)
        grams0[out_rows, :] = both
        grams1[out_rows, : last.shape[1]] = last
        return 0

    def weigh(step, _):
        look_up(step, _)
        return prepare(step, _)

    steps = frames // 2
    lax.fori_loop(0, steps // 4, weigh, 0, unroll=True)
    pl.semaphore_wait(barrier, peers)
    greeting.start()
    lax.fori_loop(steps // 4, steps, weigh, 0, unroll=True)
    lax.fori_loop(0, frames, gram, 0, unroll=True)
    def turn(scratch, rows):
        result = []
        for quad in range(SLOT // count):
            block = jnp.concatenate(
                [scratch[pl.ds(quad * count + i, frames, stride=SLOT), :] for i in range(count)], axis=0
            )
            result.append(block.T[:rows])
        return result

    def swap_quarters(r):
        low = quarter < 2
        even = quarter % 2 == 0
        u0 = jnp.where(low, r[0], pltpu.roll(r[2], 2 * frames, 1))
        u1 = jnp.where(low, r[1], pltpu.roll(r[3], 2 * frames, 1))
        u2 = jnp.where(low, pltpu.roll(r[0], 2 * frames, 1), r[2])
        u3 = jnp.where(low, pltpu.roll(r[1], 2 * frames, 1), r[3])
        back = LANES - frames
        return [
            jnp.where(even, u0, pltpu.roll(u1, frames, 1)),
            jnp.where(even, pltpu.roll(u0, back, 1), u1),
            jnp.where(even, u2, pltpu.roll(u3, frames, 1)),
            jnp.where(even, pltpu.roll(u2, back, 1), u3),
        ]

    def lay_out(turned_grams, first_view, order):
        columns, sums = [], []
        for quad, tall in enumerate(turned_grams):
            starts = [(first_view + view) * SLOT for view in range(view_count)]
            columns += swap_quarters([tall[start : start + SUB] for start in starts])
            if quad >= 2:
                total = tall[starts[0] + SUB : starts[0] + SLOT]
                for start in starts[1:]:
                    total = total + tall[start + SUB : start + SLOT]
                sums.append(total)
        return [order(value) for value in columns[:DIM]], [order(value) for value in columns[SUB : SUB + GRAD + 1] + sums]

    def hot_columns(place, codes, row, base):
        camera = codes[row : row + 1, :].astype(jnp.int32) + base * per_panel
        camera = jnp.where(camera >= width, camera - width, camera)
        chosen = jnp.broadcast_to(camera, (width, LANES)) == lax.broadcasted_iota(jnp.int32, (width, LANES), 0)
        hot[:, place * LANES : (place + 1) * LANES] = jnp.where(chosen, 1.0, 0.0).astype(jnp.bfloat16)

    def lanes_of(place, places=1):
        return slice(place * LANES, (place + places) * LANES)

    def keep(place, ref, first):
        for b in range(DIM):
            turned[place, b * SUB : (b + 1) * SUB, :] = ref[first + b]

    tall0 = turn(grams0, LANES)
    tall1 = turn(grams1, view_count * SLOT)
    front_cam, front_rest = lay_out(tall0, 0, lambda value: value)
    for index, value in enumerate(front_rest):
        own1[FRONT + index] = value

    def part(ref, first):
        return ref.at[pl.ds(first, PER_SET), pl.ds(0, DIM)]

    swap_front = to_partner(part(own1, FRONT), part(got1, FRONT), 1)
    swap_front.start()
    back0_cam, back0_rest = lay_out(tall0, view_count, to_home)
    back1_cam, back1_rest = lay_out(tall1, 0, to_home)
    for place in range(4):
        turned[place, DIM * SUB :, :] = jnp.zeros((2 * SUB, LANES), jnp.float32)
    keep(1, own1, FRONT)
    own_codes = own0[...]
    hot_columns(1, own_codes, 0, panel)
    hot_columns(2, own_codes, 1, panel)

    greeting.wait_recv()
    far_codes = got0[...]
    first_face = row_of(far_codes, 2) < 0.5
    for index, (zero, one) in enumerate(zip(back0_rest, back1_rest)):
        own1[BACK + index] = jnp.where(first_face, one, zero)
    swap_back = to_partner(part(own1, BACK), part(got1, BACK), 2)
    swap_back.start()

    stacked = jnp.concatenate(
        [
            jnp.concatenate([front, jnp.where(first_face, one, zero)], axis=1)
            for front, zero, one in zip(front_cam, back0_cam, back1_cam)
        ],
        axis=0,
    )
    summed = lax.dot_general(halves(stacked), hot[:, lanes_of(1, 2)], NT, preferred_element_type=jnp.float32)
    for b in range(DIM):
        rows = slice(b * SUB, (b + 1) * SUB)
        own2[b] = summed[rows] + summed[DIM * SUB + b * SUB : DIM * SUB + (b + 1) * SUB]
    swap_cam = to_partner(own2.at[:, pl.ds(0, DIM)], got2.at[:, pl.ds(0, DIM)], 3)
    swap_cam.start()
    keep(2, own1, BACK)
    hot_columns(0, far_codes, 1, other_panel)
    hot_columns(3, far_codes, 0, other_panel)
    swap_front.wait_recv()
    keep(3, got1, FRONT)
    swap_back.wait_recv()
    keep(0, got1, BACK)
    cam_grads = [got1[BACK + GRAD], own1[FRONT + GRAD], own1[BACK + GRAD], got1[FRONT + GRAD]]

    def spread(value, place):
        only = jnp.where(quarter == place, value, 0.0)
        only = only + pltpu.roll(only, 2 * frames, 1)
        return only + pltpu.roll(only, frames, 1)

    inverses, pose_grads = [], []
    for back, front in ((got1, own1), (own1, got1)):
        total = [jnp.where(sub < DIM, back[BACK + SUMS + i] + front[FRONT + SUMS + i], 0.0) for i in range(2)]
        columns = [spread(total[b // count], b % count) for b in range(DIM + 1)]
        pose_grads.append(columns[DIM])
        inverses.append(invert([columns[b] + jnp.where(sub == b, damp_pose, 0.0) for b in range(DIM)]))

    def solve_pose(which, value):
        result = inverses[which][0] * row_of(value, 0)
        for b in range(1, DIM):
            result = result + inverses[which][b] * row_of(value, b)
        return result

    def couple(which, seen):
        total = None
        for place in (2 * which, 2 * which + 1):
            for a in range(DIM):
                term = upright[place, a] * row_of(seen[:, lanes_of(place)], a)
                total = term if total is None else total + term
        total = total + pltpu.roll(total, 2 * frames, 1)
        return total + pltpu.roll(total, frames, 1)

    def minus_spread(place, value, solved):
        for b in range(DIM):
            value = value - turned[place, b * SUB : (b + 1) * SUB, :] * row_of(solved, b)
        return value

    def fold(place):
        for b in range(DIM):
            column = inverses[place // 2][b]
            total = turned[place, :SUB, :] * row_of(column, 0)
            for row in range(1, DIM):
                total = total + turned[place, row * SUB : (row + 1) * SUB, :] * row_of(column, row)
            folded[place, b] = total
            upright[place, b] = turned[place, pl.ds(b, SUB, stride=SUB), :]

    def look(vector, places):
        both = jnp.dot(halves(vector), hot[:, lanes_of(0, places)], preferred_element_type=jnp.float32)
        return both[:SUB] + both[SUB:]

    def scatter(pieces):
        both = lax.dot_general(
            halves(jnp.concatenate(pieces, axis=1)), hot[...], NT, preferred_element_type=jnp.float32
        )
        return both[:SUB] + both[SUB:]

    def exchange(round_id, value):
        send[round_id] = value
        each_peer(
            lambda device: pltpu.make_async_remote_copy(
                src_ref=send.at[round_id, pl.ds(0, DIM)],
                dst_ref=recv.at[round_id, me, pl.ds(0, DIM)],
                send_sem=send_sem.at[round_id],
                recv_sem=recv_sem.at[round_id],
                device_id=device,
                device_id_type=MESH,
            ).start()
        )
        recv[round_id, pl.ds(me, 1)] = value[None]
        others = recv.at[round_id, pl.ds(0, peers - 1), pl.ds(0, DIM)]

        def finish():
            pltpu.make_async_copy(others, others, recv_sem.at[round_id]).wait()
            parts = [recv[round_id, source] for source in range(peers)]
            while len(parts) > 1:
                tail = [parts[-1]] if len(parts) % 2 else []
                parts = [a + b for a, b in zip(parts[::2], parts[1::2])] + tail
            return jnp.where(lax.broadcasted_iota(jnp.int32, (SUB, width), 0) < DIM, parts[0], 0.0)

        return finish

    def drain(round_id):
        others = recv.at[round_id, pl.ds(0, peers - 1), pl.ds(0, DIM)]
        pltpu.make_async_copy(others, others, send_sem.at[round_id]).wait()

    solved = [solve_pose(which, pose_grads[which]) for which in range(2)]
    right_side = exchange(0, scatter([minus_spread(place, cam_grads[place], solved[place // 2]) for place in range(4)]))

    for place in range(4):
        fold(place)
        tall_hot[lanes_of(place), :] = hot[:, lanes_of(place)].astype(jnp.float32).T.astype(jnp.bfloat16)
    swap_cam.wait_recv()
    blocks = [own2[b] + got2[b] for b in range(DIM)]

    def apply(vector):
        seen = look(vector, 4)
        pieces = []
        for which in range(2):
            coupled = couple(which, seen)
            for place in (2 * which, 2 * which + 1):
                value = folded[place, 0] * row_of(coupled, 0)
                for b in range(1, DIM):
                    value = value + folded[place, b] * row_of(coupled, b)
                pieces.append(value)
        local_part = blocks[0] * row_of(vector, 0)
        for b in range(1, DIM):
            local_part = local_part + blocks[b] * row_of(vector, b)
        both = jnp.dot(halves(jnp.concatenate(pieces, axis=1)), tall_hot[...], preferred_element_type=jnp.float32)
        return local_part - (both[:SUB] + both[SUB:])

    def dot(left, right):
        return jnp.sum(jnp.sum(left * right, axis=1, keepdims=True), axis=0, keepdims=True)

    def pose_of(vector):
        return solve_pose(0, couple(0, look(vector, 2)))

    residual = -right_side()
    direction = residual
    update = jnp.zeros_like(residual)
    share = applied = apply(residual)
    norm_now = dot(residual, residual)
    for iteration in range(ITERS):
        finish = exchange(iteration + 1, share)
        if iteration + 1 == ITERS:
            pose_before = -solve_pose(0, pose_grads[0]) - pose_of(update)
            pose_along = pose_of(direction)
        image = damp_camera * direction + finish()
        if iteration + 1 < ITERS:
            applied_image = apply(image)
        size = norm_now / dot(direction, image)
        update = update + size * direction
        if iteration + 1 < ITERS:
            residual = residual - size * image
            applied = applied - size * applied_image
            norm_next = dot(residual, residual)
            ratio = norm_next / norm_now
            direction = residual + ratio * direction
            share = applied + ratio * share
            norm_now = norm_next

    cam_out[...] = pltpu.roll(update, lax.rem(panels - panel, panels) * per_panel, 1)[:DIM, :per_panel]
    pose_out[...] = (pose_before - size * pose_along)[:DIM, :frames]
    for copy in (greeting, swap_front, swap_back, swap_cam):
        copy.wait_send()
    for round_id in range(ITERS + 1):
        drain(round_id)


def local(
    sizes,
    front_jc,
    front_jp,
    front_res,
    front_corners,
    front_cams,
    back_jc,
    back_jp,
    back_res,
    back_corners,
    back_cams,
    back_match,
    face,
    corner_gain,
):
    frames = face.shape[0]
    view_count = front_cams.shape[1]
    views = frames * view_count
    per_panel = CAM_DEV * sizes[1]
    width = sizes[0] * per_panel
    peers = sizes[0] // 2 * sizes[1] * sizes[2]

    def as_stored(jacobian):
        return jacobian.transpose(0, 1, 3, 2, 4).reshape(-1, LANES)

    arguments = (
        face,
        back_match,
        corner_gain.reshape(-1, LANES),
        front_corners.reshape(-1, LANES),
        back_corners.reshape(-1, LANES),
        as_stored(front_jc),
        as_stored(front_jp),
        as_stored(back_jc),
        as_stored(back_jp),
        front_res.reshape(-1, LANES),
        back_res.reshape(-1, LANES),
        front_cams.T,
        back_cams.T,
        selection(view_count),
    )
    spaces = [pltpu.SMEM] * 2 + [pltpu.VMEM] * 12
    vmem = pl.BlockSpec(memory_space=pltpu.VMEM)
    return pl.pallas_call(
        functools.partial(step_kernel, sizes, per_panel, frames, view_count),
        in_specs=[pl.BlockSpec(memory_space=pltpu.HBM)] * len(arguments),
        out_specs=(vmem, vmem),
        out_shape=(
            pltpu.VMEM((DIM, per_panel), jnp.float32),
            pltpu.VMEM((DIM, frames), jnp.float32),
        ),
        scratch_shapes=[space(value.shape, value.dtype) for space, value in zip(spaces, arguments)]
        + [
            pltpu.VMEM((3, views, LANES), jnp.float32),
            pltpu.VMEM((frames, 2 * view_count * SLOT, COORDS * LANES), jnp.bfloat16),
            pltpu.VMEM((frames, 3 * view_count * SLOT, COORDS * LANES), jnp.bfloat16),
            pltpu.VMEM((frames * SLOT, LANES), jnp.float32),
            pltpu.VMEM((frames * SLOT, LANES), jnp.float32),
            pltpu.VMEM((SUB, LANES), jnp.float32),
            pltpu.VMEM((2 * PER_SET, SUB, LANES), jnp.float32),
            pltpu.VMEM((DIM, SUB, width), jnp.float32),
            pltpu.VMEM((SUB, LANES), jnp.float32),
            pltpu.VMEM((2 * PER_SET, SUB, LANES), jnp.float32),
            pltpu.VMEM((DIM, SUB, width), jnp.float32),
            pltpu.VMEM((4, SUB * SUB, LANES), jnp.float32),
            pltpu.VMEM((4, DIM, SUB, LANES), jnp.float32),
            pltpu.VMEM((4, DIM, SUB, LANES), jnp.float32),
            pltpu.VMEM((width, 4 * LANES), jnp.bfloat16),
            pltpu.VMEM((4 * LANES, width), jnp.bfloat16),
            pltpu.VMEM((ITERS + 1, SUB, width), jnp.float32),
            pltpu.VMEM((ITERS + 1, peers, SUB, width), jnp.float32),
            pltpu.SemaphoreType.DMA((4,)),
            pltpu.SemaphoreType.DMA((4,)),
            pltpu.SemaphoreType.DMA((ITERS + 1,)),
            pltpu.SemaphoreType.DMA((ITERS + 1,)),
            pltpu.SemaphoreType.DMA((len(arguments),)),
        ],
        compiler_params=pltpu.CompilerParams(
            collective_id=0, has_side_effects=True, vmem_limit_bytes=60 * 1024 * 1024
        ),
        name="step",
    )(*arguments)


def solution(mesh):
    wide = ("panel", "cam", "frame")
    sizes = tuple(mesh.shape[name] for name in wide)
    in_specs = (
        P(wide, None, None, None, None),
        P(wide, None, None, None, None),
        P(wide, None, None, None),
        P(wide, None, None),
        P(wide, None),
        P(wide, None, None, None, None),
        P(wide, None, None, None, None),
        P(wide, None, None, None),
        P(wide, None, None),
        P(wide, None),
        P(wide),
        P(wide),
        P(),
    )
    out_specs = (P(None, "panel"), P(None, wide))
    return jax.shard_map(
        functools.partial(local, sizes), mesh=mesh, in_specs=in_specs, out_specs=out_specs, check_vma=False
    )
```

```python
import functools

import jax
import jax.numpy as jnp
import numpy as np
from jax import lax
from jax.experimental import pallas as pl
from jax.experimental.pallas import tpu as pltpu
from jax.sharding import PartitionSpec as P

CAM_DEV = 8
ITERS = 4
LANES = 128
SLOT = 16
SUB = 8
DIM = 6
COORDS = 2

damp_pose = 0.1
damp_camera = 0.5
MESH = pl.DeviceIdType.MESH
NT = (((1,), (1,)), ((), ()))

GRAD, SUMS, PER_SET = 6, 7, 9
FRONT, BACK = 0, PER_SET


def selection(view_count):
    block = view_count * DIM * COORDS
    res_rows = view_count * COORDS
    table = np.zeros((2, COORDS, 2, view_count, SLOT, 4 * block + 4 * res_rows), np.float32)
    for parity in range(2):
        for coord in range(COORDS):
            for side in range(2):
                for view in range(view_count):
                    for a in range(DIM):
                        column = side * 2 * block + (view * DIM + a) * COORDS + coord
                        table[parity, coord, side, view, a, column] = 1
                        table[parity, coord, side, view, SUB + a, column + block] = 1
                    column = 4 * block + side * 2 * res_rows + parity * res_rows + view * COORDS + coord
                    table[parity, coord, side, view, SUB + DIM, column] = 1
    return jnp.asarray(table.reshape(2, COORDS * 2 * view_count * SLOT, -1), jnp.bfloat16)


def row_of(value, index):
    return jnp.broadcast_to(value[index : index + 1, :], (SUB, value.shape[1]))


def halves(value):
    high = value.astype(jnp.bfloat16)
    low = (value - high.astype(jnp.float32)).astype(jnp.bfloat16)
    return jnp.concatenate([high, low], axis=0)


def invert(working):
    sub = lax.broadcasted_iota(jnp.int32, working[0].shape, 0)
    inverse = [jnp.where(sub == row, 1.0, 0.0) for row in range(DIM)]
    working = list(working)
    for column in range(DIM):
        pivot = 1.0 / row_of(working[column], column)
        row_work = working[column] * pivot
        row_inverse = inverse[column] * pivot
        for row in range(DIM):
            if row == column:
                continue
            factor = row_of(working[row], column)
            working[row] = working[row] - factor * row_work
            inverse[row] = inverse[row] - factor * row_inverse
        working[column] = row_work
        inverse[column] = row_inverse
    return inverse


def step_kernel(
    sizes,
    per_panel,
    frames,
    view_count,
    *refs,
):
    stored, (cam_out, pose_out), held = refs[:14], refs[14:16], refs[16:30]
    step_body(sizes, per_panel, frames, view_count, stored, held, cam_out, pose_out, *held, *refs[30:])


def step_body(
    sizes,
    per_panel,
    frames,
    view_count,
    stored_refs,
    held_refs,
    cam_out,
    pose_out,
    face_s,
    match_s,
    gain,
    fcor,
    bcor,
    fjc,
    fjp,
    bjc,
    bjp,
    fres,
    bres,
    fcam,
    bcam,
    pick,
    weights,
    left,
    right,
    grams0,
    grams1,
    own0,
    own1,
    own2,
    got0,
    got1,
    got2,
    turned,
    folded,
    upright,
    hot,
    tall_hot,
    send,
    recv,
    swap_send,
    swap_recv,
    send_sem,
    recv_sem,
    load_sem,
):
    panels, cams, cores = sizes
    group = cams * cores
    half = panels // 2
    peers = half * group
    width = panels * per_panel
    views = frames * view_count
    table_rows = gain.shape[0] // 2
    panel = lax.axis_index("panel")
    cam = lax.axis_index("cam")
    core = lax.axis_index("frame")
    other_panel = lax.rem(panel + half, panels)
    partner = (other_panel, cam, core)
    side = panel // half
    me = (lax.rem(panel, half) * cams + cam) * cores + core

    near = lax.rem(panel, half)

    def device_at(panel_step, cam_step, core_step):
        place = side * half + lax.rem(near + panel_step, half)
        return (place, lax.rem(cam + cam_step, cams), lax.rem(core + core_step, cores))

    def flipped(bits, cam_step, core_step):
        place = panel
        for bit in range(bits.bit_length()):
            if bits >> bit & 1:
                place = place + 2**bit - 2 * 2**bit * lax.rem(near // 2**bit, 2)
        return (place, lax.rem(cam + cam_step, cams), lax.rem(core + core_step, cores))

    def each_peer(action):
        if peers <= 16:
            places = [(p, c, k) for p in range(half) for c in range(cams) for k in range(cores)][1:]
            for place in sorted(places, key=lambda place: -(place[0].bit_count() + place[1])):
                action((device_at if half & (half - 1) else flipped)(*place))
        else:

            @pl.loop(1, peers)
            def _(offset):
                action(device_at(offset // group, (offset // cores) % cams, offset % cores))

    loads = [
        pltpu.make_async_copy(source, target, load_sem.at[index])
        for index, (source, target) in enumerate(zip(stored_refs, held_refs))
    ]
    for load in loads:
        load.start()

    barrier = pltpu.get_barrier_semaphore()
    pl.semaphore_signal(barrier, inc=1, device_id=partner, device_id_type=MESH)
    each_peer(lambda device: pl.semaphore_signal(barrier, inc=1, device_id=device, device_id_type=MESH))

    for load in loads[:5]:
        load.wait()

    sub = lax.broadcasted_iota(jnp.int32, (SUB, LANES), 0)
    lane = lax.broadcasted_iota(jnp.int32, (SUB, LANES), 1)

    def look_up(step, _):
        rows = pl.ds(pl.multiple_of(step * SUB, SUB), SUB)
        own_face = jnp.where(sub < view_count, face_s[2 * step], face_s[2 * step + 1]) == 0
        front, back = fcor[rows, :], bcor[rows, :]
        front_low, front_high = front & (LANES - 1), front // LANES
        back_low, back_high = back & (LANES - 1), back // LANES
        found = [jnp.zeros((SUB, LANES), jnp.float32)] * 3

        def table(entry, face):
            line = face * table_rows + entry
            return jnp.broadcast_to(gain[line : line + 1, :], (SUB, LANES))

        def pick_from(source, low):
            return jnp.take_along_axis(source, low, axis=1, mode="promise_in_bounds")

        for entry in range(table_rows):
            mixed = jnp.where(own_face, table(entry, 0), table(entry, 1))
            found[0] = jnp.where(front_high == entry, pick_from(mixed, front_low), found[0])
        for entry in range(table_rows):
            here = back_high == entry
            for face in range(2):
                found[1 + face] = jnp.where(here, pick_from(table(entry, face), back_low), found[1 + face])
        for place in range(3):
            weights[place, rows, :] = found[place]
        return 0

    for load in loads[5:]:
        load.wait()

    quarter = lane // frames
    count = LANES // frames
    inverse_match = jnp.zeros((SUB, LANES), jnp.int32)
    in_frames = lane % frames
    face_row = jnp.zeros((SUB, LANES), jnp.float32)
    for frame in range(frames):
        inverse_match = jnp.where(in_frames == match_s[frame], frame, inverse_match)
        face_row = jnp.where(in_frames == frame, face_s[frame].astype(jnp.float32), face_row)
    home = quarter * frames + inverse_match

    def to_home(value):
        return jnp.take_along_axis(value, home, axis=1, mode="promise_in_bounds")

    def code_row(ref):
        row = jnp.concatenate([ref[view : view + 1, :] for view in range(view_count)], axis=1)
        return jnp.broadcast_to(row, (SUB, LANES)).astype(jnp.float32)

    own0[...] = jnp.where(sub == 2, face_row, jnp.where(sub == 0, code_row(fcam), to_home(code_row(bcam))))

    def to_partner(source, target, index):
        return pltpu.make_async_remote_copy(
            src_ref=source,
            dst_ref=target,
            send_sem=swap_send.at[index],
            recv_sem=swap_recv.at[index],
            device_id=partner,
            device_id_type=MESH,
        )

    greeting = to_partner(own0, got0, 0)

    block_rows = view_count * DIM * COORDS
    span = 2 * view_count * SLOT
    slot_view = lax.broadcasted_iota(jnp.int32, (SLOT, LANES), 1) // SLOT

    def prepare(step, _):
        for parity in range(2):
            frame = 2 * step + parity
            rows = pl.ds(pl.multiple_of(frame * block_rows, SLOT), block_rows)
            res_rows = pl.ds(pl.multiple_of(step * SLOT, SLOT), SLOT)
            stored = jnp.concatenate(
                [fjc[rows, :], fjp[rows, :], bjc[rows, :], bjp[rows, :], fres[res_rows, :], bres[res_rows, :]], axis=0
            )
            plain = jnp.dot(pick[parity], stored, preferred_element_type=jnp.float32)
            for coord in range(COORDS):
                part = plain[coord * span : (coord + 1) * span]
                lanes = slice(coord * LANES, (coord + 1) * LANES)
                left[frame, :, lanes] = part.astype(jnp.bfloat16)
                scaled = []
                for place in range(3):
                    for view in range(view_count):
                        weight = weights[place, pl.ds(frame * view_count + view, 1), :]
                        start = ((view_count if place else 0) + view) * SLOT
                        scaled.append(part[start : start + SLOT] * jnp.broadcast_to(weight, (SLOT, LANES)))
                right[frame, :, lanes] = jnp.concatenate(scaled, axis=0).astype(jnp.bfloat16)
        return 0

    def gram(frame, _):
        product = lax.dot_general(left[frame], right[frame], NT, preferred_element_type=jnp.float32)
        both = product[:SLOT, :LANES]
        for view in range(1, 2 * view_count):
            both = jnp.where(slot_view == view, product[view * SLOT : (view + 1) * SLOT, :LANES], both)
        start = view_count * SLOT
        last = product[start : start + SLOT, LANES:]
        for view in range(1, view_count):
            rows_of = product[start + view * SLOT : start + (view + 1) * SLOT, LANES:]
            last = jnp.where(slot_view[:, : last.shape[1]] == view, rows_of, last)
        out_rows = pl.ds(pl.multiple_of(frame * SLOT, SLOT), SLOT)
        grams0[out_rows, :] = both
        grams1[out_rows, : last.shape[1]] = last
        return 0

    def weigh(step, _):
        look_up(step, _)
        return prepare(step, _)

    steps = frames // 2
    lax.fori_loop(0, steps // 4, weigh, 0, unroll=True)
    pl.semaphore_wait(barrier, peers)
    greeting.start()
    lax.fori_loop(steps // 4, steps, weigh, 0, unroll=True)
    lax.fori_loop(0, frames, gram, 0, unroll=True)
    def turn(scratch, rows):
        result = []
        for quad in range(SLOT // count):
            block = jnp.concatenate(
                [scratch[pl.ds(quad * count + i, frames, stride=SLOT), :] for i in range(count)], axis=0
            )
            result.append(block.T[:rows])
        return result

    def swap_quarters(r):
        low = quarter < 2
        even = quarter % 2 == 0
        u0 = jnp.where(low, r[0], pltpu.roll(r[2], 2 * frames, 1))
        u1 = jnp.where(low, r[1], pltpu.roll(r[3], 2 * frames, 1))
        u2 = jnp.where(low, pltpu.roll(r[0], 2 * frames, 1), r[2])
        u3 = jnp.where(low, pltpu.roll(r[1], 2 * frames, 1), r[3])
        back = LANES - frames
        return [
            jnp.where(even, u0, pltpu.roll(u1, frames, 1)),
            jnp.where(even, pltpu.roll(u0, back, 1), u1),
            jnp.where(even, u2, pltpu.roll(u3, frames, 1)),
            jnp.where(even, pltpu.roll(u2, back, 1), u3),
        ]

    def lay_out(turned_grams, first_view, order):
        columns, sums = [], []
        for quad, tall in enumerate(turned_grams):
            starts = [(first_view + view) * SLOT for view in range(view_count)]
            columns += swap_quarters([tall[start : start + SUB] for start in starts])
            if quad >= 2:
                total = tall[starts[0] + SUB : starts[0] + SLOT]
                for start in starts[1:]:
                    total = total + tall[start + SUB : start + SLOT]
                sums.append(total)
        return [order(value) for value in columns[:DIM]], [order(value) for value in columns[SUB : SUB + GRAD + 1] + sums]

    def hot_columns(place, codes, row, base):
        camera = codes[row : row + 1, :].astype(jnp.int32) + base * per_panel
        camera = jnp.where(camera >= width, camera - width, camera)
        chosen = jnp.broadcast_to(camera, (width, LANES)) == lax.broadcasted_iota(jnp.int32, (width, LANES), 0)
        hot[:, place * LANES : (place + 1) * LANES] = jnp.where(chosen, 1.0, 0.0).astype(jnp.bfloat16)

    def lanes_of(place, places=1):
        return slice(place * LANES, (place + places) * LANES)

    def keep(place, ref, first):
        for b in range(DIM):
            turned[place, b * SUB : (b + 1) * SUB, :] = ref[first + b]

    tall0 = turn(grams0, LANES)
    tall1 = turn(grams1, view_count * SLOT)
    front_cam, front_rest = lay_out(tall0, 0, lambda value: value)
    for index, value in enumerate(front_rest):
        own1[FRONT + index] = value

    def part(first, entries, index):
        places = (pl.ds(first, entries), pl.ds(0, DIM))
        return to_partner(own1.at[places], got1.at[places], index)

    swap_front = part(FRONT, PER_SET, 1)
    swap_front.start()
    back0_cam, back0_rest = lay_out(tall0, view_count, to_home)
    back1_cam, back1_rest = lay_out(tall1, 0, to_home)
    for place in range(4):
        turned[place, DIM * SUB :, :] = jnp.zeros((2 * SUB, LANES), jnp.float32)
    keep(1, own1, FRONT)
    own_codes = own0[...]
    hot_columns(1, own_codes, 0, panel)
    hot_columns(2, own_codes, 1, panel)

    greeting.wait_recv()
    far_codes = got0[...]
    first_face = row_of(far_codes, 2) < 0.5
    chosen_rest = [jnp.where(first_face, one, zero) for zero, one in zip(back0_rest, back1_rest)]
    for index in range(SUMS, PER_SET):
        own1[BACK + index] = chosen_rest[index]
    swap_sums = part(BACK + SUMS, PER_SET - SUMS, 4)
    swap_sums.start()
    for index in range(SUMS):
        own1[BACK + index] = chosen_rest[index]
    swap_back = part(BACK, SUMS, 2)
    swap_back.start()

    stacked = jnp.concatenate(
        [
            jnp.concatenate([front, jnp.where(first_face, one, zero)], axis=1)
            for front, zero, one in zip(front_cam, back0_cam, back1_cam)
        ],
        axis=0,
    )
    summed = lax.dot_general(halves(stacked), hot[:, lanes_of(1, 2)], NT, preferred_element_type=jnp.float32)
    for b in range(DIM):
        rows = slice(b * SUB, (b + 1) * SUB)
        own2[b] = summed[rows] + summed[DIM * SUB + b * SUB : DIM * SUB + (b + 1) * SUB]
    swap_cam = to_partner(own2.at[:, pl.ds(0, DIM)], got2.at[:, pl.ds(0, DIM)], 3)
    keep(2, own1, BACK)
    hot_columns(0, far_codes, 1, other_panel)
    hot_columns(3, far_codes, 0, other_panel)
    for place in range(4):
        tall_hot[lanes_of(place), :] = hot[:, lanes_of(place)].astype(jnp.float32).T.astype(jnp.bfloat16)
    swap_front.wait_recv()
    keep(3, got1, FRONT)
    swap_sums.wait_recv()

    def spread(value, place):
        only = jnp.where(quarter == place, value, 0.0)
        only = only + pltpu.roll(only, 2 * frames, 1)
        return only + pltpu.roll(only, frames, 1)

    inverses, pose_grads = [], []
    for back, front in ((got1, own1), (own1, got1)):
        total = [jnp.where(sub < DIM, back[BACK + SUMS + i] + front[FRONT + SUMS + i], 0.0) for i in range(2)]
        columns = [spread(total[b // count], b % count) for b in range(DIM + 1)]
        pose_grads.append(columns[DIM])
        inverses.append(invert([columns[b] + jnp.where(sub == b, damp_pose, 0.0) for b in range(DIM)]))

    def solve_pose(which, value):
        result = inverses[which][0] * row_of(value, 0)
        for b in range(1, DIM):
            result = result + inverses[which][b] * row_of(value, b)
        return result

    def couple(which, seen):
        total = None
        for place in (2 * which, 2 * which + 1):
            for a in range(DIM):
                term = upright[place, a] * row_of(seen[:, lanes_of(place)], a)
                total = term if total is None else total + term
        total = total + pltpu.roll(total, 2 * frames, 1)
        return total + pltpu.roll(total, frames, 1)

    def minus_spread(place, value, solved):
        for b in range(DIM):
            value = value - turned[place, b * SUB : (b + 1) * SUB, :] * row_of(solved, b)
        return value

    def fold(place):
        for b in range(DIM):
            column = inverses[place // 2][b]
            total = turned[place, :SUB, :] * row_of(column, 0)
            for row in range(1, DIM):
                total = total + turned[place, row * SUB : (row + 1) * SUB, :] * row_of(column, row)
            folded[place, b] = total
            upright[place, b] = turned[place, pl.ds(b, SUB, stride=SUB), :]

    def look(vector, places):
        both = jnp.dot(halves(vector), hot[:, lanes_of(0, places)], preferred_element_type=jnp.float32)
        return both[:SUB] + both[SUB:]

    def scatter(pieces, first=0):
        rows = lanes_of(first, len(pieces))
        both = jnp.dot(halves(jnp.concatenate(pieces, axis=1)), tall_hot[rows, :], preferred_element_type=jnp.float32)
        return both[:SUB] + both[SUB:]

    def exchange(round_id, value):
        send[round_id] = value
        each_peer(
            lambda device: pltpu.make_async_remote_copy(
                src_ref=send.at[round_id, pl.ds(0, DIM)],
                dst_ref=recv.at[round_id, me, pl.ds(0, DIM)],
                send_sem=send_sem.at[round_id],
                recv_sem=recv_sem.at[round_id],
                device_id=device,
                device_id_type=MESH,
            ).start()
        )
        recv[round_id, pl.ds(me, 1)] = value[None]
        others = recv.at[round_id, pl.ds(0, peers - 1), pl.ds(0, DIM)]

        def finish():
            pltpu.make_async_copy(others, others, recv_sem.at[round_id]).wait()
            parts = [recv[round_id, source] for source in range(peers)]
            while len(parts) > 1:
                tail = [parts[-1]] if len(parts) % 2 else []
                parts = [a + b for a, b in zip(parts[::2], parts[1::2])] + tail
            return jnp.where(lax.broadcasted_iota(jnp.int32, (SUB, width), 0) < DIM, parts[0], 0.0)

        return finish

    def drain(round_id):
        others = recv.at[round_id, pl.ds(0, peers - 1), pl.ds(0, DIM)]
        pltpu.make_async_copy(others, others, send_sem.at[round_id]).wait()

    solved = [solve_pose(which, pose_grads[which]) for which in range(2)]
    here = ((own1, FRONT), (own1, BACK), (got1, FRONT))
    known = scatter(
        [minus_spread(i + 1, ref[first + GRAD], solved[(i + 1) // 2]) for i, (ref, first) in enumerate(here)], 1
    )
    swap_back.wait_recv()
    keep(0, got1, BACK)
    right_side = exchange(0, known + scatter([minus_spread(0, got1[BACK + GRAD], solved[0])]))

    swap_cam.start()
    for place in range(4):
        fold(place)
    swap_cam.wait_recv()
    blocks = [own2[b] + got2[b] for b in range(DIM)]

    def apply(vector):
        seen = look(vector, 4)
        pieces = []
        for which in range(2):
            coupled = couple(which, seen)
            for place in (2 * which, 2 * which + 1):
                value = folded[place, 0] * row_of(coupled, 0)
                for b in range(1, DIM):
                    value = value + folded[place, b] * row_of(coupled, b)
                pieces.append(value)
        local_part = blocks[0] * row_of(vector, 0)
        for b in range(1, DIM):
            local_part = local_part + blocks[b] * row_of(vector, b)
        return local_part - scatter(pieces)

    def dot(left, right):
        return jnp.sum(jnp.sum(left * right, axis=1, keepdims=True), axis=0, keepdims=True)

    def pose_of(vector):
        return solve_pose(0, couple(0, look(vector, 2)))

    residual = -right_side()
    direction = residual
    update = jnp.zeros_like(residual)
    share = applied = apply(residual)
    norm_now = dot(residual, residual)
    for iteration in range(ITERS):
        finish = exchange(iteration + 1, share)
        if iteration + 1 == ITERS:
            pose_before = -solve_pose(0, pose_grads[0]) - pose_of(update)
            pose_along = pose_of(direction)
        image = damp_camera * direction + finish()
        if iteration + 1 < ITERS:
            applied_image = apply(image)
        size = norm_now / dot(direction, image)
        update = update + size * direction
        if iteration + 1 < ITERS:
            residual = residual - size * image
            applied = applied - size * applied_image
            norm_next = dot(residual, residual)
            ratio = norm_next / norm_now
            direction = residual + ratio * direction
            share = applied + ratio * share
            norm_now = norm_next

    cam_out[...] = pltpu.roll(update, lax.rem(panels - panel, panels) * per_panel, 1)[:DIM, :per_panel]
    pose_out[...] = (pose_before - size * pose_along)[:DIM, :frames]
    for copy in (greeting, swap_front, swap_sums, swap_back, swap_cam):
        copy.wait_send()
    for round_id in range(ITERS + 1):
        drain(round_id)


def local(
    sizes,
    front_jc,
    front_jp,
    front_res,
    front_corners,
    front_cams,
    back_jc,
    back_jp,
    back_res,
    back_corners,
    back_cams,
    back_match,
    face,
    corner_gain,
):
    frames = face.shape[0]
    view_count = front_cams.shape[1]
    views = frames * view_count
    per_panel = CAM_DEV * sizes[1]
    width = sizes[0] * per_panel
    peers = sizes[0] // 2 * sizes[1] * sizes[2]

    def as_stored(jacobian):
        return jacobian.transpose(0, 1, 3, 2, 4).reshape(-1, LANES)

    arguments = (
        face,
        back_match,
        corner_gain.reshape(-1, LANES),
        front_corners.reshape(-1, LANES),
        back_corners.reshape(-1, LANES),
        as_stored(front_jc),
        as_stored(front_jp),
        as_stored(back_jc),
        as_stored(back_jp),
        front_res.reshape(-1, LANES),
        back_res.reshape(-1, LANES),
        front_cams.T,
        back_cams.T,
        selection(view_count),
    )
    spaces = [pltpu.SMEM] * 2 + [pltpu.VMEM] * 12
    vmem = pl.BlockSpec(memory_space=pltpu.VMEM)
    return pl.pallas_call(
        functools.partial(step_kernel, sizes, per_panel, frames, view_count),
        in_specs=[pl.BlockSpec(memory_space=pltpu.HBM)] * len(arguments),
        out_specs=(vmem, vmem),
        out_shape=(
            pltpu.VMEM((DIM, per_panel), jnp.float32),
            pltpu.VMEM((DIM, frames), jnp.float32),
        ),
        scratch_shapes=[space(value.shape, value.dtype) for space, value in zip(spaces, arguments)]
        + [
            pltpu.VMEM((3, views, LANES), jnp.float32),
            pltpu.VMEM((frames, 2 * view_count * SLOT, COORDS * LANES), jnp.bfloat16),
            pltpu.VMEM((frames, 3 * view_count * SLOT, COORDS * LANES), jnp.bfloat16),
            pltpu.VMEM((frames * SLOT, LANES), jnp.float32),
            pltpu.VMEM((frames * SLOT, LANES), jnp.float32),
            pltpu.VMEM((SUB, LANES), jnp.float32),
            pltpu.VMEM((2 * PER_SET, SUB, LANES), jnp.float32),
            pltpu.VMEM((DIM, SUB, width), jnp.float32),
            pltpu.VMEM((SUB, LANES), jnp.float32),
            pltpu.VMEM((2 * PER_SET, SUB, LANES), jnp.float32),
            pltpu.VMEM((DIM, SUB, width), jnp.float32),
            pltpu.VMEM((4, SUB * SUB, LANES), jnp.float32),
            pltpu.VMEM((4, DIM, SUB, LANES), jnp.float32),
            pltpu.VMEM((4, DIM, SUB, LANES), jnp.float32),
            pltpu.VMEM((width, 4 * LANES), jnp.bfloat16),
            pltpu.VMEM((4 * LANES, width), jnp.bfloat16),
            pltpu.VMEM((ITERS + 1, SUB, width), jnp.float32),
            pltpu.VMEM((ITERS + 1, peers, SUB, width), jnp.float32),
            pltpu.SemaphoreType.DMA((5,)),
            pltpu.SemaphoreType.DMA((5,)),
            pltpu.SemaphoreType.DMA((ITERS + 1,)),
            pltpu.SemaphoreType.DMA((ITERS + 1,)),
            pltpu.SemaphoreType.DMA((len(arguments),)),
        ],
        compiler_params=pltpu.CompilerParams(
            collective_id=0, has_side_effects=True, vmem_limit_bytes=60 * 1024 * 1024
        ),
        name="step",
    )(*arguments)


def solution(mesh):
    wide = ("panel", "cam", "frame")
    sizes = tuple(mesh.shape[name] for name in wide)
    in_specs = (
        P(wide, None, None, None, None),
        P(wide, None, None, None, None),
        P(wide, None, None, None),
        P(wide, None, None),
        P(wide, None),
        P(wide, None, None, None, None),
        P(wide, None, None, None, None),
        P(wide, None, None, None),
        P(wide, None, None),
        P(wide, None),
        P(wide),
        P(wide),
        P(),
    )
    out_specs = (P(None, "panel"), P(None, wide))
    return jax.shard_map(
        functools.partial(local, sizes), mesh=mesh, in_specs=in_specs, out_specs=out_specs, check_vma=False
    )
```

```python
import functools

import jax
import jax.numpy as jnp
import numpy as np
from jax import lax
from jax.experimental import pallas as pl
from jax.experimental.pallas import tpu as pltpu
from jax.sharding import PartitionSpec as P

CAM_DEV = 8
ITERS = 4
LANES = 128
SLOT = 16
SUB = 8
DIM = 6
COORDS = 2

damp_pose = 0.1
damp_camera = 0.5
MESH = pl.DeviceIdType.MESH
NT = (((1,), (1,)), ((), ()))

GRAD, SUMS, PER_SET = 6, 7, 9
FRONT, BACK = 0, PER_SET


def selection(view_count):
    block = view_count * DIM * COORDS
    res_rows = view_count * COORDS
    table = np.zeros((2, COORDS, 2, view_count, SLOT, 4 * block + 4 * res_rows), np.float32)
    for parity in range(2):
        for coord in range(COORDS):
            for side in range(2):
                for view in range(view_count):
                    for a in range(DIM):
                        column = side * 2 * block + (view * DIM + a) * COORDS + coord
                        table[parity, coord, side, view, a, column] = 1
                        table[parity, coord, side, view, SUB + a, column + block] = 1
                    column = 4 * block + side * 2 * res_rows + parity * res_rows + view * COORDS + coord
                    table[parity, coord, side, view, SUB + DIM, column] = 1
    return jnp.asarray(table.reshape(2, COORDS * 2 * view_count * SLOT, -1), jnp.bfloat16)


def row_of(value, index):
    return jnp.broadcast_to(value[index : index + 1, :], (SUB, value.shape[1]))


def halves(value):
    high = value.astype(jnp.bfloat16)
    low = (value - high.astype(jnp.float32)).astype(jnp.bfloat16)
    return jnp.concatenate([high, low], axis=0)


def invert(working):
    sub = lax.broadcasted_iota(jnp.int32, working[0].shape, 0)
    inverse = [jnp.where(sub == row, 1.0, 0.0) for row in range(DIM)]
    working = list(working)
    for column in range(DIM):
        pivot = 1.0 / row_of(working[column], column)
        row_work = working[column] * pivot
        row_inverse = inverse[column] * pivot
        for row in range(DIM):
            if row == column:
                continue
            factor = row_of(working[row], column)
            working[row] = working[row] - factor * row_work
            inverse[row] = inverse[row] - factor * row_inverse
        working[column] = row_work
        inverse[column] = row_inverse
    return inverse


def step_kernel(
    sizes,
    per_panel,
    frames,
    view_count,
    *refs,
):
    stored, (cam_out, pose_out), held = refs[:14], refs[14:16], refs[16:30]
    step_body(sizes, per_panel, frames, view_count, stored, held, cam_out, pose_out, *held, *refs[30:])


def step_body(
    sizes,
    per_panel,
    frames,
    view_count,
    stored_refs,
    held_refs,
    cam_out,
    pose_out,
    face_s,
    match_s,
    gain,
    fcor,
    bcor,
    fjc,
    fjp,
    bjc,
    bjp,
    fres,
    bres,
    fcam,
    bcam,
    pick,
    weights,
    left,
    right,
    grams0,
    grams1,
    own0,
    own1,
    own2,
    got0,
    got1,
    got2,
    turned,
    folded,
    upright,
    hot,
    tall_hot,
    send,
    recv,
    swap_send,
    swap_recv,
    send_sem,
    recv_sem,
    load_sem,
):
    panels, cams, cores = sizes
    group = cams * cores
    half = panels // 2
    peers = half * group
    width = panels * per_panel
    views = frames * view_count
    table_rows = gain.shape[0] // 2
    panel = lax.axis_index("panel")
    cam = lax.axis_index("cam")
    core = lax.axis_index("frame")
    other_panel = lax.rem(panel + half, panels)
    partner = (other_panel, cam, core)
    side = panel // half
    me = (lax.rem(panel, half) * cams + cam) * cores + core

    near = lax.rem(panel, half)

    def device_at(panel_step, cam_step, core_step):
        place = side * half + lax.rem(near + panel_step, half)
        return (place, lax.rem(cam + cam_step, cams), lax.rem(core + core_step, cores))

    def flipped(bits, cam_step, core_step):
        place = panel
        for bit in range(bits.bit_length()):
            if bits >> bit & 1:
                place = place + 2**bit - 2 * 2**bit * lax.rem(near // 2**bit, 2)
        return (place, lax.rem(cam + cam_step, cams), lax.rem(core + core_step, cores))

    def each_peer(action):
        if peers <= 16:
            places = [(p, c, k) for p in range(half) for c in range(cams) for k in range(cores)][1:]
            for place in sorted(places, key=lambda place: -(place[0].bit_count() + place[1])):
                action((device_at if half & (half - 1) else flipped)(*place))
        else:

            @pl.loop(1, peers)
            def _(offset):
                action(device_at(offset // group, (offset // cores) % cams, offset % cores))

    loads = [
        pltpu.make_async_copy(source, target, load_sem.at[index])
        for index, (source, target) in enumerate(zip(stored_refs, held_refs))
    ]
    for load in loads:
        load.start()

    barrier = pltpu.get_barrier_semaphore()
    pl.semaphore_signal(barrier, inc=1, device_id=partner, device_id_type=MESH)
    each_peer(lambda device: pl.semaphore_signal(barrier, inc=1, device_id=device, device_id_type=MESH))

    for load in loads[:5]:
        load.wait()

    sub = lax.broadcasted_iota(jnp.int32, (SUB, LANES), 0)
    lane = lax.broadcasted_iota(jnp.int32, (SUB, LANES), 1)

    def look_up(step, _):
        rows = pl.ds(pl.multiple_of(step * SUB, SUB), SUB)
        own_face = jnp.where(sub < view_count, face_s[2 * step], face_s[2 * step + 1]) == 0
        front, back = fcor[rows, :], bcor[rows, :]
        front_low, front_high = front & (LANES - 1), front // LANES
        back_low, back_high = back & (LANES - 1), back // LANES
        found = [jnp.zeros((SUB, LANES), jnp.float32)] * 3

        def table(entry, face):
            line = face * table_rows + entry
            return jnp.broadcast_to(gain[line : line + 1, :], (SUB, LANES))

        def pick_from(source, low):
            return jnp.take_along_axis(source, low, axis=1, mode="promise_in_bounds")

        for entry in range(table_rows):
            mixed = jnp.where(own_face, table(entry, 0), table(entry, 1))
            found[0] = jnp.where(front_high == entry, pick_from(mixed, front_low), found[0])
        for entry in range(table_rows):
            here = back_high == entry
            for face in range(2):
                found[1 + face] = jnp.where(here, pick_from(table(entry, face), back_low), found[1 + face])
        for place in range(3):
            weights[place, rows, :] = found[place]
        return 0

    for load in loads[5:]:
        load.wait()

    quarter = lane // frames
    count = LANES // frames
    inverse_match = jnp.zeros((SUB, LANES), jnp.int32)
    in_frames = lane % frames
    face_row = jnp.zeros((SUB, LANES), jnp.float32)
    for frame in range(frames):
        inverse_match = jnp.where(in_frames == match_s[frame], frame, inverse_match)
        face_row = jnp.where(in_frames == frame, face_s[frame].astype(jnp.float32), face_row)
    home = quarter * frames + inverse_match

    def to_home(value):
        return jnp.take_along_axis(value, home, axis=1, mode="promise_in_bounds")

    def code_row(ref):
        row = jnp.concatenate([ref[view : view + 1, :] for view in range(view_count)], axis=1)
        return jnp.broadcast_to(row, (SUB, LANES)).astype(jnp.float32)

    own0[...] = jnp.where(sub == 2, face_row, jnp.where(sub == 0, code_row(fcam), to_home(code_row(bcam))))

    def to_partner(source, target, index):
        return pltpu.make_async_remote_copy(
            src_ref=source,
            dst_ref=target,
            send_sem=swap_send.at[index],
            recv_sem=swap_recv.at[index],
            device_id=partner,
            device_id_type=MESH,
        )

    greeting = to_partner(own0, got0, 0)

    block_rows = view_count * DIM * COORDS
    span = 2 * view_count * SLOT
    slot_view = lax.broadcasted_iota(jnp.int32, (SLOT, LANES), 1) // SLOT

    def prepare(step, _):
        for parity in range(2):
            frame = 2 * step + parity
            rows = pl.ds(pl.multiple_of(frame * block_rows, SLOT), block_rows)
            res_rows = pl.ds(pl.multiple_of(step * SLOT, SLOT), SLOT)
            stored = jnp.concatenate(
                [fjc[rows, :], fjp[rows, :], bjc[rows, :], bjp[rows, :], fres[res_rows, :], bres[res_rows, :]], axis=0
            )
            plain = jnp.dot(pick[parity], stored, preferred_element_type=jnp.float32)
            for coord in range(COORDS):
                part = plain[coord * span : (coord + 1) * span]
                lanes = slice(coord * LANES, (coord + 1) * LANES)
                left[frame, :, lanes] = part.astype(jnp.bfloat16)
                scaled = []
                for place in range(3):
                    for view in range(view_count):
                        weight = weights[place, pl.ds(frame * view_count + view, 1), :]
                        start = ((view_count if place else 0) + view) * SLOT
                        scaled.append(part[start : start + SLOT] * jnp.broadcast_to(weight, (SLOT, LANES)))
                right[frame, :, lanes] = jnp.concatenate(scaled, axis=0).astype(jnp.bfloat16)
        return 0

    def gram(frame, _):
        product = lax.dot_general(left[frame], right[frame], NT, preferred_element_type=jnp.float32)
        both = product[:SLOT, :LANES]
        for view in range(1, 2 * view_count):
            both = jnp.where(slot_view == view, product[view * SLOT : (view + 1) * SLOT, :LANES], both)
        start = view_count * SLOT
        last = product[start : start + SLOT, LANES:]
        for view in range(1, view_count):
            rows_of = product[start + view * SLOT : start + (view + 1) * SLOT, LANES:]
            last = jnp.where(slot_view[:, : last.shape[1]] == view, rows_of, last)
        out_rows = pl.ds(pl.multiple_of(frame * SLOT, SLOT), SLOT)
        grams0[out_rows, :] = both
        grams1[out_rows, : last.shape[1]] = last
        return 0

    def weigh(step, _):
        look_up(step, _)
        return prepare(step, _)

    steps = frames // 2
    lax.fori_loop(0, steps // 4, weigh, 0, unroll=True)
    pl.semaphore_wait(barrier, peers)
    greeting.start()
    lax.fori_loop(steps // 4, steps, weigh, 0, unroll=True)
    lax.fori_loop(0, frames, gram, 0, unroll=True)
    def turn(scratch, rows):
        result = []
        for quad in range(SLOT // count):
            block = jnp.concatenate(
                [scratch[pl.ds(quad * count + i, frames, stride=SLOT), :] for i in range(count)], axis=0
            )
            result.append(block.T[:rows])
        return result

    def swap_quarters(r):
        low = quarter < 2
        even = quarter % 2 == 0
        u0 = jnp.where(low, r[0], pltpu.roll(r[2], 2 * frames, 1))
        u1 = jnp.where(low, r[1], pltpu.roll(r[3], 2 * frames, 1))
        u2 = jnp.where(low, pltpu.roll(r[0], 2 * frames, 1), r[2])
        u3 = jnp.where(low, pltpu.roll(r[1], 2 * frames, 1), r[3])
        back = LANES - frames
        return [
            jnp.where(even, u0, pltpu.roll(u1, frames, 1)),
            jnp.where(even, pltpu.roll(u0, back, 1), u1),
            jnp.where(even, u2, pltpu.roll(u3, frames, 1)),
            jnp.where(even, pltpu.roll(u2, back, 1), u3),
        ]

    def lay_out(turned_grams, first_view, order):
        columns, sums = [], []
        for quad, tall in enumerate(turned_grams):
            starts = [(first_view + view) * SLOT for view in range(view_count)]
            columns += swap_quarters([tall[start : start + SUB] for start in starts])
            if quad >= 2:
                total = tall[starts[0] + SUB : starts[0] + SLOT]
                for start in starts[1:]:
                    total = total + tall[start + SUB : start + SLOT]
                sums.append(total)
        return [order(value) for value in columns[:DIM]], [order(value) for value in columns[SUB : SUB + GRAD + 1] + sums]

    def hot_columns(place, codes, row, base):
        camera = codes[row : row + 1, :].astype(jnp.int32) + base * per_panel
        camera = jnp.where(camera >= width, camera - width, camera)
        chosen = jnp.broadcast_to(camera, (width, LANES)) == lax.broadcasted_iota(jnp.int32, (width, LANES), 0)
        hot[:, place * LANES : (place + 1) * LANES] = jnp.where(chosen, 1.0, 0.0).astype(jnp.bfloat16)

    def lanes_of(place, places=1):
        return slice(place * LANES, (place + places) * LANES)

    def keep(place, ref, first):
        for b in range(DIM):
            turned[place, b * SUB : (b + 1) * SUB, :] = ref[first + b]

    tall0 = turn(grams0, LANES)
    tall1 = turn(grams1, view_count * SLOT)
    front_cam, front_rest = lay_out(tall0, 0, lambda value: value)
    for index, value in enumerate(front_rest):
        own1[FRONT + index] = value

    def part(first, entries, index):
        places = (pl.ds(first, entries), pl.ds(0, DIM))
        return to_partner(own1.at[places], got1.at[places], index)

    swap_front = part(FRONT, PER_SET, 1)
    swap_front.start()
    back0_cam, back0_rest = lay_out(tall0, view_count, to_home)
    back1_cam, back1_rest = lay_out(tall1, 0, to_home)
    for place in range(4):
        turned[place, DIM * SUB :, :] = jnp.zeros((2 * SUB, LANES), jnp.float32)
    keep(1, own1, FRONT)
    own_codes = own0[...]
    hot_columns(1, own_codes, 0, panel)
    hot_columns(2, own_codes, 1, panel)

    greeting.wait_recv()
    far_codes = got0[...]
    first_face = row_of(far_codes, 2) < 0.5
    chosen_rest = [jnp.where(first_face, one, zero) for zero, one in zip(back0_rest, back1_rest)]
    for index in range(SUMS, PER_SET):
        own1[BACK + index] = chosen_rest[index]
    swap_sums = part(BACK + SUMS, PER_SET - SUMS, 4)
    swap_sums.start()
    for index in range(SUMS):
        own1[BACK + index] = chosen_rest[index]
    swap_back = part(BACK, SUMS, 2)
    swap_back.start()

    stacked = jnp.concatenate(
        [
            jnp.concatenate([front, jnp.where(first_face, one, zero)], axis=1)
            for front, zero, one in zip(front_cam, back0_cam, back1_cam)
        ],
        axis=0,
    )
    summed = lax.dot_general(halves(stacked), hot[:, lanes_of(1, 2)], NT, preferred_element_type=jnp.float32)
    for b in range(DIM):
        rows = slice(b * SUB, (b + 1) * SUB)
        own2[b] = summed[rows] + summed[DIM * SUB + b * SUB : DIM * SUB + (b + 1) * SUB]
    swap_cam = to_partner(own2.at[:, pl.ds(0, DIM)], got2.at[:, pl.ds(0, DIM)], 3)
    keep(2, own1, BACK)
    hot_columns(0, far_codes, 1, other_panel)
    hot_columns(3, far_codes, 0, other_panel)
    for place in range(4):
        tall_hot[lanes_of(place), :] = hot[:, lanes_of(place)].astype(jnp.float32).T.astype(jnp.bfloat16)
    swap_front.wait_recv()
    keep(3, got1, FRONT)
    swap_sums.wait_recv()

    def over_quarters(value):
        first, second, third = (pltpu.roll(value, i * frames, 1) for i in range(1, count))
        return (value + first) + (second + third)

    def spread(value, place):
        return over_quarters(jnp.where(quarter == place, value, 0.0))

    inverses, pose_grads = [], []
    for back, front in ((got1, own1), (own1, got1)):
        total = [jnp.where(sub < DIM, back[BACK + SUMS + i] + front[FRONT + SUMS + i], 0.0) for i in range(2)]
        columns = [spread(total[b // count], b % count) for b in range(DIM + 1)]
        pose_grads.append(columns[DIM])
        inverses.append(invert([columns[b] + jnp.where(sub == b, damp_pose, 0.0) for b in range(DIM)]))

    def solve_pose(which, value):
        result = inverses[which][0] * row_of(value, 0)
        for b in range(1, DIM):
            result = result + inverses[which][b] * row_of(value, b)
        return result

    def couple(which, seen):
        total = None
        for place in (2 * which, 2 * which + 1):
            for a in range(DIM):
                term = upright[place, a] * row_of(seen[:, lanes_of(place)], a)
                total = term if total is None else total + term
        return over_quarters(total)

    def minus_spread(place, value, solved):
        for b in range(DIM):
            value = value - turned[place, b * SUB : (b + 1) * SUB, :] * row_of(solved, b)
        return value

    def fold(place):
        for b in range(DIM):
            column = inverses[place // 2][b]
            total = turned[place, :SUB, :] * row_of(column, 0)
            for row in range(1, DIM):
                total = total + turned[place, row * SUB : (row + 1) * SUB, :] * row_of(column, row)
            folded[place, b] = total
            upright[place, b] = turned[place, pl.ds(b, SUB, stride=SUB), :]

    def look(vector, places):
        both = jnp.dot(halves(vector), hot[:, lanes_of(0, places)], preferred_element_type=jnp.float32)
        return both[:SUB] + both[SUB:]

    def scatter(pieces, first=0):
        rows = lanes_of(first, len(pieces))
        both = jnp.dot(halves(jnp.concatenate(pieces, axis=1)), tall_hot[rows, :], preferred_element_type=jnp.float32)
        return both[:SUB] + both[SUB:]

    def exchange(round_id, value):
        send[round_id] = value
        each_peer(
            lambda device: pltpu.make_async_remote_copy(
                src_ref=send.at[round_id, pl.ds(0, DIM)],
                dst_ref=recv.at[round_id, me, pl.ds(0, DIM)],
                send_sem=send_sem.at[round_id],
                recv_sem=recv_sem.at[round_id],
                device_id=device,
                device_id_type=MESH,
            ).start()
        )
        recv[round_id, pl.ds(me, 1)] = value[None]
        others = recv.at[round_id, pl.ds(0, peers - 1), pl.ds(0, DIM)]

        def finish():
            pltpu.make_async_copy(others, others, recv_sem.at[round_id]).wait()
            parts = [recv[round_id, source] for source in range(peers)]
            while len(parts) > 1:
                tail = [parts[-1]] if len(parts) % 2 else []
                parts = [a + b for a, b in zip(parts[::2], parts[1::2])] + tail
            return jnp.where(lax.broadcasted_iota(jnp.int32, (SUB, width), 0) < DIM, parts[0], 0.0)

        return finish

    def drain(round_id):
        others = recv.at[round_id, pl.ds(0, peers - 1), pl.ds(0, DIM)]
        pltpu.make_async_copy(others, others, send_sem.at[round_id]).wait()

    solved = [solve_pose(which, pose_grads[which]) for which in range(2)]
    here = ((own1, FRONT), (own1, BACK), (got1, FRONT))
    known = scatter(
        [minus_spread(i + 1, ref[first + GRAD], solved[(i + 1) // 2]) for i, (ref, first) in enumerate(here)], 1
    )
    swap_back.wait_recv()
    keep(0, got1, BACK)
    right_side = exchange(0, known + scatter([minus_spread(0, got1[BACK + GRAD], solved[0])]))

    swap_cam.start()
    for place in range(4):
        fold(place)
    swap_cam.wait_recv()
    blocks = [own2[b] + got2[b] for b in range(DIM)]

    def apply(vector):
        seen = look(vector, 4)
        pieces = []
        for which in range(2):
            coupled = couple(which, seen)
            for place in (2 * which, 2 * which + 1):
                value = folded[place, 0] * row_of(coupled, 0)
                for b in range(1, DIM):
                    value = value + folded[place, b] * row_of(coupled, b)
                pieces.append(value)
        local_part = blocks[0] * row_of(vector, 0)
        for b in range(1, DIM):
            local_part = local_part + blocks[b] * row_of(vector, b)
        return local_part - scatter(pieces)

    def dot(left, right):
        return jnp.sum(jnp.sum(left * right, axis=1, keepdims=True), axis=0, keepdims=True)

    def pose_of(vector):
        return solve_pose(0, couple(0, look(vector, 2)))

    residual = -right_side()
    direction = residual
    update = jnp.zeros_like(residual)
    share = applied = apply(residual)
    norm_now = dot(residual, residual)
    for iteration in range(ITERS):
        finish = exchange(iteration + 1, share)
        if iteration + 1 == ITERS:
            pose_before = -solve_pose(0, pose_grads[0]) - pose_of(update)
            pose_along = pose_of(direction)
            turn_by = lax.rem(panels - panel, panels) * per_panel
            cam_before = pltpu.roll(update, turn_by, 1)
            cam_along = pltpu.roll(direction, turn_by, 1)
        image = damp_camera * direction + finish()
        if iteration + 1 < ITERS:
            applied_image = apply(image)
        size = norm_now / dot(direction, image)
        if iteration + 1 < ITERS:
            update = update + size * direction
            residual = residual - size * image
            applied = applied - size * applied_image
            norm_next = dot(residual, residual)
            ratio = norm_next / norm_now
            direction = residual + ratio * direction
            share = applied + ratio * share
            norm_now = norm_next

    cam_out[...] = (cam_before + size * cam_along)[:DIM, :per_panel]
    pose_out[...] = (pose_before - size * pose_along)[:DIM, :frames]
    for copy in (greeting, swap_front, swap_sums, swap_back, swap_cam):
        copy.wait_send()
    for round_id in range(ITERS + 1):
        drain(round_id)


def local(
    sizes,
    front_jc,
    front_jp,
    front_res,
    front_corners,
    front_cams,
    back_jc,
    back_jp,
    back_res,
    back_corners,
    back_cams,
    back_match,
    face,
    corner_gain,
):
    frames = face.shape[0]
    view_count = front_cams.shape[1]
    views = frames * view_count
    per_panel = CAM_DEV * sizes[1]
    width = sizes[0] * per_panel
    peers = sizes[0] // 2 * sizes[1] * sizes[2]

    def as_stored(jacobian):
        return jacobian.transpose(0, 1, 3, 2, 4).reshape(-1, LANES)

    arguments = (
        face,
        back_match,
        corner_gain.reshape(-1, LANES),
        front_corners.reshape(-1, LANES),
        back_corners.reshape(-1, LANES),
        as_stored(front_jc),
        as_stored(front_jp),
        as_stored(back_jc),
        as_stored(back_jp),
        front_res.reshape(-1, LANES),
        back_res.reshape(-1, LANES),
        front_cams.T,
        back_cams.T,
        selection(view_count),
    )
    spaces = [pltpu.SMEM] * 2 + [pltpu.VMEM] * 12
    vmem = pl.BlockSpec(memory_space=pltpu.VMEM)
    return pl.pallas_call(
        functools.partial(step_kernel, sizes, per_panel, frames, view_count),
        in_specs=[pl.BlockSpec(memory_space=pltpu.HBM)] * len(arguments),
        out_specs=(vmem, vmem),
        out_shape=(
            pltpu.VMEM((DIM, per_panel), jnp.float32),
            pltpu.VMEM((DIM, frames), jnp.float32),
        ),
        scratch_shapes=[space(value.shape, value.dtype) for space, value in zip(spaces, arguments)]
        + [
            pltpu.VMEM((3, views, LANES), jnp.float32),
            pltpu.VMEM((frames, 2 * view_count * SLOT, COORDS * LANES), jnp.bfloat16),
            pltpu.VMEM((frames, 3 * view_count * SLOT, COORDS * LANES), jnp.bfloat16),
            pltpu.VMEM((frames * SLOT, LANES), jnp.float32),
            pltpu.VMEM((frames * SLOT, LANES), jnp.float32),
            pltpu.VMEM((SUB, LANES), jnp.float32),
            pltpu.VMEM((2 * PER_SET, SUB, LANES), jnp.float32),
            pltpu.VMEM((DIM, SUB, width), jnp.float32),
            pltpu.VMEM((SUB, LANES), jnp.float32),
            pltpu.VMEM((2 * PER_SET, SUB, LANES), jnp.float32),
            pltpu.VMEM((DIM, SUB, width), jnp.float32),
            pltpu.VMEM((4, SUB * SUB, LANES), jnp.float32),
            pltpu.VMEM((4, DIM, SUB, LANES), jnp.float32),
            pltpu.VMEM((4, DIM, SUB, LANES), jnp.float32),
            pltpu.VMEM((width, 4 * LANES), jnp.bfloat16),
            pltpu.VMEM((4 * LANES, width), jnp.bfloat16),
            pltpu.VMEM((ITERS + 1, SUB, width), jnp.float32),
            pltpu.VMEM((ITERS + 1, peers, SUB, width), jnp.float32),
            pltpu.SemaphoreType.DMA((5,)),
            pltpu.SemaphoreType.DMA((5,)),
            pltpu.SemaphoreType.DMA((ITERS + 1,)),
            pltpu.SemaphoreType.DMA((ITERS + 1,)),
            pltpu.SemaphoreType.DMA((len(arguments),)),
        ],
        compiler_params=pltpu.CompilerParams(
            collective_id=0, has_side_effects=True, vmem_limit_bytes=60 * 1024 * 1024
        ),
        name="step",
    )(*arguments)


def solution(mesh):
    wide = ("panel", "cam", "frame")
    sizes = tuple(mesh.shape[name] for name in wide)
    in_specs = (
        P(wide, None, None, None, None),
        P(wide, None, None, None, None),
        P(wide, None, None, None),
        P(wide, None, None),
        P(wide, None),
        P(wide, None, None, None, None),
        P(wide, None, None, None, None),
        P(wide, None, None, None),
        P(wide, None, None),
        P(wide, None),
        P(wide),
        P(wide),
        P(),
    )
    out_specs = (P(None, "panel"), P(None, wide))
    return jax.shard_map(
        functools.partial(local, sizes), mesh=mesh, in_specs=in_specs, out_specs=out_specs, check_vma=False
    )
```

```python
import functools

import jax
import jax.numpy as jnp
import numpy as np
from jax import lax
from jax.experimental import pallas as pl
from jax.experimental.pallas import tpu as pltpu
from jax.sharding import PartitionSpec as P

CAM_DEV = 8
ITERS = 4
LANES = 128
SLOT = 16
SUB = 8
DIM = 6
COORDS = 2

damp_pose = 0.1
damp_camera = 0.5
MESH = pl.DeviceIdType.MESH
NT = (((1,), (1,)), ((), ()))

GRAD, SUMS, PER_SET = 6, 7, 9
FRONT, BACK = 0, PER_SET


def selection(view_count):
    block = view_count * DIM * COORDS
    res_rows = view_count * COORDS
    table = np.zeros((2, COORDS, 2, view_count, SLOT, 4 * block + 4 * res_rows), np.float32)
    for parity in range(2):
        for coord in range(COORDS):
            for side in range(2):
                for view in range(view_count):
                    for a in range(DIM):
                        column = side * 2 * block + (view * DIM + a) * COORDS + coord
                        table[parity, coord, side, view, a, column] = 1
                        table[parity, coord, side, view, SUB + a, column + block] = 1
                    column = 4 * block + side * 2 * res_rows + parity * res_rows + view * COORDS + coord
                    table[parity, coord, side, view, SUB + DIM, column] = 1
    return jnp.asarray(table.reshape(2, COORDS * 2 * view_count * SLOT, -1), jnp.bfloat16)


def row_of(value, index):
    return jnp.broadcast_to(value[index : index + 1, :], (SUB, value.shape[1]))


def halves(value):
    high = value.astype(jnp.bfloat16)
    low = (value - high.astype(jnp.float32)).astype(jnp.bfloat16)
    return jnp.concatenate([high, low], axis=0)


def invert(working):
    sub = lax.broadcasted_iota(jnp.int32, working[0].shape, 0)
    inverse = [jnp.where(sub == row, 1.0, 0.0) for row in range(DIM)]
    working = list(working)
    for column in range(DIM):
        pivot = 1.0 / row_of(working[column], column)
        row_work = working[column] * pivot
        row_inverse = inverse[column] * pivot
        for row in range(DIM):
            if row == column:
                continue
            factor = row_of(working[row], column)
            working[row] = working[row] - factor * row_work
            inverse[row] = inverse[row] - factor * row_inverse
        working[column] = row_work
        inverse[column] = row_inverse
    return inverse


def step_kernel(
    sizes,
    per_panel,
    frames,
    view_count,
    *refs,
):
    stored, (cam_out, pose_out), held = refs[:14], refs[14:16], refs[16:30]
    step_body(sizes, per_panel, frames, view_count, stored, held, cam_out, pose_out, *held, *refs[30:])


def step_body(
    sizes,
    per_panel,
    frames,
    view_count,
    stored_refs,
    held_refs,
    cam_out,
    pose_out,
    face_s,
    match_s,
    gain,
    fcor,
    bcor,
    fjc,
    fjp,
    bjc,
    bjp,
    fres,
    bres,
    fcam,
    bcam,
    pick,
    weights,
    left,
    right,
    grams0,
    grams1,
    own0,
    own1,
    own2,
    got0,
    got1,
    got2,
    turned,
    folded,
    upright,
    hot,
    tall_hot,
    send,
    recv,
    swap_send,
    swap_recv,
    send_sem,
    recv_sem,
    load_sem,
):
    panels, cams, cores = sizes
    group = cams * cores
    half = panels // 2
    peers = half * group
    width = panels * per_panel
    views = frames * view_count
    table_rows = gain.shape[0] // 2
    panel = lax.axis_index("panel")
    cam = lax.axis_index("cam")
    core = lax.axis_index("frame")
    other_panel = lax.rem(panel + half, panels)
    partner = (other_panel, cam, core)
    side = panel // half
    me = (lax.rem(panel, half) * cams + cam) * cores + core

    near = lax.rem(panel, half)

    def device_at(panel_step, cam_step, core_step):
        place = side * half + lax.rem(near + panel_step, half)
        return (place, lax.rem(cam + cam_step, cams), lax.rem(core + core_step, cores))

    def flipped(bits, cam_step, core_step):
        place = panel
        for bit in range(bits.bit_length()):
            if bits >> bit & 1:
                place = place + 2**bit - 2 * 2**bit * lax.rem(near // 2**bit, 2)
        return (place, lax.rem(cam + cam_step, cams), lax.rem(core + core_step, cores))

    def each_peer(action):
        if peers <= 16:
            places = [(p, c, k) for p in range(half) for c in range(cams) for k in range(cores)][1:]
            for place in sorted(places, key=lambda place: -(place[0].bit_count() + place[1])):
                action((device_at if half & (half - 1) else flipped)(*place))
        else:

            @pl.loop(1, peers)
            def _(offset):
                action(device_at(offset // group, (offset // cores) % cams, offset % cores))

    loads = [
        pltpu.make_async_copy(source, target, load_sem.at[index])
        for index, (source, target) in enumerate(zip(stored_refs, held_refs))
    ]
    for load in loads:
        load.start()

    barrier = pltpu.get_barrier_semaphore()
    pl.semaphore_signal(barrier, inc=1, device_id=partner, device_id_type=MESH)
    each_peer(lambda device: pl.semaphore_signal(barrier, inc=1, device_id=device, device_id_type=MESH))

    for load in loads[:5]:
        load.wait()

    sub = lax.broadcasted_iota(jnp.int32, (SUB, LANES), 0)
    lane = lax.broadcasted_iota(jnp.int32, (SUB, LANES), 1)

    def look_up(step, _):
        rows = pl.ds(pl.multiple_of(step * SUB, SUB), SUB)
        own_face = jnp.where(sub < view_count, face_s[2 * step], face_s[2 * step + 1]) == 0
        front, back = fcor[rows, :], bcor[rows, :]
        front_low, front_high = front & (LANES - 1), front // LANES
        back_low, back_high = back & (LANES - 1), back // LANES
        found = [jnp.zeros((SUB, LANES), jnp.float32)] * 3

        def table(entry, face):
            line = face * table_rows + entry
            return jnp.broadcast_to(gain[line : line + 1, :], (SUB, LANES))

        def pick_from(source, low):
            return jnp.take_along_axis(source, low, axis=1, mode="promise_in_bounds")

        for entry in range(table_rows):
            mixed = jnp.where(own_face, table(entry, 0), table(entry, 1))
            found[0] = jnp.where(front_high == entry, pick_from(mixed, front_low), found[0])
        for entry in range(table_rows):
            here = back_high == entry
            for face in range(2):
                found[1 + face] = jnp.where(here, pick_from(table(entry, face), back_low), found[1 + face])
        for place in range(3):
            weights[place, rows, :] = found[place]
        return 0

    for load in loads[5:]:
        load.wait()

    quarter = lane // frames
    count = LANES // frames
    inverse_match = jnp.zeros((SUB, LANES), jnp.int32)
    in_frames = lane % frames
    face_row = jnp.zeros((SUB, LANES), jnp.float32)
    for frame in range(frames):
        inverse_match = jnp.where(in_frames == match_s[frame], frame, inverse_match)
        face_row = jnp.where(in_frames == frame, face_s[frame].astype(jnp.float32), face_row)
    home = quarter * frames + inverse_match

    def to_home(value):
        return jnp.take_along_axis(value, home, axis=1, mode="promise_in_bounds")

    def code_row(ref):
        row = jnp.concatenate([ref[view : view + 1, :] for view in range(view_count)], axis=1)
        return jnp.broadcast_to(row, (SUB, LANES)).astype(jnp.float32)

    own0[...] = jnp.where(sub == 2, face_row, jnp.where(sub == 0, code_row(fcam), to_home(code_row(bcam))))

    def to_partner(source, target, index):
        return pltpu.make_async_remote_copy(
            src_ref=source,
            dst_ref=target,
            send_sem=swap_send.at[index],
            recv_sem=swap_recv.at[index],
            device_id=partner,
            device_id_type=MESH,
        )

    greeting = to_partner(own0, got0, 0)

    block_rows = view_count * DIM * COORDS
    span = 2 * view_count * SLOT
    slot_view = lax.broadcasted_iota(jnp.int32, (SLOT, LANES), 1) // SLOT

    def prepare(step, _):
        for parity in range(2):
            frame = 2 * step + parity
            rows = pl.ds(pl.multiple_of(frame * block_rows, SLOT), block_rows)
            res_rows = pl.ds(pl.multiple_of(step * SLOT, SLOT), SLOT)
            stored = jnp.concatenate(
                [fjc[rows, :], fjp[rows, :], bjc[rows, :], bjp[rows, :], fres[res_rows, :], bres[res_rows, :]], axis=0
            )
            plain = jnp.dot(pick[parity], stored, preferred_element_type=jnp.float32)
            for coord in range(COORDS):
                part = plain[coord * span : (coord + 1) * span]
                lanes = slice(coord * LANES, (coord + 1) * LANES)
                left[frame, :, lanes] = part.astype(jnp.bfloat16)
                scaled = []
                for place in range(3):
                    for view in range(view_count):
                        weight = weights[place, pl.ds(frame * view_count + view, 1), :]
                        start = ((view_count if place else 0) + view) * SLOT
                        scaled.append(part[start : start + SLOT] * jnp.broadcast_to(weight, (SLOT, LANES)))
                right[frame, :, lanes] = jnp.concatenate(scaled, axis=0).astype(jnp.bfloat16)
        return 0

    def gram(frame, _):
        product = lax.dot_general(left[frame], right[frame], NT, preferred_element_type=jnp.float32)
        both = product[:SLOT, :LANES]
        for view in range(1, 2 * view_count):
            both = jnp.where(slot_view == view, product[view * SLOT : (view + 1) * SLOT, :LANES], both)
        start = view_count * SLOT
        last = product[start : start + SLOT, LANES:]
        for view in range(1, view_count):
            rows_of = product[start + view * SLOT : start + (view + 1) * SLOT, LANES:]
            last = jnp.where(slot_view[:, : last.shape[1]] == view, rows_of, last)
        out_rows = pl.ds(pl.multiple_of(frame * SLOT, SLOT), SLOT)
        grams0[out_rows, :] = both
        grams1[out_rows, : last.shape[1]] = last
        return 0

    def weigh(step, _):
        look_up(step, _)
        return prepare(step, _)

    steps = frames // 2
    lax.fori_loop(0, steps // 4, weigh, 0, unroll=True)
    pl.semaphore_wait(barrier, peers)
    greeting.start()
    lax.fori_loop(steps // 4, steps, weigh, 0, unroll=True)
    lax.fori_loop(0, frames, gram, 0, unroll=True)
    def turn(scratch, rows):
        result = []
        for quad in range(SLOT // count):
            block = jnp.concatenate(
                [scratch[pl.ds(quad * count + i, frames, stride=SLOT), :] for i in range(count)], axis=0
            )
            result.append(block.T[:rows])
        return result

    def swap_quarters(r):
        low = quarter < 2
        even = quarter % 2 == 0
        u0 = jnp.where(low, r[0], pltpu.roll(r[2], 2 * frames, 1))
        u1 = jnp.where(low, r[1], pltpu.roll(r[3], 2 * frames, 1))
        u2 = jnp.where(low, pltpu.roll(r[0], 2 * frames, 1), r[2])
        u3 = jnp.where(low, pltpu.roll(r[1], 2 * frames, 1), r[3])
        back = LANES - frames
        return [
            jnp.where(even, u0, pltpu.roll(u1, frames, 1)),
            jnp.where(even, pltpu.roll(u0, back, 1), u1),
            jnp.where(even, u2, pltpu.roll(u3, frames, 1)),
            jnp.where(even, pltpu.roll(u2, back, 1), u3),
        ]

    def lay_out(turned_grams, first_view, order):
        columns, sums = [], []
        for quad, tall in enumerate(turned_grams):
            starts = [(first_view + view) * SLOT for view in range(view_count)]
            columns += swap_quarters([tall[start : start + SUB] for start in starts])
            if quad >= 2:
                total = tall[starts[0] + SUB : starts[0] + SLOT]
                for start in starts[1:]:
                    total = total + tall[start + SUB : start + SLOT]
                sums.append(total)
        return [order(value) for value in columns[:DIM]], [order(value) for value in columns[SUB : SUB + GRAD + 1] + sums]

    def hot_columns(place, codes, row, base):
        camera = codes[row : row + 1, :].astype(jnp.int32) + base * per_panel
        camera = jnp.where(camera >= width, camera - width, camera)
        chosen = jnp.broadcast_to(camera, (width, LANES)) == lax.broadcasted_iota(jnp.int32, (width, LANES), 0)
        hot[:, place * LANES : (place + 1) * LANES] = jnp.where(chosen, 1.0, 0.0).astype(jnp.bfloat16)

    def lanes_of(place, places=1):
        return slice(place * LANES, (place + places) * LANES)

    def keep(place, ref, first):
        for b in range(DIM):
            turned[place, b * SUB : (b + 1) * SUB, :] = ref[first + b]

    tall0 = turn(grams0, LANES)
    tall1 = turn(grams1, view_count * SLOT)
    front_cam, front_rest = lay_out(tall0, 0, lambda value: value)
    for index, value in enumerate(front_rest):
        own1[FRONT + index] = value

    def part(first, entries, index):
        places = (pl.ds(first, entries), pl.ds(0, DIM))
        return to_partner(own1.at[places], got1.at[places], index)

    swap_front = part(FRONT, PER_SET, 1)
    swap_front.start()
    back0_cam, back0_rest = lay_out(tall0, view_count, to_home)
    back1_cam, back1_rest = lay_out(tall1, 0, to_home)
    for place in range(4):
        turned[place, DIM * SUB :, :] = jnp.zeros((2 * SUB, LANES), jnp.float32)
    keep(1, own1, FRONT)
    own_codes = own0[...]
    hot_columns(1, own_codes, 0, panel)
    hot_columns(2, own_codes, 1, panel)

    greeting.wait_recv()
    far_codes = got0[...]
    first_face = row_of(far_codes, 2) < 0.5
    chosen_rest = [jnp.where(first_face, one, zero) for zero, one in zip(back0_rest, back1_rest)]
    for index in range(SUMS, PER_SET):
        own1[BACK + index] = chosen_rest[index]
    swap_sums = part(BACK + SUMS, PER_SET - SUMS, 4)
    swap_sums.start()
    for index in range(SUMS):
        own1[BACK + index] = chosen_rest[index]
    swap_back = part(BACK, SUMS, 2)
    swap_back.start()

    stacked = jnp.concatenate(
        [
            jnp.concatenate([front, jnp.where(first_face, one, zero)], axis=1)
            for front, zero, one in zip(front_cam, back0_cam, back1_cam)
        ],
        axis=0,
    )
    summed = lax.dot_general(halves(stacked), hot[:, lanes_of(1, 2)], NT, preferred_element_type=jnp.float32)
    for b in range(DIM):
        rows = slice(b * SUB, (b + 1) * SUB)
        own2[b] = summed[rows] + summed[DIM * SUB + b * SUB : DIM * SUB + (b + 1) * SUB]
    swap_cam = to_partner(own2.at[:, pl.ds(0, DIM)], got2.at[:, pl.ds(0, DIM)], 3)
    keep(2, own1, BACK)
    hot_columns(0, far_codes, 1, other_panel)
    hot_columns(3, far_codes, 0, other_panel)
    for place in range(4):
        tall_hot[lanes_of(place), :] = hot[:, lanes_of(place)].astype(jnp.float32).T.astype(jnp.bfloat16)
    swap_front.wait_recv()
    keep(3, got1, FRONT)
    swap_sums.wait_recv()

    def over_quarters(value):
        first, second, third = (pltpu.roll(value, i * frames, 1) for i in range(1, count))
        return (value + first) + (second + third)

    def spread(value, place):
        return over_quarters(jnp.where(quarter == place, value, 0.0))

    inverses, pose_grads = [], []
    for back, front in ((got1, own1), (own1, got1)):
        total = [jnp.where(sub < DIM, back[BACK + SUMS + i] + front[FRONT + SUMS + i], 0.0) for i in range(2)]
        columns = [spread(total[b // count], b % count) for b in range(DIM + 1)]
        pose_grads.append(columns[DIM])
        inverses.append(invert([columns[b] + jnp.where(sub == b, damp_pose, 0.0) for b in range(DIM)]))

    def solve_pose(which, value):
        result = inverses[which][0] * row_of(value, 0)
        for b in range(1, DIM):
            result = result + inverses[which][b] * row_of(value, b)
        return result

    def couple(which, seen):
        sums = []
        for place in (2 * which, 2 * which + 1):
            terms = [upright[place, a] * row_of(seen[:, lanes_of(place)], a) for a in range(DIM)]
            sums.append((terms[0] + terms[1]) + (terms[2] + terms[3]) + (terms[4] + terms[5]))
        total = sums[0] + sums[1]
        return over_quarters(total)

    def minus_spread(place, value, solved):
        for b in range(DIM):
            value = value - turned[place, b * SUB : (b + 1) * SUB, :] * row_of(solved, b)
        return value

    def fold(place):
        for b in range(DIM):
            column = inverses[place // 2][b]
            total = turned[place, :SUB, :] * row_of(column, 0)
            for row in range(1, DIM):
                total = total + turned[place, row * SUB : (row + 1) * SUB, :] * row_of(column, row)
            folded[place, b] = total
            upright[place, b] = turned[place, pl.ds(b, SUB, stride=SUB), :]

    def look(vector, places):
        both = jnp.dot(halves(vector), hot[:, lanes_of(0, places)], preferred_element_type=jnp.float32)
        return both[:SUB] + both[SUB:]

    def scatter(pieces, first=0):
        rows = lanes_of(first, len(pieces))
        both = jnp.dot(halves(jnp.concatenate(pieces, axis=1)), tall_hot[rows, :], preferred_element_type=jnp.float32)
        return both[:SUB] + both[SUB:]

    def exchange(round_id, value):
        send[round_id] = value
        each_peer(
            lambda device: pltpu.make_async_remote_copy(
                src_ref=send.at[round_id, pl.ds(0, DIM)],
                dst_ref=recv.at[round_id, me, pl.ds(0, DIM)],
                send_sem=send_sem.at[round_id],
                recv_sem=recv_sem.at[round_id],
                device_id=device,
                device_id_type=MESH,
            ).start()
        )
        recv[round_id, pl.ds(me, 1)] = value[None]
        others = recv.at[round_id, pl.ds(0, peers - 1), pl.ds(0, DIM)]

        def finish():
            pltpu.make_async_copy(others, others, recv_sem.at[round_id]).wait()
            parts = [recv[round_id, source] for source in range(peers)]
            while len(parts) > 1:
                tail = [parts[-1]] if len(parts) % 2 else []
                parts = [a + b for a, b in zip(parts[::2], parts[1::2])] + tail
            return jnp.where(lax.broadcasted_iota(jnp.int32, (SUB, width), 0) < DIM, parts[0], 0.0)

        return finish

    def drain(round_id):
        others = recv.at[round_id, pl.ds(0, peers - 1), pl.ds(0, DIM)]
        pltpu.make_async_copy(others, others, send_sem.at[round_id]).wait()

    solved = [solve_pose(which, pose_grads[which]) for which in range(2)]
    here = ((own1, FRONT), (own1, BACK), (got1, FRONT))
    known = scatter(
        [minus_spread(i + 1, ref[first + GRAD], solved[(i + 1) // 2]) for i, (ref, first) in enumerate(here)], 1
    )
    swap_back.wait_recv()
    keep(0, got1, BACK)
    right_side = exchange(0, known + scatter([minus_spread(0, got1[BACK + GRAD], solved[0])]))

    swap_cam.start()
    for place in range(4):
        fold(place)
    swap_cam.wait_recv()
    blocks = [own2[b] + got2[b] for b in range(DIM)]

    def apply(vector):
        seen = look(vector, 4)
        pieces = []
        for which in range(2):
            coupled = couple(which, seen)
            for place in (2 * which, 2 * which + 1):
                value = folded[place, 0] * row_of(coupled, 0)
                for b in range(1, DIM):
                    value = value + folded[place, b] * row_of(coupled, b)
                pieces.append(value)
        local_part = blocks[0] * row_of(vector, 0)
        for b in range(1, DIM):
            local_part = local_part + blocks[b] * row_of(vector, b)
        return local_part - scatter(pieces)

    def dot(left, right):
        return jnp.sum(jnp.sum(left * right, axis=1, keepdims=True), axis=0, keepdims=True)

    def pose_of(vector):
        return solve_pose(0, couple(0, look(vector, 2)))

    residual = -right_side()
    direction = residual
    update = jnp.zeros_like(residual)
    share = applied = apply(residual)
    norm_now = dot(residual, residual)
    for iteration in range(ITERS):
        finish = exchange(iteration + 1, share)
        if iteration + 1 == ITERS:
            pose_before = -solve_pose(0, pose_grads[0]) - pose_of(update)
            pose_along = pose_of(direction)
            turn_by = lax.rem(panels - panel, panels) * per_panel
            cam_before = pltpu.roll(update, turn_by, 1)
            cam_along = pltpu.roll(direction, turn_by, 1)
        image = damp_camera * direction + finish()
        if iteration + 1 < ITERS:
            applied_image = apply(image)
        size = norm_now / dot(direction, image)
        if iteration + 1 < ITERS:
            update = update + size * direction
            residual = residual - size * image
            applied = applied - size * applied_image
            norm_next = dot(residual, residual)
            ratio = norm_next / norm_now
            direction = residual + ratio * direction
            share = applied + ratio * share
            norm_now = norm_next

    cam_out[...] = (cam_before + size * cam_along)[:DIM, :per_panel]
    pose_out[...] = (pose_before - size * pose_along)[:DIM, :frames]
    for copy in (greeting, swap_front, swap_sums, swap_back, swap_cam):
        copy.wait_send()
    for round_id in range(ITERS + 1):
        drain(round_id)


def local(
    sizes,
    front_jc,
    front_jp,
    front_res,
    front_corners,
    front_cams,
    back_jc,
    back_jp,
    back_res,
    back_corners,
    back_cams,
    back_match,
    face,
    corner_gain,
):
    frames = face.shape[0]
    view_count = front_cams.shape[1]
    views = frames * view_count
    per_panel = CAM_DEV * sizes[1]
    width = sizes[0] * per_panel
    peers = sizes[0] // 2 * sizes[1] * sizes[2]

    def as_stored(jacobian):
        return jacobian.transpose(0, 1, 3, 2, 4).reshape(-1, LANES)

    arguments = (
        face,
        back_match,
        corner_gain.reshape(-1, LANES),
        front_corners.reshape(-1, LANES),
        back_corners.reshape(-1, LANES),
        as_stored(front_jc),
        as_stored(front_jp),
        as_stored(back_jc),
        as_stored(back_jp),
        front_res.reshape(-1, LANES),
        back_res.reshape(-1, LANES),
        front_cams.T,
        back_cams.T,
        selection(view_count),
    )
    spaces = [pltpu.SMEM] * 2 + [pltpu.VMEM] * 12
    vmem = pl.BlockSpec(memory_space=pltpu.VMEM)
    return pl.pallas_call(
        functools.partial(step_kernel, sizes, per_panel, frames, view_count),
        in_specs=[pl.BlockSpec(memory_space=pltpu.HBM)] * len(arguments),
        out_specs=(vmem, vmem),
        out_shape=(
            pltpu.VMEM((DIM, per_panel), jnp.float32),
            pltpu.VMEM((DIM, frames), jnp.float32),
        ),
        scratch_shapes=[space(value.shape, value.dtype) for space, value in zip(spaces, arguments)]
        + [
            pltpu.VMEM((3, views, LANES), jnp.float32),
            pltpu.VMEM((frames, 2 * view_count * SLOT, COORDS * LANES), jnp.bfloat16),
            pltpu.VMEM((frames, 3 * view_count * SLOT, COORDS * LANES), jnp.bfloat16),
            pltpu.VMEM((frames * SLOT, LANES), jnp.float32),
            pltpu.VMEM((frames * SLOT, LANES), jnp.float32),
            pltpu.VMEM((SUB, LANES), jnp.float32),
            pltpu.VMEM((2 * PER_SET, SUB, LANES), jnp.float32),
            pltpu.VMEM((DIM, SUB, width), jnp.float32),
            pltpu.VMEM((SUB, LANES), jnp.float32),
            pltpu.VMEM((2 * PER_SET, SUB, LANES), jnp.float32),
            pltpu.VMEM((DIM, SUB, width), jnp.float32),
            pltpu.VMEM((4, SUB * SUB, LANES), jnp.float32),
            pltpu.VMEM((4, DIM, SUB, LANES), jnp.float32),
            pltpu.VMEM((4, DIM, SUB, LANES), jnp.float32),
            pltpu.VMEM((width, 4 * LANES), jnp.bfloat16),
            pltpu.VMEM((4 * LANES, width), jnp.bfloat16),
            pltpu.VMEM((ITERS + 1, SUB, width), jnp.float32),
            pltpu.VMEM((ITERS + 1, peers, SUB, width), jnp.float32),
            pltpu.SemaphoreType.DMA((5,)),
            pltpu.SemaphoreType.DMA((5,)),
            pltpu.SemaphoreType.DMA((ITERS + 1,)),
            pltpu.SemaphoreType.DMA((ITERS + 1,)),
            pltpu.SemaphoreType.DMA((len(arguments),)),
        ],
        compiler_params=pltpu.CompilerParams(
            collective_id=0, has_side_effects=True, vmem_limit_bytes=60 * 1024 * 1024
        ),
        name="step",
    )(*arguments)


def solution(mesh):
    wide = ("panel", "cam", "frame")
    sizes = tuple(mesh.shape[name] for name in wide)
    in_specs = (
        P(wide, None, None, None, None),
        P(wide, None, None, None, None),
        P(wide, None, None, None),
        P(wide, None, None),
        P(wide, None),
        P(wide, None, None, None, None),
        P(wide, None, None, None, None),
        P(wide, None, None, None),
        P(wide, None, None),
        P(wide, None),
        P(wide),
        P(wide),
        P(),
    )
    out_specs = (P(None, "panel"), P(None, wide))
    return jax.shard_map(
        functools.partial(local, sizes), mesh=mesh, in_specs=in_specs, out_specs=out_specs, check_vma=False
    )
```
